256 devices in a mesh: gx: 8 (over z), gy: 32 (over x, y, core).
Axes of the slice: x: 4, y: 4, z: 8, core: 2. Of those that a mesh axis runs over, the one named last changes fastest.
Arguments:
- permeability: float32 [3, 256, 65536], P(None, 'gx', 'gy'), may hold values from 0.03 to 1000, as said below
Outputs:
- fine_pressure: float32 [256, 65536], P('gx', 'gy')
- twin_pressure: float32 [128, 16384], P('gx', 'gy')
The draws below stay inside these ranges and needn't reach their ends.
Inputs may be any that keep to these rules, and one draw needn't show every extreme that they name: `permeability`: positive conductivities; entry 0, 1, 2 of the first dimension is the conductivity along the grid's first, second, third dimension.
All inputs are finite; a program needn't handle non-finite values.
Results may differ from the reference program's by a relative error of at most 0.0003.
Values sent between devices are 32-bit elements; how exact they have to be, the bound alone decides.
A program may use at most 192 MiB of HBM per device.

```python
import math
import jax
import jax.numpy as jnp
from jax import lax

EL = 32
ELZ = 16
MX = 4
MZ = 2
EZ = 2
PATCH_ITERS = 3
COARSE_ITERS = 2
NX = 256
NY = 2048
NZ = 32


def draw_permeability(key, part):
    noise_key, phase_key, swing_key = jax.random.split(key, 3)
    place_rows = (jnp.arange(NX, dtype=jnp.float32) + 0.5) / NX
    place_cols = (jnp.arange(NY, dtype=jnp.float32) + 0.5) / NY
    phase = jax.random.uniform(phase_key, (NZ,), jnp.float32, 0.0, 2.0 * math.pi)
    swing = jax.random.uniform(swing_key, (NZ,), jnp.float32, 0.5, 2.5)
    across = 2.0 * math.pi * (jnp.arange(NY, dtype=jnp.float32) + 0.5) / 24.0
    meander = jnp.sin(2.0 * math.pi * jnp.arange(NX, dtype=jnp.float32) / 96.0)
    wave = across[None, :, None] + phase[None, None, :] + swing[None, None, :] * meander[:, None, None]
    channel = 3.0 * jax.nn.sigmoid(6.0 * (jnp.sin(wave) - 0.5))
    trend = math.log(3.0) * (place_rows[:, None, None] + place_cols[None, :, None])
    rough = jnp.clip(0.6 * jax.random.normal(noise_key, (3, NX, NY, NZ), jnp.float32), -1.5, 1.5)
    layered = jnp.array([0.0, 0.0, -1.6], jnp.float32)[:, None, None, None]
    values = jnp.exp(trend[None] + channel[None] + rough + layered)
    return values.reshape(3, NX, NY * NZ)


def setup_inputs(seed: int = 0) -> dict:
    key_list = jax.random.split(jax.random.key(seed), 2)
    return {
        "permeability": draw_permeability(jax.random.fold_in(key_list[1], 71), 0),
    }


def harmonic(first, second, spacing):
    return spacing * 2.0 * first * second / (first + second)


def face_weights(conduct, width, spacing):
    weight_rows = harmonic(conduct[0][..., :-width], conduct[0][..., width:], spacing)
    weight_cols = harmonic(conduct[1][..., :-1], conduct[1][..., 1:], spacing)
    column = jnp.arange(weight_cols.shape[-1], dtype=jnp.int32) % width
    weight_cols = jnp.where(column == width - 1, jnp.zeros_like(weight_cols), weight_cols)
    weight_depth = harmonic(conduct[2][:, :-1], conduct[2][:, 1:], spacing)
    return weight_rows, weight_cols, weight_depth


def apply_operator(field, weights, width):
    weight_rows, weight_cols, weight_depth = weights
    flux = weight_rows * (field[..., :-width] - field[..., width:])
    result = jnp.pad(flux, ((0, 0), (0, 0), (0, 0), (0, width))) - jnp.pad(flux, ((0, 0), (0, 0), (0, 0), (width, 0)))
    flux = weight_cols * (field[..., :-1] - field[..., 1:])
    result = result + jnp.pad(flux, ((0, 0), (0, 0), (0, 0), (0, 1))) - jnp.pad(flux, ((0, 0), (0, 0), (0, 0), (1, 0)))
    flux = weight_depth * (field[:, :, :-1] - field[:, :, 1:])
    result = result + jnp.pad(flux, ((0, 0), (0, 0), (0, 1), (0, 0))) - jnp.pad(flux, ((0, 0), (0, 0), (1, 0), (0, 0)))
    return result


def interior_mask(depth, rows, width):
    level = jnp.arange(depth, dtype=jnp.int32)[:, None]
    cell = jnp.arange(rows * width, dtype=jnp.int32)[None, :]
    row_index = cell // width
    line_index = cell % width
    inside = (level > 0) & (level < depth - 1) & (row_index > 0) & (row_index < rows - 1) & (line_index > 0) & (line_index < width - 1)
    return inside.astype(jnp.float32)


def shape_functions(depth, rows, width, edge, edge_depth, margin, margin_depth):
    cell = jnp.arange(rows * width, dtype=jnp.int32)
    place_rows = ((cell // width).astype(jnp.float32) - margin + 0.5) / edge
    place_cols = ((cell % width).astype(jnp.float32) - margin + 0.5) / edge
    place_depth = (jnp.arange(depth, dtype=jnp.int32).astype(jnp.float32) - margin_depth + 0.5) / edge_depth
    factors = []
    for basis in range(8):
        along_rows = place_rows if basis // 4 else 1.0 - place_rows
        along_cols = place_cols if (basis // 2) % 2 else 1.0 - place_cols
        along_depth = place_depth if basis % 2 else 1.0 - place_depth
        factors.append(along_depth[:, None] * (along_rows * along_cols)[None, :])
    return jnp.stack(factors)[:, None]


def patch_fields(block, edge_depth, margin_depth):
    depth = edge_depth + 2 * margin_depth
    count = (block.shape[3] - 2 * margin_depth) // edge_depth
    pieces = [block[:, :, :, index * edge_depth: index * edge_depth + depth] for index in range(count)]
    stacked = jnp.stack(pieces, axis=1)
    return jnp.transpose(stacked, (0, 1, 4, 2, 3)).reshape(3, count, depth, block.shape[1] * block.shape[2])


def solve_column(block, edge, edge_depth, margin, margin_depth, spacing):
    rows = block.shape[1]
    width = block.shape[2]
    depth = edge_depth + 2 * margin_depth
    conduct = patch_fields(block, edge_depth, margin_depth)
    count = conduct.shape[1]
    weights = face_weights(conduct, width, spacing)
    inside = interior_mask(depth, rows, width)
    start = shape_functions(depth, rows, width, edge, edge_depth, margin, margin_depth)
    residual = -inside * apply_operator(start, weights, width)
    direction = residual
    norm_now = jnp.sum(residual * residual, axis=(2, 3), keepdims=True)
    update = jnp.zeros_like(residual)
    for step in range(PATCH_ITERS):
        image = inside * apply_operator(direction, weights, width)
        alpha = norm_now / jnp.sum(direction * image, axis=(2, 3), keepdims=True)
        update = update + alpha * direction
        residual = residual - alpha * image
        norm_next = jnp.sum(residual * residual, axis=(2, 3), keepdims=True)
        direction = residual + (norm_next / norm_now) * direction
        norm_now = norm_next
    solution = start + update
    local = solution.reshape(8, count, depth, rows, width)[:, :, margin_depth:margin_depth + edge_depth, margin:margin + edge, margin:margin + edge]
    local = local.reshape(8, count, edge_depth, edge * edge)
    element_conduct = conduct.reshape(3, count, depth, rows, width)[:, :, margin_depth:margin_depth + edge_depth, margin:margin + edge, margin:margin + edge]
    element_conduct = element_conduct.reshape(3, count, edge_depth, edge * edge)
    inner_rows, inner_cols, inner_depth = face_weights(element_conduct, edge, spacing)
    jump = local[..., :-edge] - local[..., edge:]
    stiffness = jnp.einsum("aezn,bezn->eab", jump * inner_rows, jump, precision=lax.Precision.HIGHEST)
    jump = local[..., :-1] - local[..., 1:]
    stiffness = stiffness + jnp.einsum("aezn,bezn->eab", jump * inner_cols, jump, precision=lax.Precision.HIGHEST)
    jump = local[:, :, :-1] - local[:, :, 1:]
    stiffness = stiffness + jnp.einsum("aezn,bezn->eab", jump * inner_depth, jump, precision=lax.Precision.HIGHEST)
    return local, stiffness


def coarsen(block):
    comps, rows, width, depth = block.shape
    grouped = block.reshape(comps, rows // 2, 2, width // 2, 2, depth // 2, 2)
    return 0.125 * jnp.sum(grouped, axis=(2, 4, 6))


def corner_stack(corner_first, corner_rows, corner_cols, corner_both, count):
    table = [[corner_first, corner_cols], [corner_rows, corner_both]]
    values = []
    for basis in range(8):
        lift = basis % 2
        values.append(table[basis // 4][(basis // 2) % 2][..., lift:lift + count])
    return jnp.stack(values, axis=-1)


def spread(values, count):
    parts = [[None, None], [None, None]]
    for basis in range(8):
        lift = basis % 2
        widths = [(0, 0)] * (values.ndim - 2) + [(lift, 1 - lift)]
        padded = jnp.pad(values[..., basis], widths)
        first = basis // 4
        second = (basis // 2) % 2
        if parts[first][second] is None:
            parts[first][second] = padded
        else:
            parts[first][second] = parts[first][second] + padded
    return parts


def pressure_tile(local, weights, edge):
    combined = jnp.sum(jnp.transpose(weights)[:, :, None, None] * local, axis=0)
    count = combined.shape[0]
    depth = combined.shape[1]
    return jnp.transpose(combined.reshape(count, depth, edge, edge), (2, 3, 0, 1)).reshape(edge, edge, count * depth)


def coarse_global(stiffness, count):
    def operate(nodes):
        shifted_rows = jnp.roll(nodes, -1, 1)
        shifted_cols = jnp.roll(nodes, -1, 2)
        shifted_both = jnp.roll(shifted_rows, -1, 2)
        element = corner_stack(nodes, shifted_rows, shifted_cols, shifted_both, count)
        local = jnp.einsum("lijkab,lijkb->lijka", stiffness, element, precision=lax.Precision.HIGHEST)
        parts = spread(local, count)
        result = parts[0][0] + jnp.roll(parts[1][0], 1, 1) + jnp.roll(parts[0][1], 1, 2)
        return result + jnp.roll(jnp.roll(parts[1][1], 1, 1), 1, 2)

    def total(first, second):
        return jnp.sum(first * second, axis=(1, 2, 3), keepdims=True)

    level = jnp.arange(count + 1, dtype=jnp.int32)
    inside = ((level > 0) & (level < count)).astype(jnp.float32)
    boundary = jnp.broadcast_to((level == 0).astype(jnp.float32), stiffness.shape[:3] + (count + 1,))
    residual = -inside * operate(boundary)
    direction = residual
    update = jnp.zeros_like(residual)
    norm_now = total(residual, residual)
    for step in range(COARSE_ITERS):
        image = inside * operate(direction)
        alpha = norm_now / total(direction, image)
        update = update + alpha * direction
        residual = residual - alpha * image
        norm_next = total(residual, residual)
        direction = residual + (norm_next / norm_now) * direction
        norm_now = norm_next
    return boundary + update


def reference(permeability):
    field = permeability.reshape(3, NX, NY, NZ)
    extended = jnp.pad(field, ((0, 0), (0, 0), (0, 0), (MZ, MZ)), mode="edge")
    twin_extended = coarsen(extended)
    half_edge = EL // 2
    half_margin = MX // 2
    row_elems = NX // EL
    col_elems = NY // EL

    def blocks(index):
        first = index // col_elems
        second = index % col_elems
        fine_rows = (first * EL - MX + jnp.arange(EL + 2 * MX, dtype=jnp.int32)) % NX
        fine_cols = (second * EL - MX + jnp.arange(EL + 2 * MX, dtype=jnp.int32)) % NY
        twin_rows = (first * half_edge - half_margin + jnp.arange(half_edge + 2 * half_margin, dtype=jnp.int32)) % (NX // 2)
        twin_cols = (second * half_edge - half_margin + jnp.arange(half_edge + 2 * half_margin, dtype=jnp.int32)) % (NY // 2)
        fine_block = jnp.take(jnp.take(extended, fine_rows, axis=1), fine_cols, axis=2)
        twin_block = jnp.take(jnp.take(twin_extended, twin_rows, axis=1), twin_cols, axis=2)
        return fine_block, twin_block

    def column_stiffness(index):
        fine_block, twin_block = blocks(index)
        fine_stiff = solve_column(fine_block, EL, ELZ, MX, MZ, 1.0)[1]
        twin_stiff = solve_column(twin_block, half_edge, ELZ // 2, half_margin, MZ // 2, 2.0)[1]
        return jnp.stack([fine_stiff, twin_stiff])

    indices = jnp.arange(row_elems * col_elems, dtype=jnp.int32)
    totals = lax.map(column_stiffness, indices)
    stiffness = jnp.transpose(totals, (1, 0, 2, 3, 4)).reshape(2, row_elems, col_elems, EZ, 8, 8)
    nodes = coarse_global(stiffness, EZ)
    shifted_rows = jnp.roll(nodes, -1, 1)
    shifted_cols = jnp.roll(nodes, -1, 2)
    shifted_both = jnp.roll(shifted_rows, -1, 2)

    def column_pressure(index):
        first = index // col_elems
        second = index % col_elems
        weights = corner_stack(nodes[:, first, second], shifted_rows[:, first, second], shifted_cols[:, first, second], shifted_both[:, first, second], EZ)
        fine_block, twin_block = blocks(index)
        fine_local = solve_column(fine_block, EL, ELZ, MX, MZ, 1.0)[0]
        twin_local = solve_column(twin_block, half_edge, ELZ // 2, half_margin, MZ // 2, 2.0)[0]
        return pressure_tile(fine_local, weights[0], EL), pressure_tile(twin_local, weights[1], half_edge)

    fine_tiles, twin_tiles = lax.map(column_pressure, indices)
    fine_pressure = jnp.transpose(fine_tiles.reshape(row_elems, col_elems, EL, EL, NZ), (0, 2, 1, 3, 4)).reshape(NX, NY * NZ)
    twin_pressure = jnp.transpose(twin_tiles.reshape(row_elems, col_elems, half_edge, half_edge, NZ // 2), (0, 2, 1, 3, 4)).reshape(NX // 2, (NY // 2) * (NZ // 2))
    return (fine_pressure, twin_pressure)
```

```python
import functools

import jax
import jax.numpy as jnp
import numpy as np
from jax import lax
from jax.experimental import pallas as pl
from jax.experimental.pallas import tpu as pltpu
from jax.sharding import PartitionSpec as P

EL = 32
ELZ = 16
MX = 4
MZ = 2
LANES = 128
GROUP = 40
MESH = pl.DeviceIdType.MESH
F32 = jnp.float32
VLIMIT = 60 * 1024 * 1024


class Level:
    def __init__(self, nk, nx, zw, edge, edge_depth, margin, margin_depth, spacing):
        self.nk = nk
        self.nx = nx
        self.nxr = -(-nx // 8) * 8
        self.zw = zw
        self.nseg = GROUP // zw
        self.edge = edge
        self.edge_depth = edge_depth
        self.margin = margin
        self.margin_depth = margin_depth
        self.spacing = spacing


FINE = Level(13, 40, 20, EL, ELZ, MX, MZ, 1.0)
TWIN = Level(7, 20, 10, EL // 2, ELZ // 2, MX // 2, MZ // 2, 2.0)


def stencil_masks():
    masks = np.zeros((10, 8, LANES), np.float32)

    def put(e, a, b, q):
        s = (b - a) % 8
        if s > 4:
            a, s = b, 8 - s
        masks[e * 5 + s, a, q] += 1.0

    q = 0
    for a in range(4):
        for b in range(a, 4):
            put(0, 2 * a + 1, 2 * b + 1, q)
            put(1, 2 * a, 2 * b, q)
            q += 1
    for a in range(4):
        for b in range(4):
            put(0, 2 * a + 1, 2 * b, q)
        q += 1
    return masks


def coarsen_matrix():
    matrix = np.zeros((LANES, LANES), np.float32)
    for h in range(4):
        for e in range(2):
            for zz in range(10):
                for part in range(2):
                    z = min(max(e * ELZ - MZ + 2 * zz + part, 0), 31)
                    matrix[h * 32 + z, (h // 2) * 20 + e * 10 + zz] += 0.125
    return matrix


def lane_iota(rows):
    return lax.broadcasted_iota(jnp.int32, (rows, LANES), 1)


def groups(lane):
    return (lane >= 40).astype(jnp.int32) + (lane >= 80).astype(jnp.int32) + (lane >= 120).astype(jnp.int32)


def split_lane(level, lane):
    chunk = groups(lane)
    inner = lane - GROUP * chunk
    seg = jnp.zeros_like(lane)
    for s in range(1, level.nseg):
        seg = seg + (inner >= s * level.zw).astype(jnp.int32)
    return chunk, seg, inner - level.zw * seg


def harmonic(first, second, spacing):
    return spacing * 2.0 * first * second / (first + second)


def halo_kernel(perm, west, east, hx, hy, hc, send, recv):
    i = lax.axis_index("gx")
    j = lax.axis_index("gy")
    ni = lax.axis_size("gx")
    nj = lax.axis_size("gy")
    up, down = lax.rem(i + 1, ni), lax.rem(i + ni - 1, ni)
    right, left = lax.rem(j + 1, nj), lax.rem(j + nj - 1, nj)
    width = perm.shape[2]
    low, high = pl.ds(0, LANES), pl.ds(width - LANES, LANES)
    plans = [
        (east, hx.at[0], (up, j)),
        (west, hx.at[1], (down, j)),
        (perm.at[:, :, high], hy.at[0], (i, right)),
        (perm.at[:, :, low], hy.at[1], (i, left)),
        (east.at[:, :, high], hc.at[0], (up, right)),
        (east.at[:, :, low], hc.at[1], (up, left)),
        (west.at[:, :, high], hc.at[2], (down, right)),
        (west.at[:, :, low], hc.at[3], (down, left)),
    ]
    barrier = pltpu.get_barrier_semaphore()
    for _, _, target in plans:
        pl.semaphore_signal(barrier, inc=1, device_id=target, device_id_type=MESH)
    pl.semaphore_wait(barrier, 8)
    copies = []
    for n, (src, dst, target) in enumerate(plans):
        copy = pltpu.make_async_remote_copy(
            src_ref=src, dst_ref=dst, send_sem=send.at[n], recv_sem=recv.at[n],
            device_id=target, device_id_type=MESH,
        )
        copy.start()
        copies.append(copy)
    for copy in copies:
        copy.wait()


def halo(perm):
    rows, width = perm.shape[1], perm.shape[2]
    west = perm[:, :MX]
    east = perm[:, rows - MX:]
    anywhere = pl.BlockSpec(memory_space=pl.ANY)
    return pl.pallas_call(
        halo_kernel,
        out_shape=(
            jax.ShapeDtypeStruct((2, 3, MX, width), F32),
            jax.ShapeDtypeStruct((2, 3, rows, LANES), F32),
            jax.ShapeDtypeStruct((4, 3, MX, LANES), F32),
        ),
        in_specs=[anywhere] * 3,
        out_specs=(anywhere,) * 3,
        scratch_shapes=[pltpu.SemaphoreType.DMA((8,)), pltpu.SemaphoreType.DMA((8,))],
        compiler_params=pltpu.CompilerParams(collective_id=0, has_side_effects=True),
    )(perm, west, east)


def assemble(own, hx, hy, hc, ext):
    rows = own.shape[1]

    def body(m, carry):
        for t in range(18):
            if t == 0:
                top, mid, low = hc[0, m], hy[0, m], hc[2, m]
            elif t == 17:
                top, mid, low = hc[1, m], hy[1, m], hc[3, m]
            else:
                lanes = pl.ds((t - 1) * LANES, LANES)
                top, mid, low = hx[0, m, :, lanes], own[m, :, lanes], hx[1, m, :, lanes]
            ext[m, t, 0:MX, :] = top
            ext[m, t, MX:MX + rows, :] = mid
            ext[m, t, MX + rows:2 * MX + rows, :] = low
            ext[m, t, 2 * MX + rows:, :] = jnp.ones((8, LANES), F32)
        return carry

    lax.fori_loop(0, 3, body, 0)


def pack_fine(ext, packed, column):
    lane = lane_iota(GROUP)
    chunk, _, _ = split_lane(FINE, lane)
    inner = lane - GROUP * chunk

    def body(m, carry):
        for k in range(FINE.nk + 1):
            lines = []
            for c in range(3):
                y = FINE.nk * c + k
                tile = ext[m, column * 8 + y // 4, 0:40, :]
                shift = (c * GROUP - (y % 4) * 32) % LANES
                lines.append(pltpu.roll(tile, shift, 1) if shift else tile)
            q = jnp.where(chunk == 0, lines[0], jnp.where(chunk == 1, lines[1], lines[2]))
            out = jnp.where(inner == 0, q, pltpu.roll(q, 1, 1))
            out = jnp.where(inner > 1, pltpu.roll(q, 2, 1), out)
            out = jnp.where(inner > 19, pltpu.roll(q, 6, 1), out)
            out = jnp.where(inner > 37, pltpu.roll(q, 7, 1), out)
            out = jnp.where(inner > 38, pltpu.roll(q, 8, 1), out)
            packed[m, k, 0:40, :] = jnp.where(chunk < 3, out, 1.0)
            packed[m, k, 40:48, :] = jnp.ones((8, LANES), F32)
        return carry

    lax.fori_loop(0, 3, body, 0)


def pack_twin(ext, matrix, pairs, small, packed):
    lane = lane_iota(24)
    chunk = groups(lane)
    half = jnp.zeros_like(lane)
    for s in range(1, 7):
        half = half + (lane >= 20 * s).astype(jnp.int32)
    weights = matrix[...]

    def body(m, carry):
        for t in range(18):
            first = ext[m, t, pl.ds(0, 24, stride=2), :]
            second = ext[m, t, pl.ds(1, 24, stride=2), :]
            pairs[t * 24:(t + 1) * 24, :] = first + second
        value = pairs[...]
        high = value.astype(jnp.bfloat16)
        rest = value - high.astype(F32)
        mid = rest.astype(jnp.bfloat16)
        low = (rest - mid.astype(F32)).astype(jnp.bfloat16)
        small[...] = (
            jnp.dot(high, weights, preferred_element_type=F32)
            + jnp.dot(mid, weights, preferred_element_type=F32)
            + jnp.dot(low, weights, preferred_element_type=F32)
        )
        for k in range(TWIN.nk + 1):
            out = jnp.ones((24, LANES), F32)
            for c in range(3):
                y = min(TWIN.nk * c + k, TWIN.nx - 1)
                for col in range(2):
                    base = (col * 8 + y // 2) * 24
                    line = small[base:base + 24, :]
                    shift = (c * GROUP + col * 20 - (y % 2) * 20) % LANES
                    line = pltpu.roll(line, shift, 1) if shift else line
                    out = jnp.where(half == 2 * c + col, line, out)
            packed[m, k, 0:24, :] = out
            packed[m, k, 24:32, :] = jnp.ones((8, LANES), F32)
        return carry

    lax.fori_loop(0, 3, body, 0)


def face_arrays(level, packed, wt):
    nk, nx, nxr = level.nk, level.nx, level.nxr
    lane = lane_iota(nxr)
    chunk, seg, z = split_lane(level, lane)
    row = lax.broadcasted_iota(jnp.int32, (nxr, LANES), 0)
    ml, mz = level.margin, level.margin_depth
    inside_xz = (row > 0) & (row < nx - 1) & (z > 0) & (z < level.zw - 1) & (chunk < 3)
    el_x = (row >= ml) & (row < ml + level.edge)
    el_z = (z >= mz) & (z < mz + level.edge_depth) & (chunk < 3)
    el_xf = (row >= ml) & (row < ml + level.edge - 1)
    el_zf = (z >= mz) & (z < mz + level.edge_depth - 1) & (chunk < 3)

    def body(k, carry):
        y = chunk * nk + k
        inside = inside_xz & (y > 0) & (y < nx - 1)
        el_y = (y >= ml) & (y < ml + level.edge)
        el_yf = (y >= ml) & (y < ml + level.edge - 1)
        tx = harmonic(packed[0, k, 0:nxr, :], packed[0, k, 1:nxr + 1, :], level.spacing)
        ty = harmonic(packed[1, k, 0:nxr, :], packed[1, k + 1, 0:nxr, :], level.spacing)
        kz = packed[2, k, 0:nxr, :]
        tz = harmonic(kz, pltpu.roll(kz, LANES - 1, 1), level.spacing)
        wt[0, k] = tx
        wt[1, k] = ty
        wt[2, k] = tz
        wt[3, k] = jnp.where(inside, tx - pltpu.roll(tx, 1, 0), 0.0)
        wt[5, k] = jnp.where(inside, tz - pltpu.roll(tz, 1, 1), 0.0)
        wt[6, k] = jnp.where(el_xf & el_y & el_z, tx, 0.0)
        wt[7, k] = jnp.where(el_x & el_yf & el_z, ty, 0.0)
        wt[8, k] = jnp.where(el_x & el_y & el_zf, tz, 0.0)
        return carry

    lax.fori_loop(0, nk, body, 0)

    def inside_at(k):
        y = chunk * nk + k
        return inside_xz & (y > 0) & (y < nx - 1)

    wt[4, 0] = jnp.where(inside_at(0), wt[1, 0] - pltpu.roll(wt[1, nk - 1], GROUP, 1), 0.0)

    def second(k, carry):
        wt[4, k] = jnp.where(inside_at(k), wt[1, k] - wt[1, k - 1], 0.0)
        return carry

    lax.fori_loop(1, nk, second, 0)


def basis_solve(level, wt, cst, r0, r1, r2, w, store_phi):
    nk, nx = level.nk, level.nx
    lane = lane_iota(8)
    chunk, seg, z = split_lane(level, lane)
    sub = lax.broadcasted_iota(jnp.int32, (8, LANES), 0)
    ax, ay, az = sub >= 4, ((sub >> 1) & 1) == 1, (sub & 1) == 1

    def ramp(flag, place, length):
        return jnp.where(flag, place / length, 1.0 - place / length)

    fz = ramp(az, z.astype(F32) - level.margin_depth + 0.5, level.edge_depth)
    sx = jnp.where(ax, 1.0 / level.edge, -1.0 / level.edge)
    sy = jnp.where(ay, 1.0 / level.edge, -1.0 / level.edge)
    sz = jnp.where(az, 1.0 / level.edge_depth, -1.0 / level.edge_depth)
    cst[4, 0] = sy * fz
    cst[4, 1] = sx
    for k in range(nk):
        fy = ramp(ay, (chunk * nk + k).astype(F32) - level.margin + 0.5, level.edge)
        cst[0, k] = sx * fy * fz
        cst[1, k] = sz * fy
        cst[2, k] = fy * fz

    cst[4, 2] = jnp.where(ax, (0.5 - level.margin) / level.edge, 1.0 - (0.5 - level.margin) / level.edge)

    def fx_at(x):
        return cst[4, 2] + cst[4, 1] * x.astype(F32)

    def mask_at(k):
        y = chunk * nk + k
        return (y > 0) & (y < nx - 1) & (z > 0) & (z < level.zw - 1) & (chunk < 3)

    cst[4, 3] = jnp.zeros((8, LANES), F32)
    zero = cst[4, 3]

    def row(n, k, x):
        return wt[n, k, pl.ds(x, 8, stride=0), :]

    def operate(base, x, u_new, u_prev, fx_prev):
        fx_new, image = [], []
        fy_last = row(base + 1, nk - 1, x) * (u_prev[nk - 1] - pltpu.roll(u_prev[0], LANES - GROUP, 1))
        fy_prev = pltpu.roll(fy_last, GROUP, 1)
        for k in range(nk):
            flux = row(base, k, x) * (u_prev[k] - u_new[k])
            fx_new.append(flux)
            out = flux - fx_prev[k]
            fy = fy_last if k == nk - 1 else row(base + 1, k, x) * (u_prev[k] - u_prev[k + 1])
            out = out + (fy - fy_prev)
            fy_prev = fy
            fz_flux = row(base + 2, k, x) * (u_prev[k] - pltpu.roll(u_prev[k], LANES - 1, 1))
            image.append(out + (fz_flux - pltpu.roll(fz_flux, 1, 1)))
        return fx_new, image

    def sweep(produce, keep_u, keep_w):
        def body(x, carry):
            u_prev, fx_prev, rr, rw = carry
            u_new = produce(x)
            if keep_u is not None:
                for k in range(nk):
                    keep_u[x, k] = u_new[k]
            fx_new, image = operate(0, x - 1, u_new, u_prev, fx_prev)
            for k in range(nk):
                if keep_w is not None:
                    keep_w[x - 1, k] = image[k]
                rr = rr + u_prev[k] * u_prev[k]
                rw = rw + u_prev[k] * image[k]
            return u_new, fx_new, rr, rw

        start = ([zero] * nk, [zero] * nk, zero, zero)
        _, _, rr, rw = lax.fori_loop(1, nx, body, start)
        return rr, rw

    def by_segment(acc):
        out = zero
        for s in range(level.nseg):
            total = jnp.sum(jnp.where(seg == s, acc, 0.0), axis=1, keepdims=True)
            out = jnp.where(seg == s, total, out)
        return out

    for k in range(nk):
        w[nx - 1, k] = zero

    def first(x):
        fx = fx_at(x)
        return [
            row(3, k, x) * cst[0, k] + fx * (row(4, k, x) * cst[4, 0] + row(5, k, x) * cst[1, k])
            for k in range(nk)
        ]

    rr, rw = sweep(first, r0, w)
    rr0, rw0 = by_segment(rr), by_segment(rw)
    alpha0 = rr0 / rw0
    for k in range(nk):
        cst[3, k] = jnp.where(mask_at(k), alpha0, 0.0)
    rr, rw = sweep(lambda x: [r0[x, k] - cst[3, k] * w[x, k] for k in range(nk)], r1, w)
    rr1, rw1 = by_segment(rr), by_segment(rw)
    beta0 = rr1 / rr0
    alpha1 = rr1 / (rw1 - beta0 / alpha0 * rr1)
    gamma = alpha1 * beta0 / alpha0
    for k in range(nk):
        cst[3, k] = jnp.where(mask_at(k), alpha1, 0.0)

    def third(x):
        return [
            r1[x, k] + gamma * (r1[x, k] - r0[x, k]) - cst[3, k] * w[x, k] for k in range(nk)
        ]

    rr, rw = sweep(third, r2, None)
    rr2, rw2 = by_segment(rr), by_segment(rw)
    beta1 = rr2 / rr1
    alpha2 = rr2 / (rw2 - beta1 / alpha1 * rr2)
    c2 = alpha2
    c1 = alpha1 + alpha2 * beta1
    c0 = alpha0 + c1 * beta0

    def basis(x):
        fx = fx_at(x)
        return [
            fx * cst[2, k] + (c0 * r0[x, k] + (c1 * r1[x, k] + c2 * r2[x, k])) for k in range(nk)
        ]

    low = level.margin
    high = level.margin + level.edge

    def body(x, carry):
        u_prev, fx_prev, acc = carry
        u_new = basis(x)
        fx_new, image = operate(6, x - 1, u_new, u_prev, fx_prev)
        acc = list(acc)
        for k in range(nk):
            store_phi(x - 1 - low, k, u_prev[k])
            for s in range(5):
                turned = pltpu.roll(image[k], 8 - s, 0) if s else image[k]
                acc[s] = acc[s] + u_prev[k] * turned
        return u_new, fx_new, tuple(acc)

    start = (basis(jnp.int32(low)), [zero] * nk, (zero,) * 5)
    _, _, acc = lax.fori_loop(low + 1, high + 1, body, start)
    return acc, seg


def stencil(level, acc, seg, masks, elements):
    out = jnp.zeros((8, LANES), F32)
    for e, s in enumerate(elements):
        for n in range(5):
            total = jnp.sum(jnp.where(seg == s, acc[n], 0.0), axis=1, keepdims=True)
            out = out + total * masks[e * 5 + n]
    return out


def local_kernel(own, hx, hy, hc, matrix, masks, phi_f, phi_t, line, ext, pairs, small, pk_f, pk_t,
                 wt_f, wt_t, cst_f, cst_t, f0, f1, f2, fw, g0, g1, g2, gw):
    assemble(own, hx, hy, hc, ext)
    pack_twin(ext, matrix, pairs, small, pk_t)
    face_arrays(TWIN, pk_t, wt_t)

    def store_twin(x, k, value):
        phi_t[x, k] = value

    acc, seg = basis_solve(TWIN, wt_t, cst_t, g0, g1, g2, gw, store_twin)
    parts = [stencil(TWIN, acc, seg, masks, (2 * col, 2 * col + 1)) for col in range(2)]
    total = pltpu.roll(parts[0], 32, 1) + pltpu.roll(parts[1], 48, 1)

    def body(col, total):
        pack_fine(ext, pk_f, col)
        face_arrays(FINE, pk_f, wt_f)

        def store_fine(x, k, value):
            phi_f[col, x, k] = value

        acc, seg = basis_solve(FINE, wt_f, cst_f, f0, f1, f2, fw, store_fine)
        part = stencil(FINE, acc, seg, masks, (0, 1))
        here = jnp.full((8, LANES), col, jnp.int32) == 0
        return total + jnp.where(here, part, pltpu.roll(part, 16, 1))

    total = lax.fori_loop(0, 2, body, total)
    line[...] = jnp.broadcast_to(jnp.sum(total, axis=0, keepdims=True), (8, LANES))


def local_solve(perm, hx, hy, hc):
    vmem = pl.BlockSpec(memory_space=pltpu.VMEM)

    def fields(level):
        return [pltpu.VMEM((level.nx, level.nk, 8, LANES), F32)] * 4

    def scratch(level):
        return (
            pltpu.VMEM((3, level.nk + 1, level.nxr + 8, LANES), F32),
            pltpu.VMEM((9, level.nk, level.nxr, LANES), F32),
            pltpu.VMEM((5, level.nk, 8, LANES), F32),
        )

    pk_f, wt_f, cst_f = scratch(FINE)
    pk_t, wt_t, cst_t = scratch(TWIN)
    return pl.pallas_call(
        local_kernel,
        out_shape=(
            jax.ShapeDtypeStruct((2, EL, FINE.nk, 8, LANES), F32),
            jax.ShapeDtypeStruct((EL // 2, TWIN.nk, 8, LANES), F32),
            jax.ShapeDtypeStruct((8, LANES), F32),
        ),
        in_specs=[vmem] * 6,
        out_specs=(vmem,) * 3,
        scratch_shapes=[
            pltpu.VMEM((3, 18, 48, LANES), F32),
            pltpu.VMEM((18 * 24, LANES), F32),
            pltpu.VMEM((18 * 24, LANES), F32),
            pk_f, pk_t, wt_f, wt_t, cst_f, cst_t,
        ] + fields(FINE) + fields(TWIN),
        compiler_params=pltpu.CompilerParams(vmem_limit_bytes=VLIMIT),
    )(
        perm, hx, hy, hc,
        jnp.asarray(coarsen_matrix(), jnp.bfloat16), jnp.asarray(stencil_masks()),
    )


def coarse_solve(quantity, lane):
    second = (lane & 63) >= 32
    place = lane & 31

    def next_q(x):
        same = pltpu.roll(x, LANES - 32, 1)
        inner = pltpu.roll(x, 31, 1)
        outer = pltpu.roll(x, 63, 1)
        return jnp.where(second, jnp.where(place < 31, inner, outer), same)

    def prev_q(x):
        same = pltpu.roll(x, 32, 1)
        inner = pltpu.roll(x, LANES - 31, 1)
        outer = pltpu.roll(x, LANES - 63, 1)
        return jnp.where(second, same, jnp.where(place > 0, inner, outer))

    def next_p(x):
        return pltpu.roll(x, 7, 0)

    def prev_p(x):
        return pltpu.roll(x, 1, 0)

    entry = {}
    n = 0
    for a in range(4):
        for b in range(a, 4):
            entry[a, b] = entry[b, a] = quantity(n)
            n += 1

    def corners(x):
        side = next_q(x)
        return [x, side, next_p(x), next_p(side)]

    def gather(parts):
        side = prev_q(parts[1] + prev_p(parts[3]))
        return parts[0] + side + prev_p(parts[2])

    def operate(x):
        values = corners(x)
        parts = []
        for a in range(4):
            terms = [entry[a, b] * values[b] for b in range(4)]
            parts.append((terms[0] + terms[1]) + (terms[2] + terms[3]))
        return gather(parts)

    upper = lane >= 64

    def total(x):
        column = jnp.sum(x, axis=0, keepdims=True)
        lo = jnp.sum(jnp.where(upper[:1], 0.0, column), axis=1, keepdims=True)
        hi = jnp.sum(jnp.where(upper[:1], column, 0.0), axis=1, keepdims=True)
        return jnp.where(upper, hi, lo)

    residual = -gather([quantity(10 + a) for a in range(4)])
    norm = total(residual * residual)
    image = operate(residual)
    alpha = norm / total(residual * image)
    update = alpha * residual
    after = residual - alpha * image
    norm_next = total(after * after)
    direction = after + norm_next / norm * residual
    image = operate(direction)
    alpha = norm_next / total(direction * image)
    update = update + alpha * direction
    return [value for value in corners(update)]


def coarse_kernel(line, nodes, rows, block, grid, send1, recv1, send2, recv2):
    i = lax.axis_index("gx")
    j = lax.axis_index("gy")
    ni = lax.axis_size("gx")
    nj = lax.axis_size("gy")
    barrier = pltpu.get_barrier_semaphore()

    def greet_y(d, carry):
        pl.semaphore_signal(barrier, inc=1, device_id=(i, lax.rem(j + d, nj)), device_id_type=MESH)
        return carry

    def greet_x(d, carry):
        pl.semaphore_signal(barrier, inc=1, device_id=(lax.rem(i + d, ni), j), device_id_type=MESH)
        return carry

    lax.fori_loop(1, nj, greet_y, 0)
    lax.fori_loop(1, ni, greet_x, 0)
    pl.semaphore_wait(barrier, ni + nj - 2)

    def copy_y(d):
        return pltpu.make_async_remote_copy(
            src_ref=line, dst_ref=rows.at[j], send_sem=send1.at[d], recv_sem=recv1.at[d],
            device_id=(i, lax.rem(j + d, nj)), device_id_type=MESH,
        )

    def copy_x(d):
        return pltpu.make_async_remote_copy(
            src_ref=block, dst_ref=grid.at[i], send_sem=send2.at[d], recv_sem=recv2.at[d],
            device_id=(lax.rem(i + d, ni), j), device_id_type=MESH,
        )

    def start_y(d, carry):
        copy_y(d).start()
        return carry

    def wait_y(d, carry):
        copy_y(d).wait()
        return carry

    def start_x(d, carry):
        copy_x(d).start()
        return carry

    def wait_x(d, carry):
        copy_x(d).wait()
        return carry

    lax.fori_loop(1, nj, start_y, 0)
    rows[j] = line[...]
    lax.fori_loop(1, nj, wait_y, 0)
    quarter = rows[:, 0, :]
    turned = jnp.transpose(jnp.concatenate([quarter] * 4, axis=0))
    lane16 = lane_iota(16)
    out = turned[48:64]
    for b in range(3):
        out = jnp.where((lane16 >= 32 * b) & (lane16 < 32 * b + 32), turned[16 * b:16 * b + 16], out)
    block[...] = out
    lax.fori_loop(1, ni, start_x, 0)
    grid[i] = out
    lax.fori_loop(1, ni, wait_x, 0)
    values = coarse_solve(lambda q: grid[:, q, :], lane_iota(8))
    for a in range(4):
        nodes[a] = values[a]


def coarse(line, ni, nj):
    vmem = pl.BlockSpec(memory_space=pltpu.VMEM)
    return pl.pallas_call(
        coarse_kernel,
        out_shape=jax.ShapeDtypeStruct((4, 8, LANES), F32),
        in_specs=[vmem],
        out_specs=vmem,
        scratch_shapes=[
            pltpu.VMEM((nj, 8, LANES), F32),
            pltpu.VMEM((16, LANES), F32),
            pltpu.VMEM((ni, 16, LANES), F32),
            pltpu.SemaphoreType.DMA((nj,)),
            pltpu.SemaphoreType.DMA((nj,)),
            pltpu.SemaphoreType.DMA((ni,)),
            pltpu.SemaphoreType.DMA((ni,)),
        ],
        compiler_params=pltpu.CompilerParams(collective_id=1, has_side_effects=True),
    )(line)


def fold_rows(values, sub):
    low = sub < 4
    step = [
        jnp.where(low, values[n], values[n + 4])
        + pltpu.roll(jnp.where(low, values[n + 4], values[n]), 4, 0)
        for n in range(4)
    ]
    for shift in (2, 1):
        keep = (sub & shift) == 0
        step = [
            jnp.where(
                keep,
                step[n] + pltpu.roll(step[n], 8 - shift, 0),
                step[n + shift] + pltpu.roll(step[n + shift], shift, 0),
            )
            for n in range(shift)
        ]
    return step[0]


def pressure_kernel(phi_f, phi_t, nodes, fine, twin, rows_f, rows_t):
    i = lax.axis_index("gx")
    j = lax.axis_index("gy")
    sub = lax.broadcasted_iota(jnp.int32, (8, LANES), 0)
    lane = lane_iota(8)
    corner, az = sub >> 1, (sub & 1) == 1

    def own_nodes(level, col):
        here = (sub == i) & (lane == level * 64 + col * 32 + j)
        out = jnp.zeros((8, LANES), F32)
        for a in range(4):
            value = jnp.where(here, nodes[a], 0.0)
            value = jnp.sum(jnp.sum(value, axis=0, keepdims=True), axis=1, keepdims=True)
            out = jnp.where(corner == a, value, out)
        return jnp.where(az, out, 1.0), jnp.where(az, 0.0, out)

    _, seg, _ = split_lane(FINE, lane)
    fine_weights = []
    for col in range(2):
        first, second = own_nodes(0, col)
        fine_weights.append(jnp.where(seg == 0, first, second))
    _, seg, _ = split_lane(TWIN, lane)
    twin_weights = jnp.zeros((8, LANES), F32)
    for col in range(2):
        first, second = own_nodes(1, col)
        twin_weights = jnp.where(seg == 2 * col, first, twin_weights)
        twin_weights = jnp.where(seg == 2 * col + 1, second, twin_weights)

    def fine_rows(k, carry):
        for col in range(2):
            for g in range(EL // 8):
                values = [phi_f[col, 8 * g + n, k] * fine_weights[col] for n in range(8)]
                rows_f[col, k, 8 * g:8 * g + 8, :] = fold_rows(values, sub)
        return carry

    lax.fori_loop(0, FINE.nk, fine_rows, 0)

    def twin_rows(k, carry):
        for g in range(EL // 16):
            values = [phi_t[8 * g + n, k] * twin_weights for n in range(8)]
            rows_t[k, 8 * g:8 * g + 8, :] = fold_rows(values, sub)
        return carry

    lax.fori_loop(0, TWIN.nk, twin_rows, 0)

    def turn(value, shift):
        return pltpu.roll(value, shift % LANES, 1) if shift % LANES else value

    wide = lane_iota(EL)
    for col in range(2):
        for t in range(8):
            out = None
            for h in range(4):
                y = 4 * t + h + MX
                c, k = y // FINE.nk, y % FINE.nk
                for e in range(2):
                    to = h * 32 + e * 16
                    piece = turn(rows_f[col, k], to - (c * GROUP + e * 20 + MZ))
                    out = piece if out is None else jnp.where(wide >= to, piece, out)
            fine[:, (col * 8 + t) * LANES:(col * 8 + t + 1) * LANES] = out
    wide = lane_iota(EL // 2)
    for t in range(4):
        out = None
        for h in range(8):
            col, y = (8 * t + h) // 16, (8 * t + h) % 16 + MX // 2
            c, k = y // TWIN.nk, y % TWIN.nk
            for e in range(2):
                to = h * 16 + e * 8
                piece = turn(rows_t[k], to - (c * GROUP + col * 20 + e * 10 + MZ // 2))
                out = piece if out is None else jnp.where(wide >= to, piece, out)
        twin[:, t * LANES:(t + 1) * LANES] = out


def pressures(phi_f, phi_t, nodes):
    vmem = pl.BlockSpec(memory_space=pltpu.VMEM)
    return pl.pallas_call(
        pressure_kernel,
        out_shape=(
            jax.ShapeDtypeStruct((EL, 2048), F32),
            jax.ShapeDtypeStruct((EL // 2, 512), F32),
        ),
        in_specs=[vmem] * 3,
        out_specs=(vmem, vmem),
        scratch_shapes=[
            pltpu.VMEM((2, FINE.nk, EL, LANES), F32),
            pltpu.VMEM((TWIN.nk, EL // 2, LANES), F32),
        ],
        compiler_params=pltpu.CompilerParams(vmem_limit_bytes=VLIMIT),
    )(phi_f, phi_t, nodes)


def solution(mesh):
    ni, nj = mesh.shape["gx"], mesh.shape["gy"]

    def shards(perm):
        hx, hy, hc = halo(perm)
        phi_f, phi_t, line = local_solve(perm, hx, hy, hc)
        nodes = coarse(line, ni, nj)
        return pressures(phi_f, phi_t, nodes)

    return jax.shard_map(
        shards,
        mesh=mesh,
        in_specs=(P(None, "gx", "gy"),),
        out_specs=(P("gx", "gy"), P("gx", "gy")),
        check_vma=False,
    )
```

```python
import functools

import jax
import jax.numpy as jnp
import numpy as np
from jax import lax
from jax.experimental import pallas as pl
from jax.experimental.pallas import tpu as pltpu
from jax.sharding import PartitionSpec as P

EL = 32
ELZ = 16
MX = 4
MZ = 2
LANES = 128
GROUP = 40
MESH = pl.DeviceIdType.MESH
F32 = jnp.float32
VLIMIT = 60 * 1024 * 1024
FINE_PLANES = (4, 4)
TWIN_PLANES = (10, 8)


class Level:
    def __init__(self, nk, nx, zw, edge, edge_depth, margin, margin_depth, spacing):
        self.nk = nk
        self.nx = nx
        self.nxr = -(-nx // 8) * 8
        self.zw = zw
        self.nseg = GROUP // zw
        self.edge = edge
        self.edge_depth = edge_depth
        self.margin = margin
        self.margin_depth = margin_depth
        self.spacing = spacing


FINE = Level(13, 40, 20, EL, ELZ, MX, MZ, 1.0)
TWIN = Level(7, 20, 10, EL // 2, ELZ // 2, MX // 2, MZ // 2, 2.0)


def stencil_masks():
    masks = np.zeros((10, 8, LANES), np.float32)

    def put(e, a, b, q):
        s = (b - a) % 8
        if s > 4:
            a, s = b, 8 - s
        masks[e * 5 + s, a, q] += 1.0

    q = 0
    for a in range(4):
        for b in range(a, 4):
            put(0, 2 * a + 1, 2 * b + 1, q)
            put(1, 2 * a, 2 * b, q)
            q += 1
    for a in range(4):
        for b in range(4):
            put(0, 2 * a + 1, 2 * b, q)
        q += 1
    return masks


def coarsen_matrix():
    matrix = np.zeros((LANES, LANES), np.float32)
    for h in range(4):
        for e in range(2):
            for zz in range(10):
                for part in range(2):
                    z = min(max(e * ELZ - MZ + 2 * zz + part, 0), 31)
                    matrix[h * 32 + z, (h // 2) * 20 + e * 10 + zz] += 0.125
    return matrix


def lane_iota(rows):
    return lax.broadcasted_iota(jnp.int32, (rows, LANES), 1)


def groups(lane):
    return (lane >= 40).astype(jnp.int32) + (lane >= 80).astype(jnp.int32) + (lane >= 120).astype(jnp.int32)


def split_lane(level, lane):
    chunk = groups(lane)
    inner = lane - GROUP * chunk
    seg = jnp.zeros_like(lane)
    for s in range(1, level.nseg):
        seg = seg + (inner >= s * level.zw).astype(jnp.int32)
    return chunk, seg, inner - level.zw * seg


def harmonic(first, second, spacing):
    return spacing * 2.0 * first * second / (first + second)


def halo_kernel(perm, west, east, hx, hy, hc, send, recv):
    i = lax.axis_index("gx")
    j = lax.axis_index("gy")
    ni = lax.axis_size("gx")
    nj = lax.axis_size("gy")
    up, down = lax.rem(i + 1, ni), lax.rem(i + ni - 1, ni)
    right, left = lax.rem(j + 1, nj), lax.rem(j + nj - 1, nj)
    width = perm.shape[2]
    low, high = pl.ds(0, LANES), pl.ds(width - LANES, LANES)
    plans = [
        (east, hx.at[0], (up, j)),
        (west, hx.at[1], (down, j)),
        (perm.at[:, :, high], hy.at[0], (i, right)),
        (perm.at[:, :, low], hy.at[1], (i, left)),
        (east.at[:, :, high], hc.at[0], (up, right)),
        (east.at[:, :, low], hc.at[1], (up, left)),
        (west.at[:, :, high], hc.at[2], (down, right)),
        (west.at[:, :, low], hc.at[3], (down, left)),
    ]
    barrier = pltpu.get_barrier_semaphore()
    for _, _, target in plans:
        pl.semaphore_signal(barrier, inc=1, device_id=target, device_id_type=MESH)
    pl.semaphore_wait(barrier, 8)
    copies = []
    for n, (src, dst, target) in enumerate(plans):
        copy = pltpu.make_async_remote_copy(
            src_ref=src, dst_ref=dst, send_sem=send.at[n], recv_sem=recv.at[n],
            device_id=target, device_id_type=MESH,
        )
        copy.start()
        copies.append(copy)
    for copy in copies:
        copy.wait()


def halo(perm):
    rows, width = perm.shape[1], perm.shape[2]
    west = perm[:, :MX]
    east = perm[:, rows - MX:]
    anywhere = pl.BlockSpec(memory_space=pl.ANY)
    return pl.pallas_call(
        halo_kernel,
        out_shape=(
            jax.ShapeDtypeStruct((2, 3, MX, width), F32),
            jax.ShapeDtypeStruct((2, 3, rows, LANES), F32),
            jax.ShapeDtypeStruct((4, 3, MX, LANES), F32),
        ),
        in_specs=[anywhere] * 3,
        out_specs=(anywhere,) * 3,
        scratch_shapes=[pltpu.SemaphoreType.DMA((8,)), pltpu.SemaphoreType.DMA((8,))],
        compiler_params=pltpu.CompilerParams(collective_id=0, has_side_effects=True),
    )(perm, west, east)


def assemble(own, hx, hy, hc, ext):
    rows = own.shape[1]

    def body(m, carry):
        for t in range(18):
            if t == 0:
                top, mid, low = hc[0, m], hy[0, m], hc[2, m]
            elif t == 17:
                top, mid, low = hc[1, m], hy[1, m], hc[3, m]
            else:
                lanes = pl.ds((t - 1) * LANES, LANES)
                top, mid, low = hx[0, m, :, lanes], own[m, :, lanes], hx[1, m, :, lanes]
            ext[m, t, 0:MX, :] = top
            ext[m, t, MX:MX + rows, :] = mid
            ext[m, t, MX + rows:2 * MX + rows, :] = low
            ext[m, t, 2 * MX + rows:, :] = jnp.ones((8, LANES), F32)
        return carry

    lax.fori_loop(0, 3, body, 0)


def pack_fine(ext, packed, merged, column):
    lane = lane_iota(GROUP)
    chunk, _, _ = split_lane(FINE, lane)
    inner = lane - GROUP * chunk

    def body(m, carry):
        for k in range(FINE.nk + 1):
            lines = []
            for c in range(3):
                y = FINE.nk * c + k
                tile = ext[m, column * 8 + y // 4, 0:40, :]
                shift = (c * GROUP + MZ - (y % 4) * 32) % LANES
                lines.append(pltpu.roll(tile, shift, 1) if shift else tile)
            merged[m, k] = jnp.where(lane < GROUP, lines[0], jnp.where(lane < 2 * GROUP, lines[1], lines[2]))
        return carry

    lax.fori_loop(0, 3, body, 0)

    def widen(m, carry):
        for k in range(FINE.nk + 1):
            q = merged[m, k]
            out = jnp.where(inner < MZ, pltpu.roll(q, LANES - 1, 1), q)
            out = jnp.where(inner > 19, pltpu.roll(q, 4, 1), out)
            packed[m, k, 0:40, :] = jnp.where(inner > 37, pltpu.roll(q, 5, 1), out)
            packed[m, k, 40:48, :] = jnp.ones((8, LANES), F32)
        return carry

    lax.fori_loop(0, 3, widen, 0)


def pack_twin(ext, matrix, pairs, small, packed):
    lane = lane_iota(24)
    chunk = groups(lane)
    half = jnp.zeros_like(lane)
    for s in range(1, 7):
        half = half + (lane >= 20 * s).astype(jnp.int32)
    weights = matrix[...]

    def body(m, carry):
        for t in range(18):
            first = ext[m, t, pl.ds(0, 24, stride=2), :]
            second = ext[m, t, pl.ds(1, 24, stride=2), :]
            pairs[t * 24:(t + 1) * 24, :] = first + second
        value = pairs[...]
        high = value.astype(jnp.bfloat16)
        rest = value - high.astype(F32)
        mid = rest.astype(jnp.bfloat16)
        low = (rest - mid.astype(F32)).astype(jnp.bfloat16)
        small[...] = (
            jnp.dot(high, weights, preferred_element_type=F32)
            + jnp.dot(mid, weights, preferred_element_type=F32)
            + jnp.dot(low, weights, preferred_element_type=F32)
        )
        for k in range(TWIN.nk + 1):
            out = jnp.ones((24, LANES), F32)
            for c in range(3):
                y = min(TWIN.nk * c + k, TWIN.nx - 1)
                for col in range(2):
                    base = (col * 8 + y // 2) * 24
                    line = small[base:base + 24, :]
                    shift = (c * GROUP + col * 20 - (y % 2) * 20) % LANES
                    line = pltpu.roll(line, shift, 1) if shift else line
                    out = jnp.where(half == 2 * c + col, line, out)
            packed[m, k, 0:24, :] = out
            packed[m, k, 24:32, :] = jnp.ones((8, LANES), F32)
        return carry

    lax.fori_loop(0, 3, body, 0)


def face_arrays(level, packed, wt, ym, turned):
    nk, nx, nxr = level.nk, level.nx, level.nxr
    lane = lane_iota(nxr)
    chunk, seg, z = split_lane(level, lane)
    row = lax.broadcasted_iota(jnp.int32, (nxr, LANES), 0)
    ml, mz = level.margin, level.margin_depth
    inside_xz = (row > 0) & (row < nx - 1) & (z > 0) & (z < level.zw - 1) & (chunk < 3)
    el_x = (row >= ml) & (row < ml + level.edge)
    el_z = (z >= mz) & (z < mz + level.edge_depth) & (chunk < 3)
    el_xf = (row >= ml) & (row < ml + level.edge - 1)
    el_zf = (z >= mz) & (z < mz + level.edge_depth - 1) & (chunk < 3)
    first_edge = seg == 0
    if level.nseg == 4:
        first_edge = first_edge | (seg == 2)
    first_edge = first_edge & (z == 0)
    last_edge = jnp.logical_not((seg == 0) | (seg == 2)) & (z == level.zw - 2)

    el_zb = (z > mz) & (z < mz + level.edge_depth) & (chunk < 3)
    below_first = (z == 1) & ((seg == 0) | (seg == 2))
    below_last = (z == level.zw - 1) & jnp.logical_not((seg == 0) | (seg == 2))
    for k in range(nk):
        kz = packed[2, k, 0:nxr, :]
        turned[0, k] = pltpu.roll(kz, LANES - 1, 1)
        turned[1, k] = pltpu.roll(kz, 1, 1)

    def body(k, carry):
        y = chunk * nk + k
        inside = inside_xz & (y > 0) & (y < nx - 1)
        el_y = (y >= ml) & (y < ml + level.edge)
        el_yf = (y >= ml) & (y < ml + level.edge - 1)
        tx = harmonic(packed[0, k, 0:nxr, :], packed[0, k, 1:nxr + 1, :], level.spacing)
        ty = harmonic(packed[1, k, 0:nxr, :], packed[1, k + 1, 0:nxr, :], level.spacing)
        kz = packed[2, k, 0:nxr, :]
        kz_after, kz_before, kz_here = turned[0, k], turned[1, k], kz
        if level is FINE:
            kz_here = jnp.where(first_edge, kz_after, kz)
            kz_after = jnp.where(last_edge, kz, kz_after)
            kz_before = jnp.where(below_first, kz, kz_before)
            kz = jnp.where(below_last, kz_before, kz)
        tz = harmonic(kz_here, kz_after, level.spacing)
        tz_below = harmonic(kz_before, kz, level.spacing)
        wt[0, k] = tx
        wt[1, k] = ty
        wt[2, k] = tz
        wt[3, k] = tz_below
        wt[4, k] = jnp.where(inside, tx - pltpu.roll(tx, 1, 0), 0.0)
        wt[6, k] = jnp.where(inside, tz - tz_below, 0.0)
        wt[7, k] = jnp.where(el_xf & el_y & el_z, tx, 0.0)
        wt[8, k] = jnp.where(el_x & el_yf & el_z, ty, 0.0)
        wt[9, k] = jnp.where(el_x & el_y & el_zf, tz, 0.0)
        wt[10, k] = jnp.where(el_x & el_y & el_zb, tz_below, 0.0)
        return carry

    lax.fori_loop(0, nk, body, 0)
    ym[0] = pltpu.roll(wt[1, nk - 1], GROUP, 1)
    ym[1] = pltpu.roll(wt[8, nk - 1], GROUP, 1)

    def inside_at(k):
        y = chunk * nk + k
        return inside_xz & (y > 0) & (y < nx - 1)

    wt[5, 0] = jnp.where(inside_at(0), wt[1, 0] - ym[0], 0.0)

    def second(k, carry):
        wt[5, k] = jnp.where(inside_at(k), wt[1, k] - wt[1, k - 1], 0.0)
        return carry

    lax.fori_loop(1, nk, second, 0)


def basis_solve(level, wt, ym, cst, r0, r1, r2, w, above, below, beside, phi, planes):
    nk, nx = level.nk, level.nx
    lane = lane_iota(8)
    chunk, seg, z = split_lane(level, lane)
    sub = lax.broadcasted_iota(jnp.int32, (8, LANES), 0)
    ax, ay, az = sub >= 4, ((sub >> 1) & 1) == 1, (sub & 1) == 1

    def ramp(flag, place, length):
        return jnp.where(flag, place / length, 1.0 - place / length)

    fz = ramp(az, z.astype(F32) - level.margin_depth + 0.5, level.edge_depth)
    sx = jnp.where(ax, 1.0 / level.edge, -1.0 / level.edge)
    sy = jnp.where(ay, 1.0 / level.edge, -1.0 / level.edge)
    sz = jnp.where(az, 1.0 / level.edge_depth, -1.0 / level.edge_depth)
    cst[4, 0] = sy * fz
    cst[4, 1] = sx
    for k in range(nk):
        fy = ramp(ay, (chunk * nk + k).astype(F32) - level.margin + 0.5, level.edge)
        cst[0, k] = sx * fy * fz
        cst[1, k] = sz * fy
        cst[2, k] = fy * fz

    cst[4, 2] = jnp.where(ax, (0.5 - level.margin) / level.edge, 1.0 - (0.5 - level.margin) / level.edge)

    def fx_at(x):
        return cst[4, 2] + cst[4, 1] * x.astype(F32)

    def mask_at(k):
        y = chunk * nk + k
        return (y > 0) & (y < nx - 1) & (z > 0) & (z < level.zw - 1) & (chunk < 3)

    cst[4, 3] = jnp.zeros((8, LANES), F32)
    zero = cst[4, 3]

    def row(n, k, x):
        return wt[n, k, pl.ds(x, 8, stride=0), :]

    def pipeline(base, low, high, depth, produce, keep, keep_w, consume, state):
        def apply(x0, after, fx_prev, state):
            ahead = [keep[x0, k] for k in range(nk)]
            for p in range(depth):
                x = x0 + p
                u = ahead
                ahead = after if p == depth - 1 else [keep[x + 1, k] for k in range(nk)]
                fy_prev = ym[base // 7, pl.ds(x, 8, stride=0), :] * (beside[x, 1] - u[0])
                image, fx_new = [], []
                for k in range(nk):
                    flux = row(base, k, x) * (u[k] - ahead[k])
                    fx_new.append(flux)
                    out = flux - fx_prev[k]
                    side = u[k + 1] if k < nk - 1 else beside[x, 0]
                    fy = row(base + 1, k, x) * (u[k] - side)
                    out = out + (fy - fy_prev)
                    fy_prev = fy
                    out = out + row(base + 2, k, x) * (u[k] - above[x, k])
                    image.append(out + row(base + 3, k, x) * (u[k] - below[x, k]))
                fx_prev = fx_new
                if keep_w is not None:
                    for k in range(nk):
                        keep_w[x, k] = image[k]
                for k in range(nk):
                    state = consume(state, u[k], image[k])
            return fx_prev, state

        def store(x0, block):
            for p in range(depth):
                u = block[p]
                for k in range(nk):
                    keep[x0 + p, k] = u[k]
                    above[x0 + p, k] = pltpu.roll(u[k], LANES - 1, 1)
                    below[x0 + p, k] = pltpu.roll(u[k], 1, 1)
                beside[x0 + p, 0] = pltpu.roll(u[0], LANES - GROUP, 1)
                beside[x0 + p, 1] = pltpu.roll(u[nk - 1], GROUP, 1)

        def make(x0):
            return [produce(x0 + p) for p in range(depth)]

        start = jnp.int32(low)
        block = make(start)
        fx_prev = [zero] * nk
        store(start, block)

        def body(n, carry):
            fx_prev, state = carry
            x0 = low + n * depth
            block = make(x0)
            fx_prev, state = apply(x0 - depth, block[0], fx_prev, state)
            store(x0, block)
            return fx_prev, state

        count = (high - low) // depth
        fx_prev, state = lax.fori_loop(1, count, body, (fx_prev, state))
        _, state = apply(jnp.int32(high - depth), [zero] * nk, fx_prev, state)
        return state

    def norms(state, u, image):
        return state[0] + u * u, state[1] + u * image

    def sweep(produce, keep, keep_w):
        state = pipeline(0, 0, nx, planes[0], produce, keep, keep_w, norms, (zero, zero))
        if keep_w is not None:
            for k in range(nk):
                keep_w[0, k] = zero
                keep_w[nx - 1, k] = zero
        return by_segment(state[0]), by_segment(state[1])

    def by_segment(acc):
        out = jnp.sum(jnp.where(seg == 0, acc, 0.0), axis=1, keepdims=True)
        for s in range(1, level.nseg):
            total = jnp.sum(jnp.where(seg == s, acc, 0.0), axis=1, keepdims=True)
            out = jnp.where(seg == s, total, out)
        return out

    def first(x):
        fx = fx_at(x)
        return [
            row(4, k, x) * cst[0, k] + fx * (row(5, k, x) * cst[4, 0] + row(6, k, x) * cst[1, k])
            for k in range(nk)
        ]

    rr0, rw0 = sweep(first, r0, w)
    alpha0 = rr0 / rw0
    for k in range(nk):
        cst[3, k] = jnp.where(mask_at(k), alpha0, 0.0)
    rr1, rw1 = sweep(lambda x: [r0[x, k] - cst[3, k] * w[x, k] for k in range(nk)], r1, w)
    beta0 = rr1 / rr0
    alpha1 = rr1 / (rw1 - beta0 / alpha0 * rr1)
    gamma = alpha1 * beta0 / alpha0
    for k in range(nk):
        cst[3, k] = jnp.where(mask_at(k), alpha1, 0.0)

    def third(x):
        return [
            r1[x, k] + gamma * (r1[x, k] - r0[x, k]) - cst[3, k] * w[x, k] for k in range(nk)
        ]

    rr2, rw2 = sweep(third, r2, None)
    beta1 = rr2 / rr1
    alpha2 = rr2 / (rw2 - beta1 / alpha1 * rr2)
    c2 = alpha2
    c1 = alpha1 + alpha2 * beta1
    c0 = alpha0 + c1 * beta0
    low = level.margin

    def basis(x):
        fx = fx_at(x)
        return [
            fx * cst[2, k] + (c0 * r0[x, k] + (c1 * r1[x, k] + c2 * r2[x, k])) for k in range(nk)
        ]

    def diagonals(state, u, image):
        return tuple(
            state[s] + u * (pltpu.roll(image, 8 - s, 0) if s else image) for s in range(5)
        )

    acc = pipeline(7, low, low + level.edge, planes[1], basis, phi, None, diagonals, (zero,) * 5)
    return acc, seg


def stencil(level, acc, seg, masks, elements):
    out = jnp.zeros((8, LANES), F32)
    for e, s in enumerate(elements):
        for n in range(5):
            total = jnp.sum(jnp.where(seg == s, acc[n], 0.0), axis=1, keepdims=True)
            out = out + total * masks[e * 5 + n]
    return out


class Shifted:
    def __init__(self, ref, first, column=None):
        self.ref = ref
        self.first = first
        self.column = column

    def place(self, index):
        x, k = index
        return (x - self.first, k) if self.column is None else (self.column, x - self.first, k)

    def __getitem__(self, index):
        return self.ref[self.place(index)]

    def __setitem__(self, index, value):
        self.ref[self.place(index)] = value


def local_kernel(own, hx, hy, hc, matrix, masks, phi_f, phi_t, line, ext, pairs, small, merged, *scratch):
    pk_f, wt_f, ym_f, turned_f, cst_f, *fields_f = scratch[:12]
    pk_t, wt_t, ym_t, turned_t, cst_t, *fields_t = scratch[12:]
    assemble(own, hx, hy, hc, ext)
    pack_twin(ext, matrix, pairs, small, pk_t)
    face_arrays(TWIN, pk_t, wt_t, ym_t, turned_t)
    acc, seg = basis_solve(TWIN, wt_t, ym_t, cst_t, *fields_t, Shifted(phi_t, TWIN.margin), TWIN_PLANES)
    parts = [stencil(TWIN, acc, seg, masks, (2 * col, 2 * col + 1)) for col in range(2)]
    total = pltpu.roll(parts[0], 32, 1) + pltpu.roll(parts[1], 48, 1)

    def body(col, total):
        pack_fine(ext, pk_f, merged, col)
        face_arrays(FINE, pk_f, wt_f, ym_f, turned_f)
        phi = Shifted(phi_f, FINE.margin, col)
        acc, seg = basis_solve(FINE, wt_f, ym_f, cst_f, *fields_f, phi, FINE_PLANES)
        part = stencil(FINE, acc, seg, masks, (0, 1))
        here = jnp.full((8, LANES), col, jnp.int32) == 0
        return total + jnp.where(here, part, pltpu.roll(part, 16, 1))

    total = lax.fori_loop(0, 2, body, total)
    line[...] = jnp.broadcast_to(jnp.sum(total, axis=0, keepdims=True), (8, LANES))


def local_solve(perm, hx, hy, hc):
    vmem = pl.BlockSpec(memory_space=pltpu.VMEM)

    def scratch(level):
        field = pltpu.VMEM((level.nx, level.nk, 8, LANES), F32)
        return [
            pltpu.VMEM((3, level.nk + 1, level.nxr + 8, LANES), F32),
            pltpu.VMEM((11, level.nk, level.nxr, LANES), F32),
            pltpu.VMEM((2, level.nxr, LANES), F32),
            pltpu.VMEM((2, level.nk, level.nxr, LANES), F32),
            pltpu.VMEM((5, level.nk, 8, LANES), F32),
        ] + [field] * 6 + [pltpu.VMEM((level.nx, 2, 8, LANES), F32)]

    return pl.pallas_call(
        local_kernel,
        out_shape=(
            jax.ShapeDtypeStruct((2, EL, FINE.nk, 8, LANES), F32),
            jax.ShapeDtypeStruct((EL // 2, TWIN.nk, 8, LANES), F32),
            jax.ShapeDtypeStruct((8, LANES), F32),
        ),
        in_specs=[vmem] * 6,
        out_specs=(vmem,) * 3,
        scratch_shapes=[
            pltpu.VMEM((3, 18, 48, LANES), F32),
            pltpu.VMEM((18 * 24, LANES), F32),
            pltpu.VMEM((18 * 24, LANES), F32),
            pltpu.VMEM((3, FINE.nk + 1, GROUP, LANES), F32),
        ] + scratch(FINE) + scratch(TWIN),
        compiler_params=pltpu.CompilerParams(vmem_limit_bytes=VLIMIT),
    )(
        perm, hx, hy, hc,
        jnp.asarray(coarsen_matrix(), jnp.bfloat16), jnp.asarray(stencil_masks()),
    )


def coarse_solve(quantity, lane):
    second = (lane & 63) >= 32
    place = lane & 31

    def next_q(x):
        same = pltpu.roll(x, LANES - 32, 1)
        inner = pltpu.roll(x, 31, 1)
        outer = pltpu.roll(x, 63, 1)
        return jnp.where(second, jnp.where(place < 31, inner, outer), same)

    def prev_q(x):
        same = pltpu.roll(x, 32, 1)
        inner = pltpu.roll(x, LANES - 31, 1)
        outer = pltpu.roll(x, LANES - 63, 1)
        return jnp.where(second, same, jnp.where(place > 0, inner, outer))

    def next_p(x):
        return pltpu.roll(x, 7, 0)

    def prev_p(x):
        return pltpu.roll(x, 1, 0)

    entry = {}
    n = 0
    for a in range(4):
        for b in range(a, 4):
            entry[a, b] = entry[b, a] = quantity(n)
            n += 1

    def corners(x):
        side = next_q(x)
        return [x, side, next_p(x), next_p(side)]

    def gather(parts):
        side = prev_q(parts[1] + prev_p(parts[3]))
        return parts[0] + side + prev_p(parts[2])

    def operate(x):
        values = corners(x)
        parts = []
        for a in range(4):
            terms = [entry[a, b] * values[b] for b in range(4)]
            parts.append((terms[0] + terms[1]) + (terms[2] + terms[3]))
        return gather(parts)

    upper = lane >= 64

    def total(x):
        column = jnp.sum(x, axis=0, keepdims=True)
        lo = jnp.sum(jnp.where(upper[:1], 0.0, column), axis=1, keepdims=True)
        hi = jnp.sum(jnp.where(upper[:1], column, 0.0), axis=1, keepdims=True)
        return jnp.where(upper, hi, lo)

    residual = -gather([quantity(10 + a) for a in range(4)])
    norm = total(residual * residual)
    image = operate(residual)
    alpha = norm / total(residual * image)
    update = alpha * residual
    after = residual - alpha * image
    norm_next = total(after * after)
    direction = after + norm_next / norm * residual
    image = operate(direction)
    alpha = norm_next / total(direction * image)
    update = update + alpha * direction
    return [value for value in corners(update)]


def coarse_kernel(line, nodes, rows, block, grid, send1, recv1, send2, recv2):
    i = lax.axis_index("gx")
    j = lax.axis_index("gy")
    ni = lax.axis_size("gx")
    nj = lax.axis_size("gy")
    barrier = pltpu.get_barrier_semaphore()

    def greet_y(d, carry):
        pl.semaphore_signal(barrier, inc=1, device_id=(i, lax.rem(j + d, nj)), device_id_type=MESH)
        return carry

    def greet_x(d, carry):
        pl.semaphore_signal(barrier, inc=1, device_id=(lax.rem(i + d, ni), j), device_id_type=MESH)
        return carry

    lax.fori_loop(1, nj, greet_y, 0)
    lax.fori_loop(1, ni, greet_x, 0)
    pl.semaphore_wait(barrier, ni + nj - 2)

    def copy_y(d):
        return pltpu.make_async_remote_copy(
            src_ref=line, dst_ref=rows.at[j], send_sem=send1.at[d], recv_sem=recv1.at[d],
            device_id=(i, lax.rem(j + d, nj)), device_id_type=MESH,
        )

    def copy_x(d):
        return pltpu.make_async_remote_copy(
            src_ref=block, dst_ref=grid.at[i], send_sem=send2.at[d], recv_sem=recv2.at[d],
            device_id=(lax.rem(i + d, ni), j), device_id_type=MESH,
        )

    def start_y(d, carry):
        copy_y(d).start()
        return carry

    def wait_y(d, carry):
        copy_y(d).wait()
        return carry

    def start_x(d, carry):
        copy_x(d).start()
        return carry

    def wait_x(d, carry):
        copy_x(d).wait()
        return carry

    lax.fori_loop(1, nj, start_y, 0)
    rows[j] = line[...]
    lax.fori_loop(1, nj, wait_y, 0)
    quarter = rows[:, 0, :]
    turned = jnp.transpose(jnp.concatenate([quarter] * 4, axis=0))
    lane16 = lane_iota(16)
    out = turned[48:64]
    for b in range(3):
        out = jnp.where((lane16 >= 32 * b) & (lane16 < 32 * b + 32), turned[16 * b:16 * b + 16], out)
    block[...] = out
    lax.fori_loop(1, ni, start_x, 0)
    grid[i] = out
    lax.fori_loop(1, ni, wait_x, 0)
    values = coarse_solve(lambda q: grid[:, q, :], lane_iota(8))
    for a in range(4):
        nodes[a] = values[a]


def coarse(line, ni, nj):
    vmem = pl.BlockSpec(memory_space=pltpu.VMEM)
    return pl.pallas_call(
        coarse_kernel,
        out_shape=jax.ShapeDtypeStruct((4, 8, LANES), F32),
        in_specs=[vmem],
        out_specs=vmem,
        scratch_shapes=[
            pltpu.VMEM((nj, 8, LANES), F32),
            pltpu.VMEM((16, LANES), F32),
            pltpu.VMEM((ni, 16, LANES), F32),
            pltpu.SemaphoreType.DMA((nj,)),
            pltpu.SemaphoreType.DMA((nj,)),
            pltpu.SemaphoreType.DMA((ni,)),
            pltpu.SemaphoreType.DMA((ni,)),
        ],
        compiler_params=pltpu.CompilerParams(collective_id=1, has_side_effects=True),
    )(line)


def fold_rows(values, sub):
    low = sub < 4
    step = [
        jnp.where(low, values[n], values[n + 4])
        + pltpu.roll(jnp.where(low, values[n + 4], values[n]), 4, 0)
        for n in range(4)
    ]
    for shift in (2, 1):
        keep = (sub & shift) == 0
        step = [
            jnp.where(
                keep,
                step[n] + pltpu.roll(step[n], 8 - shift, 0),
                step[n + shift] + pltpu.roll(step[n + shift], shift, 0),
            )
            for n in range(shift)
        ]
    return step[0]


def pressure_kernel(phi_f, phi_t, nodes, fine, twin, rows_f, rows_t):
    i = lax.axis_index("gx")
    j = lax.axis_index("gy")
    sub = lax.broadcasted_iota(jnp.int32, (8, LANES), 0)
    lane = lane_iota(8)
    corner, az = sub >> 1, (sub & 1) == 1

    def own_nodes(level, col):
        here = (sub == i) & (lane == level * 64 + col * 32 + j)
        out = jnp.zeros((8, LANES), F32)
        for a in range(4):
            value = jnp.where(here, nodes[a], 0.0)
            value = jnp.sum(jnp.sum(value, axis=0, keepdims=True), axis=1, keepdims=True)
            out = jnp.where(corner == a, value, out)
        return jnp.where(az, out, 1.0), jnp.where(az, 0.0, out)

    _, seg, _ = split_lane(FINE, lane)
    fine_weights = []
    for col in range(2):
        first, second = own_nodes(0, col)
        fine_weights.append(jnp.where(seg == 0, first, second))
    _, seg, _ = split_lane(TWIN, lane)
    twin_weights = jnp.zeros((8, LANES), F32)
    for col in range(2):
        first, second = own_nodes(1, col)
        twin_weights = jnp.where(seg == 2 * col, first, twin_weights)
        twin_weights = jnp.where(seg == 2 * col + 1, second, twin_weights)

    def fine_rows(k, carry):
        for col in range(2):
            for g in range(EL // 8):
                values = [phi_f[col, 8 * g + n, k] * fine_weights[col] for n in range(8)]
                rows_f[col, k, 8 * g:8 * g + 8, :] = fold_rows(values, sub)
        return carry

    lax.fori_loop(0, FINE.nk, fine_rows, 0)

    def twin_rows(k, carry):
        for g in range(EL // 16):
            values = [phi_t[8 * g + n, k] * twin_weights for n in range(8)]
            rows_t[k, 8 * g:8 * g + 8, :] = fold_rows(values, sub)
        return carry

    lax.fori_loop(0, TWIN.nk, twin_rows, 0)

    def turn(value, shift):
        return pltpu.roll(value, shift % LANES, 1) if shift % LANES else value

    wide = lane_iota(EL)
    for col in range(2):
        for t in range(8):
            out = None
            for h in range(4):
                y = 4 * t + h + MX
                c, k = y // FINE.nk, y % FINE.nk
                for e in range(2):
                    to = h * 32 + e * 16
                    piece = turn(rows_f[col, k], to - (c * GROUP + e * 20 + MZ))
                    out = piece if out is None else jnp.where(wide >= to, piece, out)
            fine[:, (col * 8 + t) * LANES:(col * 8 + t + 1) * LANES] = out
    wide = lane_iota(EL // 2)
    for t in range(4):
        out = None
        for h in range(8):
            col, y = (8 * t + h) // 16, (8 * t + h) % 16 + MX // 2
            c, k = y // TWIN.nk, y % TWIN.nk
            for e in range(2):
                to = h * 16 + e * 8
                piece = turn(rows_t[k], to - (c * GROUP + col * 20 + e * 10 + MZ // 2))
                out = piece if out is None else jnp.where(wide >= to, piece, out)
        twin[:, t * LANES:(t + 1) * LANES] = out


def pressures(phi_f, phi_t, nodes):
    vmem = pl.BlockSpec(memory_space=pltpu.VMEM)
    return pl.pallas_call(
        pressure_kernel,
        out_shape=(
            jax.ShapeDtypeStruct((EL, 2048), F32),
            jax.ShapeDtypeStruct((EL // 2, 512), F32),
        ),
        in_specs=[vmem] * 3,
        out_specs=(vmem, vmem),
        scratch_shapes=[
            pltpu.VMEM((2, FINE.nk, EL, LANES), F32),
            pltpu.VMEM((TWIN.nk, EL // 2, LANES), F32),
        ],
        compiler_params=pltpu.CompilerParams(vmem_limit_bytes=VLIMIT),
    )(phi_f, phi_t, nodes)


def solution(mesh):
    ni, nj = mesh.shape["gx"], mesh.shape["gy"]

    def shards(perm):
        hx, hy, hc = halo(perm)
        phi_f, phi_t, line = local_solve(perm, hx, hy, hc)
        nodes = coarse(line, ni, nj)
        return pressures(phi_f, phi_t, nodes)

    return jax.shard_map(
        shards,
        mesh=mesh,
        in_specs=(P(None, "gx", "gy"),),
        out_specs=(P("gx", "gy"), P("gx", "gy")),
        check_vma=False,
    )
```

```python
import functools

import jax
import jax.numpy as jnp
import numpy as np
from jax import lax
from jax.experimental import pallas as pl
from jax.experimental.pallas import tpu as pltpu
from jax.sharding import PartitionSpec as P

EL = 32
ELZ = 16
MX = 4
MZ = 2
LANES = 128
GROUP = 40
MESH = pl.DeviceIdType.MESH
F32 = jnp.float32
VLIMIT = 60 * 1024 * 1024
FINE_PLANES = (4, 4)
TWIN_PLANES = (10, 8)


class Level:
    def __init__(self, nk, nx, zw, edge, edge_depth, margin, margin_depth, spacing):
        self.nk = nk
        self.nx = nx
        self.nxr = -(-nx // 8) * 8
        self.zw = zw
        self.nseg = GROUP // zw
        self.edge = edge
        self.edge_depth = edge_depth
        self.margin = margin
        self.margin_depth = margin_depth
        self.spacing = spacing


FINE = Level(13, 40, 20, EL, ELZ, MX, MZ, 1.0)
TWIN = Level(7, 20, 10, EL // 2, ELZ // 2, MX // 2, MZ // 2, 2.0)


def stencil_masks():
    masks = np.zeros((10, 8, LANES), np.float32)

    def put(e, a, b, q):
        s = (b - a) % 8
        if s > 4:
            a, s = b, 8 - s
        masks[e * 5 + s, a, q] += 1.0

    q = 0
    for a in range(4):
        for b in range(a, 4):
            put(0, 2 * a + 1, 2 * b + 1, q)
            put(1, 2 * a, 2 * b, q)
            q += 1
    for a in range(4):
        for b in range(4):
            put(0, 2 * a + 1, 2 * b, q)
        q += 1
    return masks


def coarsen_matrix():
    matrix = np.zeros((LANES, LANES), np.float32)
    for h in range(4):
        for e in range(2):
            for zz in range(10):
                for part in range(2):
                    z = min(max(e * ELZ - MZ + 2 * zz + part, 0), 31)
                    matrix[h * 32 + z, (h // 2) * 20 + e * 10 + zz] += 0.125
    return matrix


def lane_iota(rows):
    return lax.broadcasted_iota(jnp.int32, (rows, LANES), 1)


def groups(lane):
    return (lane >= 40).astype(jnp.int32) + (lane >= 80).astype(jnp.int32) + (lane >= 120).astype(jnp.int32)


def split_lane(level, lane):
    chunk = groups(lane)
    inner = lane - GROUP * chunk
    seg = jnp.zeros_like(lane)
    for s in range(1, level.nseg):
        seg = seg + (inner >= s * level.zw).astype(jnp.int32)
    return chunk, seg, inner - level.zw * seg


def harmonic(first, second, spacing):
    return spacing * 2.0 * first * second / (first + second)


def halo_kernel(perm, hx, hy, hc, send, recv):
    i = lax.axis_index("gx")
    j = lax.axis_index("gy")
    ni = lax.axis_size("gx")
    nj = lax.axis_size("gy")
    up, down = lax.rem(i + 1, ni), lax.rem(i + ni - 1, ni)
    right, left = lax.rem(j + 1, nj), lax.rem(j + nj - 1, nj)
    width = perm.shape[2]
    west, east = perm.at[:, pl.ds(0, MX)], perm.at[:, pl.ds(perm.shape[1] - MX, MX)]
    low, high = pl.ds(0, LANES), pl.ds(width - LANES, LANES)
    plans = [
        (east, hx.at[0], (up, j)),
        (west, hx.at[1], (down, j)),
        (perm.at[:, :, high], hy.at[0], (i, right)),
        (perm.at[:, :, low], hy.at[1], (i, left)),
        (east.at[:, :, high], hc.at[0], (up, right)),
        (east.at[:, :, low], hc.at[1], (up, left)),
        (west.at[:, :, high], hc.at[2], (down, right)),
        (west.at[:, :, low], hc.at[3], (down, left)),
    ]
    barrier = pltpu.get_barrier_semaphore()
    for _, _, target in plans:
        pl.semaphore_signal(barrier, inc=1, device_id=target, device_id_type=MESH)
    pl.semaphore_wait(barrier, 8)
    copies = []
    for n, (src, dst, target) in enumerate(plans):
        copy = pltpu.make_async_remote_copy(
            src_ref=src, dst_ref=dst, send_sem=send.at[n], recv_sem=recv.at[n],
            device_id=target, device_id_type=MESH,
        )
        copy.start()
        copies.append(copy)
    for copy in copies:
        copy.wait()


def halo(perm):
    rows, width = perm.shape[1], perm.shape[2]
    anywhere = pl.BlockSpec(memory_space=pl.ANY)
    return pl.pallas_call(
        halo_kernel,
        out_shape=(
            jax.ShapeDtypeStruct((2, 3, MX, width), F32),
            jax.ShapeDtypeStruct((2, 3, rows, LANES), F32),
            jax.ShapeDtypeStruct((4, 3, MX, LANES), F32),
        ),
        in_specs=[anywhere],
        out_specs=(anywhere,) * 3,
        scratch_shapes=[pltpu.SemaphoreType.DMA((8,)), pltpu.SemaphoreType.DMA((8,))],
        compiler_params=pltpu.CompilerParams(collective_id=0, has_side_effects=True),
    )(perm)


def assemble(own, hx, hy, hc, ext):
    rows = own.shape[1]

    def body(m, carry):
        for t in range(18):
            if t == 0:
                top, mid, low = hc[0, m], hy[0, m], hc[2, m]
            elif t == 17:
                top, mid, low = hc[1, m], hy[1, m], hc[3, m]
            else:
                lanes = pl.ds((t - 1) * LANES, LANES)
                top, mid, low = hx[0, m, :, lanes], own[m, :, lanes], hx[1, m, :, lanes]
            ext[m, t, 0:MX, :] = top
            ext[m, t, MX:MX + rows, :] = mid
            ext[m, t, MX + rows:2 * MX + rows, :] = low
            ext[m, t, 2 * MX + rows:, :] = jnp.ones((8, LANES), F32)
        return carry

    lax.fori_loop(0, 3, body, 0)


def pack_fine(ext, packed, merged, column):
    lane = lane_iota(GROUP)
    chunk, _, _ = split_lane(FINE, lane)
    inner = lane - GROUP * chunk

    def body(m, carry):
        for k in range(FINE.nk + 1):
            lines = []
            for c in range(3):
                y = FINE.nk * c + k
                tile = ext[m, column * 8 + y // 4, 0:40, :]
                shift = (c * GROUP + MZ - (y % 4) * 32) % LANES
                lines.append(pltpu.roll(tile, shift, 1) if shift else tile)
            merged[m, k] = jnp.where(lane < GROUP, lines[0], jnp.where(lane < 2 * GROUP, lines[1], lines[2]))
        return carry

    lax.fori_loop(0, 3, body, 0)

    def widen(m, carry):
        for k in range(FINE.nk + 1):
            q = merged[m, k]
            out = jnp.where(inner < MZ, pltpu.roll(q, LANES - 1, 1), q)
            out = jnp.where(inner > 19, pltpu.roll(q, 4, 1), out)
            packed[m, k, 0:40, :] = jnp.where(inner > 37, pltpu.roll(q, 5, 1), out)
            packed[m, k, 40:48, :] = jnp.ones((8, LANES), F32)
        return carry

    lax.fori_loop(0, 3, widen, 0)


def pack_twin(ext, matrix, pairs, small, packed):
    lane = lane_iota(24)
    chunk = groups(lane)
    half = jnp.zeros_like(lane)
    for s in range(1, 7):
        half = half + (lane >= 20 * s).astype(jnp.int32)
    weights = matrix[...]

    def body(m, carry):
        for t in range(18):
            first = ext[m, t, pl.ds(0, 24, stride=2), :]
            second = ext[m, t, pl.ds(1, 24, stride=2), :]
            pairs[t * 24:(t + 1) * 24, :] = first + second
        value = pairs[...]
        high = value.astype(jnp.bfloat16)
        rest = value - high.astype(F32)
        mid = rest.astype(jnp.bfloat16)
        low = (rest - mid.astype(F32)).astype(jnp.bfloat16)
        small[...] = (
            jnp.dot(high, weights, preferred_element_type=F32)
            + jnp.dot(mid, weights, preferred_element_type=F32)
            + jnp.dot(low, weights, preferred_element_type=F32)
        )
        for k in range(TWIN.nk + 1):
            out = jnp.ones((24, LANES), F32)
            for c in range(3):
                y = min(TWIN.nk * c + k, TWIN.nx - 1)
                for col in range(2):
                    base = (col * 8 + y // 2) * 24
                    line = small[base:base + 24, :]
                    shift = (c * GROUP + col * 20 - (y % 2) * 20) % LANES
                    line = pltpu.roll(line, shift, 1) if shift else line
                    out = jnp.where(half == 2 * c + col, line, out)
            packed[m, k, 0:24, :] = out
            packed[m, k, 24:32, :] = jnp.ones((8, LANES), F32)
        return carry

    lax.fori_loop(0, 3, body, 0)


def face_arrays(level, packed, wt, ym, turned):
    nk, nx, nxr = level.nk, level.nx, level.nxr
    lane = lane_iota(nxr)
    chunk, seg, z = split_lane(level, lane)
    row = lax.broadcasted_iota(jnp.int32, (nxr, LANES), 0)
    ml, mz = level.margin, level.margin_depth
    inside_xz = (row > 0) & (row < nx - 1) & (z > 0) & (z < level.zw - 1) & (chunk < 3)
    el_x = (row >= ml) & (row < ml + level.edge)
    el_z = (z >= mz) & (z < mz + level.edge_depth) & (chunk < 3)
    el_xf = (row >= ml) & (row < ml + level.edge - 1)
    el_zf = (z >= mz) & (z < mz + level.edge_depth - 1) & (chunk < 3)
    first_edge = seg == 0
    if level.nseg == 4:
        first_edge = first_edge | (seg == 2)
    first_edge = first_edge & (z == 0)
    last_edge = jnp.logical_not((seg == 0) | (seg == 2)) & (z == level.zw - 2)

    el_zb = (z > mz) & (z < mz + level.edge_depth) & (chunk < 3)
    below_first = (z == 1) & ((seg == 0) | (seg == 2))
    below_last = (z == level.zw - 1) & jnp.logical_not((seg == 0) | (seg == 2))
    for k in range(nk):
        kz = packed[2, k, 0:nxr, :]
        turned[0, k] = pltpu.roll(kz, LANES - 1, 1)
        turned[1, k] = pltpu.roll(kz, 1, 1)

    def body(k, carry):
        y = chunk * nk + k
        inside = inside_xz & (y > 0) & (y < nx - 1)
        el_y = (y >= ml) & (y < ml + level.edge)
        el_yf = (y >= ml) & (y < ml + level.edge - 1)
        tx = harmonic(packed[0, k, 0:nxr, :], packed[0, k, 1:nxr + 1, :], level.spacing)
        ty = harmonic(packed[1, k, 0:nxr, :], packed[1, k + 1, 0:nxr, :], level.spacing)
        kz = packed[2, k, 0:nxr, :]
        kz_after, kz_before, kz_here = turned[0, k], turned[1, k], kz
        if level is FINE:
            kz_here = jnp.where(first_edge, kz_after, kz)
            kz_after = jnp.where(last_edge, kz, kz_after)
            kz_before = jnp.where(below_first, kz, kz_before)
            kz = jnp.where(below_last, kz_before, kz)
        tz = harmonic(kz_here, kz_after, level.spacing)
        tz_below = harmonic(kz_before, kz, level.spacing)
        wt[0, k] = tx
        wt[1, k] = ty
        wt[2, k] = tz
        wt[3, k] = tz_below
        wt[4, k] = jnp.where(inside, tx - pltpu.roll(tx, 1, 0), 0.0)
        wt[6, k] = jnp.where(inside, tz - tz_below, 0.0)
        wt[7, k] = jnp.where(el_xf & el_y & el_z, tx, 0.0)
        wt[8, k] = jnp.where(el_x & el_yf & el_z, ty, 0.0)
        wt[9, k] = jnp.where(el_x & el_y & el_zf, tz, 0.0)
        wt[10, k] = jnp.where(el_x & el_y & el_zb, tz_below, 0.0)
        return carry

    lax.fori_loop(0, nk, body, 0)
    ym[0] = pltpu.roll(wt[1, nk - 1], GROUP, 1)
    ym[1] = pltpu.roll(wt[8, nk - 1], GROUP, 1)

    def inside_at(k):
        y = chunk * nk + k
        return inside_xz & (y > 0) & (y < nx - 1)

    wt[5, 0] = jnp.where(inside_at(0), wt[1, 0] - ym[0], 0.0)

    def second(k, carry):
        wt[5, k] = jnp.where(inside_at(k), wt[1, k] - wt[1, k - 1], 0.0)
        return carry

    lax.fori_loop(1, nk, second, 0)


def basis_solve(level, wt, ym, cst, r0, r1, r2, w, above, below, beside, phi, planes):
    nk, nx = level.nk, level.nx
    lane = lane_iota(8)
    chunk, seg, z = split_lane(level, lane)
    sub = lax.broadcasted_iota(jnp.int32, (8, LANES), 0)
    ax, ay, az = sub >= 4, ((sub >> 1) & 1) == 1, (sub & 1) == 1

    def ramp(flag, place, length):
        return jnp.where(flag, place / length, 1.0 - place / length)

    fz = ramp(az, z.astype(F32) - level.margin_depth + 0.5, level.edge_depth)
    sx = jnp.where(ax, 1.0 / level.edge, -1.0 / level.edge)
    sy = jnp.where(ay, 1.0 / level.edge, -1.0 / level.edge)
    sz = jnp.where(az, 1.0 / level.edge_depth, -1.0 / level.edge_depth)
    cst[4, 0] = sy * fz
    cst[4, 1] = sx
    for k in range(nk):
        fy = ramp(ay, (chunk * nk + k).astype(F32) - level.margin + 0.5, level.edge)
        cst[0, k] = sx * fy * fz
        cst[1, k] = sz * fy
        cst[2, k] = fy * fz

    cst[4, 2] = jnp.where(ax, (0.5 - level.margin) / level.edge, 1.0 - (0.5 - level.margin) / level.edge)

    def fx_at(x):
        return cst[4, 2] + cst[4, 1] * x.astype(F32)

    def mask_at(k):
        y = chunk * nk + k
        return (y > 0) & (y < nx - 1) & (z > 0) & (z < level.zw - 1) & (chunk < 3)

    cst[4, 3] = jnp.zeros((8, LANES), F32)
    zero = cst[4, 3]

    def row(n, k, x):
        return wt[n, k, pl.ds(x, 8, stride=0), :]

    def pipeline(base, low, high, depth, produce, keep, keep_w, consume, state):
        def apply(x0, after, fx_prev, state):
            ahead = [keep[x0, k] for k in range(nk)]
            for p in range(depth):
                x = x0 + p
                u = ahead
                ahead = after if p == depth - 1 else [keep[x + 1, k] for k in range(nk)]
                fy_prev = ym[base // 7, pl.ds(x, 8, stride=0), :] * (beside[x, 1] - u[0])
                image, fx_new = [], []
                for k in range(nk):
                    flux = row(base, k, x) * (u[k] - ahead[k])
                    fx_new.append(flux)
                    out = flux - fx_prev[k]
                    side = u[k + 1] if k < nk - 1 else beside[x, 0]
                    fy = row(base + 1, k, x) * (u[k] - side)
                    out = out + (fy - fy_prev)
                    fy_prev = fy
                    out = out + row(base + 2, k, x) * (u[k] - above[x, k])
                    image.append(out + row(base + 3, k, x) * (u[k] - below[x, k]))
                fx_prev = fx_new
                if keep_w is not None:
                    for k in range(nk):
                        keep_w[x, k] = image[k]
                for k in range(nk):
                    state = consume(state, u[k], image[k])
            return fx_prev, state

        def store(x0, block):
            for p in range(depth):
                u = block[p]
                for k in range(nk):
                    keep[x0 + p, k] = u[k]
                    above[x0 + p, k] = pltpu.roll(u[k], LANES - 1, 1)
                    below[x0 + p, k] = pltpu.roll(u[k], 1, 1)
                beside[x0 + p, 0] = pltpu.roll(u[0], LANES - GROUP, 1)
                beside[x0 + p, 1] = pltpu.roll(u[nk - 1], GROUP, 1)

        def make(x0):
            return [produce(x0 + p) for p in range(depth)]

        start = jnp.int32(low)
        block = make(start)
        fx_prev = [zero] * nk
        store(start, block)

        def body(n, carry):
            fx_prev, state = carry
            x0 = low + n * depth
            block = make(x0)
            fx_prev, state = apply(x0 - depth, block[0], fx_prev, state)
            store(x0, block)
            return fx_prev, state

        count = (high - low) // depth
        fx_prev, state = lax.fori_loop(1, count, body, (fx_prev, state))
        _, state = apply(jnp.int32(high - depth), [zero] * nk, fx_prev, state)
        return state

    def norms(state, u, image):
        return state[0] + u * u, state[1] + u * image

    def sweep(produce, keep, keep_w):
        state = pipeline(0, 0, nx, planes[0], produce, keep, keep_w, norms, (zero, zero))
        if keep_w is not None:
            for k in range(nk):
                keep_w[0, k] = zero
                keep_w[nx - 1, k] = zero
        return by_segment(state[0]), by_segment(state[1])

    def by_segment(acc):
        out = jnp.sum(jnp.where(seg == 0, acc, 0.0), axis=1, keepdims=True)
        for s in range(1, level.nseg):
            total = jnp.sum(jnp.where(seg == s, acc, 0.0), axis=1, keepdims=True)
            out = jnp.where(seg == s, total, out)
        return out

    def first(x):
        fx = fx_at(x)
        return [
            row(4, k, x) * cst[0, k] + fx * (row(5, k, x) * cst[4, 0] + row(6, k, x) * cst[1, k])
            for k in range(nk)
        ]

    rr0, rw0 = sweep(first, r0, w)
    alpha0 = rr0 / rw0
    for k in range(nk):
        cst[3, k] = jnp.where(mask_at(k), alpha0, 0.0)
    rr1, rw1 = sweep(lambda x: [r0[x, k] - cst[3, k] * w[x, k] for k in range(nk)], r1, w)
    beta0 = rr1 / rr0
    alpha1 = rr1 / (rw1 - beta0 / alpha0 * rr1)
    gamma = alpha1 * beta0 / alpha0
    for k in range(nk):
        cst[3, k] = jnp.where(mask_at(k), alpha1, 0.0)

    def third(x):
        return [
            r1[x, k] + gamma * (r1[x, k] - r0[x, k]) - cst[3, k] * w[x, k] for k in range(nk)
        ]

    rr2, rw2 = sweep(third, r2, None)
    beta1 = rr2 / rr1
    alpha2 = rr2 / (rw2 - beta1 / alpha1 * rr2)
    c2 = alpha2
    c1 = alpha1 + alpha2 * beta1
    c0 = alpha0 + c1 * beta0
    low = level.margin

    def basis(x):
        fx = fx_at(x)
        return [
            fx * cst[2, k] + (c0 * r0[x, k] + (c1 * r1[x, k] + c2 * r2[x, k])) for k in range(nk)
        ]

    def diagonals(state, u, image):
        return tuple(
            state[s] + u * (pltpu.roll(image, 8 - s, 0) if s else image) for s in range(5)
        )

    acc = pipeline(7, low, low + level.edge, planes[1], basis, phi, None, diagonals, (zero,) * 5)
    return acc, seg


def stencil(level, acc, seg, masks, elements):
    out = jnp.zeros((8, LANES), F32)
    for e, s in enumerate(elements):
        for n in range(5):
            total = jnp.sum(jnp.where(seg == s, acc[n], 0.0), axis=1, keepdims=True)
            out = out + total * masks[e * 5 + n]
    return out


class Shifted:
    def __init__(self, ref, first, column=None):
        self.ref = ref
        self.first = first
        self.column = column

    def place(self, index):
        x, k = index
        return (x - self.first, k) if self.column is None else (self.column, x - self.first, k)

    def __getitem__(self, index):
        return self.ref[self.place(index)]

    def __setitem__(self, index, value):
        self.ref[self.place(index)] = value


def local_work(own, hx, hy, hc, matrix, masks, phi_f, phi_t, line, ext, pairs, small, merged, *scratch):
    pk_f, wt_f, ym_f, turned_f, cst_f, *fields_f = scratch[:12]
    pk_t, wt_t, ym_t, turned_t, cst_t, *fields_t = scratch[12:]
    assemble(own, hx, hy, hc, ext)
    pack_twin(ext, matrix, pairs, small, pk_t)
    face_arrays(TWIN, pk_t, wt_t, ym_t, turned_t)
    acc, seg = basis_solve(TWIN, wt_t, ym_t, cst_t, *fields_t, Shifted(phi_t, TWIN.margin), TWIN_PLANES)
    parts = [stencil(TWIN, acc, seg, masks, (2 * col, 2 * col + 1)) for col in range(2)]
    total = pltpu.roll(parts[0], 32, 1) + pltpu.roll(parts[1], 48, 1)

    def body(col, total):
        pack_fine(ext, pk_f, merged, col)
        face_arrays(FINE, pk_f, wt_f, ym_f, turned_f)
        phi = Shifted(phi_f, FINE.margin, col)
        acc, seg = basis_solve(FINE, wt_f, ym_f, cst_f, *fields_f, phi, FINE_PLANES)
        part = stencil(FINE, acc, seg, masks, (0, 1))
        here = jnp.full((8, LANES), col, jnp.int32) == 0
        return total + jnp.where(here, part, pltpu.roll(part, 16, 1))

    total = lax.fori_loop(0, 2, body, total)
    line[...] = jnp.broadcast_to(jnp.sum(total, axis=0, keepdims=True), (8, LANES))


def local_scratch():
    def scratch(level):
        field = pltpu.VMEM((level.nx, level.nk, 8, LANES), F32)
        return [
            pltpu.VMEM((3, level.nk + 1, level.nxr + 8, LANES), F32),
            pltpu.VMEM((11, level.nk, level.nxr, LANES), F32),
            pltpu.VMEM((2, level.nxr, LANES), F32),
            pltpu.VMEM((2, level.nk, level.nxr, LANES), F32),
            pltpu.VMEM((5, level.nk, 8, LANES), F32),
        ] + [field] * 6 + [pltpu.VMEM((level.nx, 2, 8, LANES), F32)]

    return [
        pltpu.VMEM((3, 18, 48, LANES), F32),
        pltpu.VMEM((18 * 24, LANES), F32),
        pltpu.VMEM((18 * 24, LANES), F32),
        pltpu.VMEM((3, FINE.nk + 1, GROUP, LANES), F32),
    ] + scratch(FINE) + scratch(TWIN)


def coarse_solve(quantity, lane):
    second = (lane & 63) >= 32
    place = lane & 31

    def next_q(x):
        same = pltpu.roll(x, LANES - 32, 1)
        inner = pltpu.roll(x, 31, 1)
        outer = pltpu.roll(x, 63, 1)
        return jnp.where(second, jnp.where(place < 31, inner, outer), same)

    def prev_q(x):
        same = pltpu.roll(x, 32, 1)
        inner = pltpu.roll(x, LANES - 31, 1)
        outer = pltpu.roll(x, LANES - 63, 1)
        return jnp.where(second, same, jnp.where(place > 0, inner, outer))

    def next_p(x):
        return pltpu.roll(x, 7, 0)

    def prev_p(x):
        return pltpu.roll(x, 1, 0)

    entry = {}
    n = 0
    for a in range(4):
        for b in range(a, 4):
            entry[a, b] = entry[b, a] = quantity(n)
            n += 1

    def corners(x):
        side = next_q(x)
        return [x, side, next_p(x), next_p(side)]

    def gather(parts):
        side = prev_q(parts[1] + prev_p(parts[3]))
        return parts[0] + side + prev_p(parts[2])

    def operate(x):
        values = corners(x)
        parts = []
        for a in range(4):
            terms = [entry[a, b] * values[b] for b in range(4)]
            parts.append((terms[0] + terms[1]) + (terms[2] + terms[3]))
        return gather(parts)

    upper = lane >= 64

    def total(x):
        column = jnp.sum(x, axis=0, keepdims=True)
        lo = jnp.sum(jnp.where(upper[:1], 0.0, column), axis=1, keepdims=True)
        hi = jnp.sum(jnp.where(upper[:1], column, 0.0), axis=1, keepdims=True)
        return jnp.where(upper, hi, lo)

    residual = -gather([quantity(10 + a) for a in range(4)])
    norm = total(residual * residual)
    image = operate(residual)
    alpha = norm / total(residual * image)
    update = alpha * residual
    after = residual - alpha * image
    norm_next = total(after * after)
    direction = after + norm_next / norm * residual
    image = operate(direction)
    alpha = norm_next / total(direction * image)
    update = update + alpha * direction
    return [value for value in corners(update)]


def greet_groups():
    i = lax.axis_index("gx")
    j = lax.axis_index("gy")
    ni = lax.axis_size("gx")
    nj = lax.axis_size("gy")
    barrier = pltpu.get_barrier_semaphore()

    def greet_y(d, carry):
        pl.semaphore_signal(barrier, inc=1, device_id=(i, lax.rem(j + d, nj)), device_id_type=MESH)
        return carry

    def greet_x(d, carry):
        pl.semaphore_signal(barrier, inc=1, device_id=(lax.rem(i + d, ni), j), device_id_type=MESH)
        return carry

    lax.fori_loop(1, nj, greet_y, 0)
    lax.fori_loop(1, ni, greet_x, 0)


def coarse_work(line, rows, block, grid, send1, recv1, send2, recv2):
    i = lax.axis_index("gx")
    j = lax.axis_index("gy")
    ni = lax.axis_size("gx")
    nj = lax.axis_size("gy")
    pl.semaphore_wait(pltpu.get_barrier_semaphore(), ni + nj - 2)

    def copy_y(d):
        return pltpu.make_async_remote_copy(
            src_ref=line, dst_ref=rows.at[j], send_sem=send1.at[d], recv_sem=recv1.at[d],
            device_id=(i, lax.rem(j + d, nj)), device_id_type=MESH,
        )

    def copy_x(d):
        return pltpu.make_async_remote_copy(
            src_ref=block, dst_ref=grid.at[i], send_sem=send2.at[d], recv_sem=recv2.at[d],
            device_id=(lax.rem(i + d, ni), j), device_id_type=MESH,
        )

    def start_y(d, carry):
        copy_y(d).start()
        return carry

    def wait_y(d, carry):
        copy_y(d).wait()
        return carry

    def start_x(d, carry):
        copy_x(d).start()
        return carry

    def wait_x(d, carry):
        copy_x(d).wait()
        return carry

    lax.fori_loop(1, nj, start_y, 0)
    rows[j] = line[...]
    lax.fori_loop(1, nj, wait_y, 0)
    quarter = rows[:, 0, :]
    turned = jnp.transpose(jnp.concatenate([quarter] * 4, axis=0))
    lane16 = lane_iota(16)
    out = turned[48:64]
    for b in range(3):
        out = jnp.where((lane16 >= 32 * b) & (lane16 < 32 * b + 32), turned[16 * b:16 * b + 16], out)
    block[...] = out
    lax.fori_loop(1, ni, start_x, 0)
    grid[i] = out
    lax.fori_loop(1, ni, wait_x, 0)
    return coarse_solve(lambda q: grid[:, q, :], lane_iota(8))


def fold_rows(values, sub):
    low = sub < 4
    step = [
        jnp.where(low, values[n], values[n + 4])
        + pltpu.roll(jnp.where(low, values[n + 4], values[n]), 4, 0)
        for n in range(4)
    ]
    for shift in (2, 1):
        keep = (sub & shift) == 0
        step = [
            jnp.where(
                keep,
                step[n] + pltpu.roll(step[n], 8 - shift, 0),
                step[n + shift] + pltpu.roll(step[n + shift], shift, 0),
            )
            for n in range(shift)
        ]
    return step[0]


def pressure_work(phi_f, phi_t, nodes, fine, twin, rows_f, rows_t):
    i = lax.axis_index("gx")
    j = lax.axis_index("gy")
    sub = lax.broadcasted_iota(jnp.int32, (8, LANES), 0)
    lane = lane_iota(8)
    corner, az = sub >> 1, (sub & 1) == 1

    def own_nodes(level, col):
        here = (sub == i) & (lane == level * 64 + col * 32 + j)
        out = jnp.zeros((8, LANES), F32)
        for a in range(4):
            value = jnp.where(here, nodes[a], 0.0)
            value = jnp.sum(jnp.sum(value, axis=0, keepdims=True), axis=1, keepdims=True)
            out = jnp.where(corner == a, value, out)
        return jnp.where(az, out, 1.0), jnp.where(az, 0.0, out)

    _, seg, _ = split_lane(FINE, lane)
    fine_weights = []
    for col in range(2):
        first, second = own_nodes(0, col)
        fine_weights.append(jnp.where(seg == 0, first, second))
    _, seg, _ = split_lane(TWIN, lane)
    twin_weights = jnp.zeros((8, LANES), F32)
    for col in range(2):
        first, second = own_nodes(1, col)
        twin_weights = jnp.where(seg == 2 * col, first, twin_weights)
        twin_weights = jnp.where(seg == 2 * col + 1, second, twin_weights)

    def fine_rows(k, carry):
        for col in range(2):
            for g in range(EL // 8):
                values = [phi_f[col, 8 * g + n, k] * fine_weights[col] for n in range(8)]
                rows_f[col, k, 8 * g:8 * g + 8, :] = fold_rows(values, sub)
        return carry

    lax.fori_loop(0, FINE.nk, fine_rows, 0)

    def twin_rows(k, carry):
        for g in range(EL // 16):
            values = [phi_t[8 * g + n, k] * twin_weights for n in range(8)]
            rows_t[k, 8 * g:8 * g + 8, :] = fold_rows(values, sub)
        return carry

    lax.fori_loop(0, TWIN.nk, twin_rows, 0)

    def turn(value, shift):
        return pltpu.roll(value, shift % LANES, 1) if shift % LANES else value

    wide = lane_iota(EL)
    for col in range(2):
        for t in range(8):
            out = None
            for h in range(4):
                y = 4 * t + h + MX
                c, k = y // FINE.nk, y % FINE.nk
                for e in range(2):
                    to = h * 32 + e * 16
                    piece = turn(rows_f[col, k], to - (c * GROUP + e * 20 + MZ))
                    out = piece if out is None else jnp.where(wide >= to, piece, out)
            fine[:, (col * 8 + t) * LANES:(col * 8 + t + 1) * LANES] = out
    wide = lane_iota(EL // 2)
    for t in range(4):
        out = None
        for h in range(8):
            col, y = (8 * t + h) // 16, (8 * t + h) % 16 + MX // 2
            c, k = y // TWIN.nk, y % TWIN.nk
            for e in range(2):
                to = h * 16 + e * 8
                piece = turn(rows_t[k], to - (c * GROUP + col * 20 + e * 10 + MZ // 2))
                out = piece if out is None else jnp.where(wide >= to, piece, out)
        twin[:, t * LANES:(t + 1) * LANES] = out


def solve_kernel(own, hx, hy, hc, matrix, masks, fine, twin, phi_f, phi_t, rows_f, rows_t, line, *scratch):
    exchange, local = scratch[:7], scratch[7:]
    greet_groups()
    local_work(own, hx, hy, hc, matrix, masks, phi_f, phi_t, line, *local)
    nodes = coarse_work(line, *exchange)
    pressure_work(phi_f, phi_t, nodes, fine, twin, rows_f, rows_t)


def solve(perm, hx, hy, hc, ni, nj):
    vmem = pl.BlockSpec(memory_space=pltpu.VMEM)
    return pl.pallas_call(
        solve_kernel,
        out_shape=(
            jax.ShapeDtypeStruct((EL, 2048), F32),
            jax.ShapeDtypeStruct((EL // 2, 512), F32),
        ),
        in_specs=[vmem] * 6,
        out_specs=(vmem, vmem),
        scratch_shapes=[
            pltpu.VMEM((2, EL, FINE.nk, 8, LANES), F32),
            pltpu.VMEM((EL // 2, TWIN.nk, 8, LANES), F32),
            pltpu.VMEM((2, FINE.nk, EL, LANES), F32),
            pltpu.VMEM((TWIN.nk, EL // 2, LANES), F32),
            pltpu.VMEM((8, LANES), F32),
            pltpu.VMEM((nj, 8, LANES), F32),
            pltpu.VMEM((16, LANES), F32),
            pltpu.VMEM((ni, 16, LANES), F32),
            pltpu.SemaphoreType.DMA((nj,)),
            pltpu.SemaphoreType.DMA((nj,)),
            pltpu.SemaphoreType.DMA((ni,)),
            pltpu.SemaphoreType.DMA((ni,)),
        ] + local_scratch(),
        compiler_params=pltpu.CompilerParams(
            collective_id=1, has_side_effects=True, vmem_limit_bytes=VLIMIT
        ),
    )(
        perm, hx, hy, hc,
        jnp.asarray(coarsen_matrix(), jnp.bfloat16), jnp.asarray(stencil_masks()),
    )


def solution(mesh):
    ni, nj = mesh.shape["gx"], mesh.shape["gy"]

    def shards(perm):
        hx, hy, hc = halo(perm)
        return solve(perm, hx, hy, hc, ni, nj)

    return jax.shard_map(
        shards,
        mesh=mesh,
        in_specs=(P(None, "gx", "gy"),),
        out_specs=(P("gx", "gy"), P("gx", "gy")),
        check_vma=False,
    )
```

```python
import functools

import jax
import jax.numpy as jnp
import numpy as np
from jax import lax
from jax.experimental import pallas as pl
from jax.experimental.pallas import tpu as pltpu
from jax.sharding import PartitionSpec as P

EL = 32
ELZ = 16
MX = 4
MZ = 2
LANES = 128
GROUP = 40
MESH = pl.DeviceIdType.MESH
F32 = jnp.float32
VLIMIT = 60 * 1024 * 1024
FINE_PLANES = (4, 4)
TWIN_PLANES = (5, 8)


class Level:
    def __init__(self, nk, nx, zw, edge, edge_depth, margin, margin_depth, spacing):
        self.nk = nk
        self.nx = nx
        self.nxr = -(-nx // 8) * 8
        self.zw = zw
        self.nseg = GROUP // zw
        self.edge = edge
        self.edge_depth = edge_depth
        self.margin = margin
        self.margin_depth = margin_depth
        self.spacing = spacing


FINE = Level(13, 40, 20, EL, ELZ, MX, MZ, 1.0)
TWIN = Level(7, 20, 10, EL // 2, ELZ // 2, MX // 2, MZ // 2, 2.0)


def stencil_masks():
    masks = np.zeros((10, 8, LANES), np.float32)

    def put(e, a, b, q):
        s = (b - a) % 8
        if s > 4:
            a, s = b, 8 - s
        masks[e * 5 + s, a, q] += 1.0

    q = 0
    for a in range(4):
        for b in range(a, 4):
            put(0, 2 * a + 1, 2 * b + 1, q)
            put(1, 2 * a, 2 * b, q)
            q += 1
    for a in range(4):
        for b in range(4):
            put(0, 2 * a + 1, 2 * b, q)
        q += 1
    return masks


def coarsen_matrix():
    matrix = np.zeros((LANES, LANES), np.float32)
    for h in range(4):
        for e in range(2):
            for zz in range(10):
                for part in range(2):
                    z = min(max(e * ELZ - MZ + 2 * zz + part, 0), 31)
                    matrix[h * 32 + z, (h // 2) * 20 + e * 10 + zz] += 0.125
    return matrix


def lane_iota(rows):
    return lax.broadcasted_iota(jnp.int32, (rows, LANES), 1)


def groups(lane):
    return (lane >= 40).astype(jnp.int32) + (lane >= 80).astype(jnp.int32) + (lane >= 120).astype(jnp.int32)


def split_lane(level, lane):
    chunk = groups(lane)
    inner = lane - GROUP * chunk
    seg = jnp.zeros_like(lane)
    for s in range(1, level.nseg):
        seg = seg + (inner >= s * level.zw).astype(jnp.int32)
    return chunk, seg, inner - level.zw * seg


def harmonic(first, second, spacing):
    return spacing * 2.0 * first * second / (first + second)


def halo_kernel(perm, hx, hy, hc, send, recv):
    i = lax.axis_index("gx")
    j = lax.axis_index("gy")
    ni = lax.axis_size("gx")
    nj = lax.axis_size("gy")
    up, down = lax.rem(i + 1, ni), lax.rem(i + ni - 1, ni)
    right, left = lax.rem(j + 1, nj), lax.rem(j + nj - 1, nj)
    width = perm.shape[2]
    west, east = perm.at[:, pl.ds(0, MX)], perm.at[:, pl.ds(perm.shape[1] - MX, MX)]
    low, high = pl.ds(0, LANES), pl.ds(width - LANES, LANES)
    plans = [
        (east, hx.at[0], (up, j)),
        (west, hx.at[1], (down, j)),
        (perm.at[:, :, high], hy.at[0], (i, right)),
        (perm.at[:, :, low], hy.at[1], (i, left)),
        (east.at[:, :, high], hc.at[0], (up, right)),
        (east.at[:, :, low], hc.at[1], (up, left)),
        (west.at[:, :, high], hc.at[2], (down, right)),
        (west.at[:, :, low], hc.at[3], (down, left)),
    ]
    barrier = pltpu.get_barrier_semaphore()
    for _, _, target in plans:
        pl.semaphore_signal(barrier, inc=1, device_id=target, device_id_type=MESH)
    pl.semaphore_wait(barrier, 8)
    copies = []
    for n, (src, dst, target) in enumerate(plans):
        copy = pltpu.make_async_remote_copy(
            src_ref=src, dst_ref=dst, send_sem=send.at[n], recv_sem=recv.at[n],
            device_id=target, device_id_type=MESH,
        )
        copy.start()
        copies.append(copy)
    for copy in copies:
        copy.wait()


def halo(perm):
    rows, width = perm.shape[1], perm.shape[2]
    anywhere = pl.BlockSpec(memory_space=pl.ANY)
    return pl.pallas_call(
        halo_kernel,
        out_shape=(
            jax.ShapeDtypeStruct((2, 3, MX, width), F32),
            jax.ShapeDtypeStruct((2, 3, rows, LANES), F32),
            jax.ShapeDtypeStruct((4, 3, MX, LANES), F32),
        ),
        in_specs=[anywhere],
        out_specs=(anywhere,) * 3,
        scratch_shapes=[pltpu.SemaphoreType.DMA((8,)), pltpu.SemaphoreType.DMA((8,))],
        compiler_params=pltpu.CompilerParams(collective_id=0, has_side_effects=True),
    )(perm)


def assemble(own, hx, hy, hc, ext):
    rows = own.shape[1]

    def body(m, carry):
        for t in range(18):
            if t == 0:
                top, mid, low = hc[0, m], hy[0, m], hc[2, m]
            elif t == 17:
                top, mid, low = hc[1, m], hy[1, m], hc[3, m]
            else:
                lanes = pl.ds((t - 1) * LANES, LANES)
                top, mid, low = hx[0, m, :, lanes], own[m, :, lanes], hx[1, m, :, lanes]
            ext[m, t, 0:MX, :] = top
            ext[m, t, MX:MX + rows, :] = mid
            ext[m, t, MX + rows:2 * MX + rows, :] = low
            ext[m, t, 2 * MX + rows:, :] = jnp.ones((8, LANES), F32)
        return carry

    lax.fori_loop(0, 3, body, 0)


def pack_fine(ext, packed, merged, column):
    lane = lane_iota(GROUP)
    chunk, _, _ = split_lane(FINE, lane)
    inner = lane - GROUP * chunk

    def body(m, carry):
        for k in range(FINE.nk + 1):
            lines = []
            for c in range(3):
                y = FINE.nk * c + k
                tile = ext[m, column * 8 + y // 4, 0:40, :]
                shift = (c * GROUP + MZ - (y % 4) * 32) % LANES
                lines.append(pltpu.roll(tile, shift, 1) if shift else tile)
            merged[m, k] = jnp.where(lane < GROUP, lines[0], jnp.where(lane < 2 * GROUP, lines[1], lines[2]))
        return carry

    lax.fori_loop(0, 3, body, 0)

    def widen(m, carry):
        for k in range(FINE.nk + 1):
            q = merged[m, k]
            out = jnp.where(inner < MZ, pltpu.roll(q, LANES - 1, 1), q)
            out = jnp.where(inner > 19, pltpu.roll(q, 4, 1), out)
            packed[m, k, 0:40, :] = jnp.where(inner > 37, pltpu.roll(q, 5, 1), out)
            packed[m, k, 40:48, :] = jnp.ones((8, LANES), F32)
        return carry

    lax.fori_loop(0, 3, widen, 0)


def pack_twin(ext, matrix, pairs, small, packed):
    lane = lane_iota(24)
    chunk = groups(lane)
    half = jnp.zeros_like(lane)
    for s in range(1, 7):
        half = half + (lane >= 20 * s).astype(jnp.int32)
    weights = matrix[...]

    def body(m, carry):
        for t in range(18):
            first = ext[m, t, pl.ds(0, 24, stride=2), :]
            second = ext[m, t, pl.ds(1, 24, stride=2), :]
            pairs[t * 24:(t + 1) * 24, :] = first + second
        value = pairs[...]
        high = value.astype(jnp.bfloat16)
        rest = value - high.astype(F32)
        mid = rest.astype(jnp.bfloat16)
        low = (rest - mid.astype(F32)).astype(jnp.bfloat16)
        small[...] = (
            jnp.dot(high, weights, preferred_element_type=F32)
            + jnp.dot(mid, weights, preferred_element_type=F32)
            + jnp.dot(low, weights, preferred_element_type=F32)
        )
        for k in range(TWIN.nk + 1):
            out = jnp.ones((24, LANES), F32)
            for c in range(3):
                y = min(TWIN.nk * c + k, TWIN.nx - 1)
                for col in range(2):
                    base = (col * 8 + y // 2) * 24
                    line = small[base:base + 24, :]
                    shift = (c * GROUP + col * 20 - (y % 2) * 20) % LANES
                    line = pltpu.roll(line, shift, 1) if shift else line
                    out = jnp.where(half == 2 * c + col, line, out)
            packed[m, k, 0:24, :] = out
            packed[m, k, 24:32, :] = jnp.ones((8, LANES), F32)
        return carry

    lax.fori_loop(0, 3, body, 0)


def face_arrays(level, packed, wt, ym, turned):
    nk, nx, nxr = level.nk, level.nx, level.nxr
    lane = lane_iota(nxr)
    chunk, seg, z = split_lane(level, lane)
    row = lax.broadcasted_iota(jnp.int32, (nxr, LANES), 0)
    ml, mz = level.margin, level.margin_depth
    inside_xz = (row > 0) & (row < nx - 1) & (z > 0) & (z < level.zw - 1) & (chunk < 3)
    el_x = (row >= ml) & (row < ml + level.edge)
    el_z = (z >= mz) & (z < mz + level.edge_depth) & (chunk < 3)
    el_xf = (row >= ml) & (row < ml + level.edge - 1)
    el_zf = (z >= mz) & (z < mz + level.edge_depth - 1) & (chunk < 3)
    first_edge = seg == 0
    if level.nseg == 4:
        first_edge = first_edge | (seg == 2)
    first_edge = first_edge & (z == 0)
    last_edge = jnp.logical_not((seg == 0) | (seg == 2)) & (z == level.zw - 2)

    el_zb = (z > mz) & (z < mz + level.edge_depth) & (chunk < 3)
    below_first = (z == 1) & ((seg == 0) | (seg == 2))
    below_last = (z == level.zw - 1) & jnp.logical_not((seg == 0) | (seg == 2))
    for k in range(nk):
        kz = packed[2, k, 0:nxr, :]
        turned[0, k] = pltpu.roll(kz, LANES - 1, 1)
        turned[1, k] = pltpu.roll(kz, 1, 1)

    def body(k, carry):
        y = chunk * nk + k
        inside = inside_xz & (y > 0) & (y < nx - 1)
        el_y = (y >= ml) & (y < ml + level.edge)
        el_yf = (y >= ml) & (y < ml + level.edge - 1)
        tx = harmonic(packed[0, k, 0:nxr, :], packed[0, k, 1:nxr + 1, :], level.spacing)
        ty = harmonic(packed[1, k, 0:nxr, :], packed[1, k + 1, 0:nxr, :], level.spacing)
        kz = packed[2, k, 0:nxr, :]
        kz_after, kz_before, kz_here = turned[0, k], turned[1, k], kz
        if level is FINE:
            kz_here = jnp.where(first_edge, kz_after, kz)
            kz_after = jnp.where(last_edge, kz, kz_after)
            kz_before = jnp.where(below_first, kz, kz_before)
            kz = jnp.where(below_last, kz_before, kz)
        tz = harmonic(kz_here, kz_after, level.spacing)
        tz_below = harmonic(kz_before, kz, level.spacing)
        wt[0, k] = tx
        wt[1, k] = ty
        wt[2, k] = tz
        wt[3, k] = tz_below
        wt[4, k] = jnp.where(inside, tx - pltpu.roll(tx, 1, 0), 0.0)
        wt[6, k] = jnp.where(inside, tz - tz_below, 0.0)
        wt[7, k] = jnp.where(el_xf & el_y & el_z, tx, 0.0)
        wt[8, k] = jnp.where(el_x & el_yf & el_z, ty, 0.0)
        wt[9, k] = jnp.where(el_x & el_y & el_zf, tz, 0.0)
        wt[10, k] = jnp.where(el_x & el_y & el_zb, tz_below, 0.0)
        return carry

    lax.fori_loop(0, nk, body, 0)
    ym[0] = pltpu.roll(wt[1, nk - 1], GROUP, 1)
    ym[1] = pltpu.roll(wt[8, nk - 1], GROUP, 1)

    def inside_at(k):
        y = chunk * nk + k
        return inside_xz & (y > 0) & (y < nx - 1)

    wt[5, 0] = jnp.where(inside_at(0), wt[1, 0] - ym[0], 0.0)

    def second(k, carry):
        wt[5, k] = jnp.where(inside_at(k), wt[1, k] - wt[1, k - 1], 0.0)
        return carry

    lax.fori_loop(1, nk, second, 0)


def basis_solve(level, wt, ym, cst, r0, r1, r2, w, w2, *rest):
    *rings, phi, planes = rest
    rings = rings[:4], rings[4:]
    nk, nx = level.nk, level.nx
    lane = lane_iota(8)
    chunk, seg, z = split_lane(level, lane)
    sub = lax.broadcasted_iota(jnp.int32, (8, LANES), 0)
    ax, ay, az = sub >= 4, ((sub >> 1) & 1) == 1, (sub & 1) == 1

    def ramp(flag, place, length):
        return jnp.where(flag, place / length, 1.0 - place / length)

    fz = ramp(az, z.astype(F32) - level.margin_depth + 0.5, level.edge_depth)
    sx = jnp.where(ax, 1.0 / level.edge, -1.0 / level.edge)
    sy = jnp.where(ay, 1.0 / level.edge, -1.0 / level.edge)
    sz = jnp.where(az, 1.0 / level.edge_depth, -1.0 / level.edge_depth)
    cst[4, 0] = sy * fz
    cst[4, 1] = sx
    for k in range(nk):
        fy = ramp(ay, (chunk * nk + k).astype(F32) - level.margin + 0.5, level.edge)
        cst[0, k] = sx * fy * fz
        cst[1, k] = sz * fy
        cst[2, k] = fy * fz

    cst[4, 2] = jnp.where(ax, (0.5 - level.margin) / level.edge, 1.0 - (0.5 - level.margin) / level.edge)

    def fx_at(x):
        return cst[4, 2] + cst[4, 1] * x.astype(F32)

    def mask_at(k):
        y = chunk * nk + k
        return (y > 0) & (y < nx - 1) & (z > 0) & (z < level.zw - 1) & (chunk < 3)

    cst[4, 3] = jnp.zeros((8, LANES), F32)
    zero = cst[4, 3]

    def row(n, k, x):
        return wt[n, k, pl.ds(x, 8, stride=0), :]

    def pipeline(base, low, high, depth, produce, keep, keep_w, consume, state):
        def apply(ring, x0, after, fx_prev, state):
            u_ring, above, below, beside = ring
            ahead = [u_ring[0, k] for k in range(nk)]
            for p in range(depth):
                x = x0 + p
                u = ahead
                ahead = after if p == depth - 1 else [u_ring[p + 1, k] for k in range(nk)]
                fy_prev = ym[base // 7, pl.ds(x, 8, stride=0), :] * (beside[p, 1] - u[0])
                image, fx_new = [], []
                for k in range(nk):
                    flux = row(base, k, x) * (u[k] - ahead[k])
                    fx_new.append(flux)
                    out = flux - fx_prev[k]
                    side = u[k + 1] if k < nk - 1 else beside[p, 0]
                    fy = row(base + 1, k, x) * (u[k] - side)
                    out = out + (fy - fy_prev)
                    fy_prev = fy
                    out = out + row(base + 2, k, x) * (u[k] - above[p, k])
                    image.append(out + row(base + 3, k, x) * (u[k] - below[p, k]))
                    if keep_w is not None:
                        keep_w[x, k] = image[k]
                    state = consume(state, u[k], image[k])
                fx_prev = fx_new
            return fx_prev, state

        def make(ring, x0):
            u_ring, above, below, beside = ring
            first = None
            for p in range(depth):
                u = produce(x0 + p)
                first = u if first is None else first
                for k in range(nk):
                    keep[x0 + p, k] = u[k]
                    u_ring[p, k] = u[k]
                    above[p, k] = pltpu.roll(u[k], LANES - 1, 1)
                    below[p, k] = pltpu.roll(u[k], 1, 1)
                beside[p, 0] = pltpu.roll(u[0], LANES - GROUP, 1)
                beside[p, 1] = pltpu.roll(u[nk - 1], GROUP, 1)
            return first

        even, odd = rings
        make(even, jnp.int32(low))

        def body(n, carry):
            fx_prev, state = carry
            x0 = low + n * (2 * depth)
            after = make(odd, x0 + depth)
            fx_prev, state = apply(even, x0, after, fx_prev, state)
            after = make(even, x0 + 2 * depth)
            return apply(odd, x0 + depth, after, fx_prev, state)

        count = (high - low) // (2 * depth)
        fx_prev, state = lax.fori_loop(0, count - 1, body, ([zero] * nk, state))
        x0 = jnp.int32(high - 2 * depth)
        after = make(odd, x0 + depth)
        fx_prev, state = apply(even, x0, after, fx_prev, state)
        _, state = apply(odd, x0 + depth, [zero] * nk, fx_prev, state)
        return state

    def norms(state, u, image):
        return state[0] + u * u, state[1] + u * image

    def sweep(produce, keep, keep_w):
        state = pipeline(0, 0, nx, planes[0], produce, keep, keep_w, norms, (zero, zero))
        if keep_w is not None:
            for k in range(nk):
                keep_w[0, k] = zero
                keep_w[nx - 1, k] = zero
        return by_segment(state[0]), by_segment(state[1])

    def by_segment(acc):
        out = jnp.sum(jnp.where(seg == 0, acc, 0.0), axis=1, keepdims=True)
        for s in range(1, level.nseg):
            total = jnp.sum(jnp.where(seg == s, acc, 0.0), axis=1, keepdims=True)
            out = jnp.where(seg == s, total, out)
        return out

    def first(x):
        fx = fx_at(x)
        return [
            row(4, k, x) * cst[0, k] + fx * (row(5, k, x) * cst[4, 0] + row(6, k, x) * cst[1, k])
            for k in range(nk)
        ]

    rr0, rw0 = sweep(first, r0, w)
    alpha0 = rr0 / rw0
    for k in range(nk):
        cst[3, k] = jnp.where(mask_at(k), alpha0, 0.0)
    rr1, rw1 = sweep(lambda x: [r0[x, k] - cst[3, k] * w[x, k] for k in range(nk)], r1, w2)
    beta0 = rr1 / rr0
    alpha1 = rr1 / (rw1 - beta0 / alpha0 * rr1)
    gamma = alpha1 * beta0 / alpha0
    for k in range(nk):
        cst[3, k] = jnp.where(mask_at(k), alpha1, 0.0)

    def third(x):
        return [
            r1[x, k] + gamma * (r1[x, k] - r0[x, k]) - cst[3, k] * w2[x, k] for k in range(nk)
        ]

    rr2, rw2 = sweep(third, r2, None)
    beta1 = rr2 / rr1
    alpha2 = rr2 / (rw2 - beta1 / alpha1 * rr2)
    c2 = alpha2
    c1 = alpha1 + alpha2 * beta1
    c0 = alpha0 + c1 * beta0
    low = level.margin

    def basis(x):
        fx = fx_at(x)
        return [
            fx * cst[2, k] + (c0 * r0[x, k] + (c1 * r1[x, k] + c2 * r2[x, k])) for k in range(nk)
        ]

    def diagonals(state, u, image):
        return tuple(
            state[s] + u * (pltpu.roll(image, 8 - s, 0) if s else image) for s in range(5)
        )

    acc = pipeline(7, low, low + level.edge, planes[1], basis, phi, None, diagonals, (zero,) * 5)
    return acc, seg


def stencil(level, acc, seg, masks, elements):
    out = jnp.zeros((8, LANES), F32)
    for e, s in enumerate(elements):
        for n in range(5):
            total = jnp.sum(jnp.where(seg == s, acc[n], 0.0), axis=1, keepdims=True)
            out = out + total * masks[e * 5 + n]
    return out


class Shifted:
    def __init__(self, ref, first, column=None):
        self.ref = ref
        self.first = first
        self.column = column

    def place(self, index):
        x, k = index
        return (x - self.first, k) if self.column is None else (self.column, x - self.first, k)

    def __getitem__(self, index):
        return self.ref[self.place(index)]

    def __setitem__(self, index, value):
        self.ref[self.place(index)] = value


def local_work(own, hx, hy, hc, matrix, masks, phi_f, phi_t, line, ext, pairs, small, merged, *scratch):
    pk_f, wt_f, ym_f, turned_f, cst_f, *fields_f = scratch[:18]
    pk_t, wt_t, ym_t, turned_t, cst_t, *fields_t = scratch[18:]
    assemble(own, hx, hy, hc, ext)
    pack_twin(ext, matrix, pairs, small, pk_t)
    face_arrays(TWIN, pk_t, wt_t, ym_t, turned_t)
    acc, seg = basis_solve(TWIN, wt_t, ym_t, cst_t, *fields_t, Shifted(phi_t, TWIN.margin), TWIN_PLANES)
    parts = [stencil(TWIN, acc, seg, masks, (2 * col, 2 * col + 1)) for col in range(2)]
    total = pltpu.roll(parts[0], 32, 1) + pltpu.roll(parts[1], 48, 1)

    def body(col, total):
        pack_fine(ext, pk_f, merged, col)
        face_arrays(FINE, pk_f, wt_f, ym_f, turned_f)
        phi = Shifted(phi_f, FINE.margin, col)
        acc, seg = basis_solve(FINE, wt_f, ym_f, cst_f, *fields_f, phi, FINE_PLANES)
        part = stencil(FINE, acc, seg, masks, (0, 1))
        here = jnp.full((8, LANES), col, jnp.int32) == 0
        return total + jnp.where(here, part, pltpu.roll(part, 16, 1))

    total = lax.fori_loop(0, 2, body, total)
    line[...] = jnp.sum(total, axis=0, keepdims=True)


def local_scratch():
    def scratch(level, depth):
        field = pltpu.VMEM((level.nx, level.nk, 8, LANES), F32)
        return [
            pltpu.VMEM((3, level.nk + 1, level.nxr + 8, LANES), F32),
            pltpu.VMEM((11, level.nk, level.nxr, LANES), F32),
            pltpu.VMEM((2, level.nxr, LANES), F32),
            pltpu.VMEM((2, level.nk, level.nxr, LANES), F32),
            pltpu.VMEM((5, level.nk, 8, LANES), F32),
        ] + [field] * 5 + (
            [pltpu.VMEM((depth, level.nk, 8, LANES), F32)] * 3 + [pltpu.VMEM((depth, 2, 8, LANES), F32)]
        ) * 2

    return [
        pltpu.VMEM((3, 18, 48, LANES), F32),
        pltpu.VMEM((18 * 24, LANES), F32),
        pltpu.VMEM((18 * 24, LANES), F32),
        pltpu.VMEM((3, FINE.nk + 1, GROUP, LANES), F32),
    ] + scratch(FINE, max(FINE_PLANES)) + scratch(TWIN, max(TWIN_PLANES))


def coarse_solve(quantity, lane):
    second = (lane & 63) >= 32
    place = lane & 31

    def next_q(x):
        same = pltpu.roll(x, LANES - 32, 1)
        inner = pltpu.roll(x, 31, 1)
        outer = pltpu.roll(x, 63, 1)
        return jnp.where(second, jnp.where(place < 31, inner, outer), same)

    def prev_q(x):
        same = pltpu.roll(x, 32, 1)
        inner = pltpu.roll(x, LANES - 31, 1)
        outer = pltpu.roll(x, LANES - 63, 1)
        return jnp.where(second, same, jnp.where(place > 0, inner, outer))

    def next_p(x):
        return pltpu.roll(x, 7, 0)

    def prev_p(x):
        return pltpu.roll(x, 1, 0)

    entry = {}
    n = 0
    for a in range(4):
        for b in range(a, 4):
            entry[a, b] = entry[b, a] = quantity(n)
            n += 1

    def corners(x):
        side = next_q(x)
        return [x, side, next_p(x), next_p(side)]

    def gather(parts):
        side = prev_q(parts[1] + prev_p(parts[3]))
        return parts[0] + side + prev_p(parts[2])

    def operate(x):
        values = corners(x)
        parts = []
        for a in range(4):
            terms = [entry[a, b] * values[b] for b in range(4)]
            parts.append((terms[0] + terms[1]) + (terms[2] + terms[3]))
        return gather(parts)

    upper = lane >= 64

    def total(x):
        column = jnp.sum(x, axis=0, keepdims=True)
        lo = jnp.sum(jnp.where(upper[:1], 0.0, column), axis=1, keepdims=True)
        hi = jnp.sum(jnp.where(upper[:1], column, 0.0), axis=1, keepdims=True)
        return jnp.where(upper, hi, lo)

    residual = -gather([quantity(10 + a) for a in range(4)])
    norm = total(residual * residual)
    image = operate(residual)
    alpha = norm / total(residual * image)
    update = alpha * residual
    after = residual - alpha * image
    norm_next = total(after * after)
    direction = after + norm_next / norm * residual
    image = operate(direction)
    alpha = norm_next / total(direction * image)
    update = update + alpha * direction
    return [value for value in corners(update)]


def greet_groups():
    i = lax.axis_index("gx")
    j = lax.axis_index("gy")
    ni = lax.axis_size("gx")
    nj = lax.axis_size("gy")
    barrier = pltpu.get_barrier_semaphore()

    def greet_y(d, carry):
        pl.semaphore_signal(barrier, inc=1, device_id=(i, lax.rem(j + d, nj)), device_id_type=MESH)
        return carry

    def greet_x(d, carry):
        pl.semaphore_signal(barrier, inc=1, device_id=(lax.rem(i + d, ni), j), device_id_type=MESH)
        return carry

    lax.fori_loop(1, nj, greet_y, 0)
    lax.fori_loop(1, ni, greet_x, 0)


def coarse_work(line, rows, block, grid, send1, recv1, send2, recv2):
    i = lax.axis_index("gx")
    j = lax.axis_index("gy")
    ni = lax.axis_size("gx")
    nj = lax.axis_size("gy")
    pl.semaphore_wait(pltpu.get_barrier_semaphore(), ni + nj - 2)

    def copy_y(d):
        return pltpu.make_async_remote_copy(
            src_ref=line, dst_ref=rows.at[j], send_sem=send1.at[d], recv_sem=recv1.at[d],
            device_id=(i, lax.rem(j + d, nj)), device_id_type=MESH,
        )

    def copy_x(d):
        return pltpu.make_async_remote_copy(
            src_ref=block, dst_ref=grid.at[pl.ds(pl.multiple_of(i * 16, 16), 16)], send_sem=send2.at[d], recv_sem=recv2.at[d],
            device_id=(lax.rem(i + d, ni), j), device_id_type=MESH,
        )

    def start_y(d, carry):
        copy_y(d).start()
        return carry

    def wait_y(d, carry):
        copy_y(d).wait()
        return carry

    def start_x(d, carry):
        copy_x(d).start()
        return carry

    def wait_x(d, carry):
        copy_x(d).wait()
        return carry

    lax.fori_loop(1, nj, start_y, 0)
    rows[j] = line[...]
    lax.fori_loop(1, nj, wait_y, 0)
    quarter = rows[:, 0, :]
    turned = jnp.transpose(jnp.concatenate([quarter] * 4, axis=0))
    lane16 = lane_iota(16)
    out = turned[48:64]
    for b in range(3):
        out = jnp.where((lane16 >= 32 * b) & (lane16 < 32 * b + 32), turned[16 * b:16 * b + 16], out)
    block[...] = out
    lax.fori_loop(1, ni, start_x, 0)
    grid[pl.ds(pl.multiple_of(i * 16, 16), 16), :] = out
    lax.fori_loop(1, ni, wait_x, 0)
    return coarse_solve(lambda q: grid[pl.ds(q, 8, stride=16), :], lane_iota(8))


def fold_rows(values, sub):
    low = sub < 4
    step = [
        jnp.where(low, values[n], values[n + 4])
        + pltpu.roll(jnp.where(low, values[n + 4], values[n]), 4, 0)
        for n in range(4)
    ]
    for shift in (2, 1):
        keep = (sub & shift) == 0
        step = [
            jnp.where(
                keep,
                step[n] + pltpu.roll(step[n], 8 - shift, 0),
                step[n + shift] + pltpu.roll(step[n + shift], shift, 0),
            )
            for n in range(shift)
        ]
    return step[0]


def pressure_work(phi_f, phi_t, nodes, fine, twin, rows_f, rows_t):
    i = lax.axis_index("gx")
    j = lax.axis_index("gy")
    sub = lax.broadcasted_iota(jnp.int32, (8, LANES), 0)
    lane = lane_iota(8)
    corner, az = sub >> 1, (sub & 1) == 1

    def own_nodes(level, col):
        here = (sub == i) & (lane == level * 64 + col * 32 + j)
        out = jnp.zeros((8, LANES), F32)
        for a in range(4):
            value = jnp.where(here, nodes[a], 0.0)
            value = jnp.sum(jnp.sum(value, axis=0, keepdims=True), axis=1, keepdims=True)
            out = jnp.where(corner == a, value, out)
        return jnp.where(az, out, 1.0), jnp.where(az, 0.0, out)

    _, seg, _ = split_lane(FINE, lane)
    fine_weights = []
    for col in range(2):
        first, second = own_nodes(0, col)
        fine_weights.append(jnp.where(seg == 0, first, second))
    _, seg, _ = split_lane(TWIN, lane)
    twin_weights = jnp.zeros((8, LANES), F32)
    for col in range(2):
        first, second = own_nodes(1, col)
        twin_weights = jnp.where(seg == 2 * col, first, twin_weights)
        twin_weights = jnp.where(seg == 2 * col + 1, second, twin_weights)

    def fine_rows(k, carry):
        for col in range(2):
            for g in range(EL // 8):
                values = [phi_f[col, 8 * g + n, k] * fine_weights[col] for n in range(8)]
                rows_f[col, k, 8 * g:8 * g + 8, :] = fold_rows(values, sub)
        return carry

    lax.fori_loop(0, FINE.nk, fine_rows, 0)

    def twin_rows(k, carry):
        for g in range(EL // 16):
            values = [phi_t[8 * g + n, k] * twin_weights for n in range(8)]
            rows_t[k, 8 * g:8 * g + 8, :] = fold_rows(values, sub)
        return carry

    lax.fori_loop(0, TWIN.nk, twin_rows, 0)

    def turn(value, shift):
        return pltpu.roll(value, shift % LANES, 1) if shift % LANES else value

    wide = lane_iota(EL)
    for col in range(2):
        for t in range(8):
            out = None
            for h in range(4):
                y = 4 * t + h + MX
                c, k = y // FINE.nk, y % FINE.nk
                for e in range(2):
                    to = h * 32 + e * 16
                    piece = turn(rows_f[col, k], to - (c * GROUP + e * 20 + MZ))
                    out = piece if out is None else jnp.where(wide >= to, piece, out)
            fine[:, (col * 8 + t) * LANES:(col * 8 + t + 1) * LANES] = out
    wide = lane_iota(EL // 2)
    for t in range(4):
        out = None
        for h in range(8):
            col, y = (8 * t + h) // 16, (8 * t + h) % 16 + MX // 2
            c, k = y // TWIN.nk, y % TWIN.nk
            for e in range(2):
                to = h * 16 + e * 8
                piece = turn(rows_t[k], to - (c * GROUP + col * 20 + e * 10 + MZ // 2))
                out = piece if out is None else jnp.where(wide >= to, piece, out)
        twin[:, t * LANES:(t + 1) * LANES] = out


def solve_kernel(own, hx, hy, hc, matrix, masks, fine, twin, phi_f, phi_t, rows_f, rows_t, line, *scratch):
    exchange, local = scratch[:7], scratch[7:]
    greet_groups()
    local_work(own, hx, hy, hc, matrix, masks, phi_f, phi_t, line, *local)
    nodes = coarse_work(line, *exchange)
    pressure_work(phi_f, phi_t, nodes, fine, twin, rows_f, rows_t)


def solve(perm, hx, hy, hc, ni, nj):
    vmem = pl.BlockSpec(memory_space=pltpu.VMEM)
    return pl.pallas_call(
        solve_kernel,
        out_shape=(
            jax.ShapeDtypeStruct((EL, 2048), F32),
            jax.ShapeDtypeStruct((EL // 2, 512), F32),
        ),
        in_specs=[vmem] * 6,
        out_specs=(vmem, vmem),
        scratch_shapes=[
            pltpu.VMEM((2, EL, FINE.nk, 8, LANES), F32),
            pltpu.VMEM((EL // 2, TWIN.nk, 8, LANES), F32),
            pltpu.VMEM((2, FINE.nk, EL, LANES), F32),
            pltpu.VMEM((TWIN.nk, EL // 2, LANES), F32),
            pltpu.VMEM((1, LANES), F32),
            pltpu.VMEM((nj, 1, LANES), F32),
            pltpu.VMEM((16, LANES), F32),
            pltpu.VMEM((ni * 16, LANES), F32),
            pltpu.SemaphoreType.DMA((nj,)),
            pltpu.SemaphoreType.DMA((nj,)),
            pltpu.SemaphoreType.DMA((ni,)),
            pltpu.SemaphoreType.DMA((ni,)),
        ] + local_scratch(),
        compiler_params=pltpu.CompilerParams(
            collective_id=1, has_side_effects=True, vmem_limit_bytes=VLIMIT
        ),
    )(
        perm, hx, hy, hc,
        jnp.asarray(coarsen_matrix(), jnp.bfloat16), jnp.asarray(stencil_masks()),
    )


def solution(mesh):
    ni, nj = mesh.shape["gx"], mesh.shape["gy"]

    def shards(perm):
        hx, hy, hc = halo(perm)
        return solve(perm, hx, hy, hc, ni, nj)

    return jax.shard_map(
        shards,
        mesh=mesh,
        in_specs=(P(None, "gx", "gy"),),
        out_specs=(P("gx", "gy"), P("gx", "gy")),
        check_vma=False,
    )
```

```python
import functools

import jax
import jax.numpy as jnp
import numpy as np
from jax import lax
from jax.experimental import pallas as pl
from jax.experimental.pallas import tpu as pltpu
from jax.sharding import PartitionSpec as P

EL = 32
ELZ = 16
MX = 4
MZ = 2
LANES = 128
GROUP = 40
MESH = pl.DeviceIdType.MESH
F32 = jnp.float32
VLIMIT = 60 * 1024 * 1024
FINE_PLANES = (4, 4)
TWIN_PLANES = (5, 8)


class Level:
    def __init__(self, nk, nx, zw, edge, edge_depth, margin, margin_depth, spacing):
        self.nk = nk
        self.nx = nx
        self.nxr = -(-nx // 8) * 8
        self.zw = zw
        self.nseg = GROUP // zw
        self.edge = edge
        self.edge_depth = edge_depth
        self.margin = margin
        self.margin_depth = margin_depth
        self.spacing = spacing


FINE = Level(13, 40, 20, EL, ELZ, MX, MZ, 1.0)
TWIN = Level(7, 20, 10, EL // 2, ELZ // 2, MX // 2, MZ // 2, 2.0)


def stencil_masks():
    masks = np.zeros((10, 8, LANES), np.float32)

    def put(e, a, b, q):
        s = (b - a) % 8
        if s > 4:
            a, s = b, 8 - s
        masks[e * 5 + s, a, q] += 1.0

    q = 0
    for a in range(4):
        for b in range(a, 4):
            put(0, 2 * a + 1, 2 * b + 1, q)
            put(1, 2 * a, 2 * b, q)
            q += 1
    for a in range(4):
        for b in range(4):
            put(0, 2 * a + 1, 2 * b, q)
        q += 1
    return masks


def coarsen_matrix():
    matrix = np.zeros((LANES, LANES), np.float32)
    for h in range(4):
        for e in range(2):
            for zz in range(10):
                for part in range(2):
                    z = min(max(e * ELZ - MZ + 2 * zz + part, 0), 31)
                    matrix[h * 32 + z, (h // 2) * 20 + e * 10 + zz] += 0.125
    return matrix


def lane_iota(rows):
    return lax.broadcasted_iota(jnp.int32, (rows, LANES), 1)


def groups(lane):
    return (lane >= 40).astype(jnp.int32) + (lane >= 80).astype(jnp.int32) + (lane >= 120).astype(jnp.int32)


def split_lane(level, lane):
    chunk = groups(lane)
    inner = lane - GROUP * chunk
    seg = jnp.zeros_like(lane)
    for s in range(1, level.nseg):
        seg = seg + (inner >= s * level.zw).astype(jnp.int32)
    return chunk, seg, inner - level.zw * seg


def harmonic(first, second, spacing):
    return spacing * 2.0 * first * second / (first + second)


def halo_plans(perm, hx, hy, hc):
    i = lax.axis_index("gx")
    j = lax.axis_index("gy")
    ni = lax.axis_size("gx")
    nj = lax.axis_size("gy")
    up, down = lax.rem(i + 1, ni), lax.rem(i + ni - 1, ni)
    right, left = lax.rem(j + 1, nj), lax.rem(j + nj - 1, nj)
    rows, width = perm.shape[1], perm.shape[2]
    west, east = pl.ds(0, MX), pl.ds(rows - MX, MX)
    low, high = pl.ds(0, LANES), pl.ds(width - LANES, LANES)
    return [
        (perm.at[:, east], hx.at[0], (up, j)),
        (perm.at[:, west], hx.at[1], (down, j)),
        (perm.at[:, :, high], hy.at[0], (i, right)),
        (perm.at[:, :, low], hy.at[1], (i, left)),
        (perm.at[:, east, high], hc.at[0], (up, right)),
        (perm.at[:, east, low], hc.at[1], (up, left)),
        (perm.at[:, west, high], hc.at[2], (down, right)),
        (perm.at[:, west, low], hc.at[3], (down, left)),
    ]


def halo_copies(plans, send, recv):
    return [
        pltpu.make_async_remote_copy(
            src_ref=src, dst_ref=dst, send_sem=send.at[n], recv_sem=recv.at[n],
            device_id=target, device_id_type=MESH,
        )
        for n, (src, dst, target) in enumerate(plans)
    ]


def assemble(own, hx, hy, hc, ext):
    rows = own.shape[1]

    def body(m, carry):
        for t in range(18):
            if t == 0:
                top, mid, low = hc[0, m], hy[0, m], hc[2, m]
            elif t == 17:
                top, mid, low = hc[1, m], hy[1, m], hc[3, m]
            else:
                lanes = pl.ds((t - 1) * LANES, LANES)
                top, mid, low = hx[0, m, :, lanes], own[m, :, lanes], hx[1, m, :, lanes]
            ext[m, t, 0:MX, :] = top
            ext[m, t, MX:MX + rows, :] = mid
            ext[m, t, MX + rows:2 * MX + rows, :] = low
            ext[m, t, 2 * MX + rows:, :] = jnp.ones((8, LANES), F32)
        return carry

    lax.fori_loop(0, 3, body, 0)


def pack_fine(ext, packed, merged, column):
    lane = lane_iota(GROUP)
    chunk, _, _ = split_lane(FINE, lane)
    inner = lane - GROUP * chunk

    def body(m, carry):
        for k in range(FINE.nk + 1):
            lines = []
            for c in range(3):
                y = FINE.nk * c + k
                tile = ext[m, column * 8 + y // 4, 0:40, :]
                shift = (c * GROUP + MZ - (y % 4) * 32) % LANES
                lines.append(pltpu.roll(tile, shift, 1) if shift else tile)
            merged[m, k] = jnp.where(lane < GROUP, lines[0], jnp.where(lane < 2 * GROUP, lines[1], lines[2]))
        return carry

    lax.fori_loop(0, 3, body, 0)

    def widen(m, carry):
        for k in range(FINE.nk + 1):
            q = merged[m, k]
            out = jnp.where(inner < MZ, pltpu.roll(q, LANES - 1, 1), q)
            out = jnp.where(inner > 19, pltpu.roll(q, 4, 1), out)
            packed[m, k, 0:40, :] = jnp.where(inner > 37, pltpu.roll(q, 5, 1), out)
            packed[m, k, 40:48, :] = jnp.ones((8, LANES), F32)
        return carry

    lax.fori_loop(0, 3, widen, 0)


def pack_twin(ext, matrix, pairs, small, packed):
    lane = lane_iota(24)
    chunk = groups(lane)
    half = jnp.zeros_like(lane)
    for s in range(1, 7):
        half = half + (lane >= 20 * s).astype(jnp.int32)
    weights = matrix[...]

    def body(m, carry):
        for t in range(18):
            first = ext[m, t, pl.ds(0, 24, stride=2), :]
            second = ext[m, t, pl.ds(1, 24, stride=2), :]
            pairs[t * 24:(t + 1) * 24, :] = first + second
        value = pairs[...]
        high = value.astype(jnp.bfloat16)
        rest = value - high.astype(F32)
        mid = rest.astype(jnp.bfloat16)
        low = (rest - mid.astype(F32)).astype(jnp.bfloat16)
        small[...] = (
            jnp.dot(high, weights, preferred_element_type=F32)
            + jnp.dot(mid, weights, preferred_element_type=F32)
            + jnp.dot(low, weights, preferred_element_type=F32)
        )
        for k in range(TWIN.nk + 1):
            out = jnp.ones((24, LANES), F32)
            for c in range(3):
                y = min(TWIN.nk * c + k, TWIN.nx - 1)
                for col in range(2):
                    base = (col * 8 + y // 2) * 24
                    line = small[base:base + 24, :]
                    shift = (c * GROUP + col * 20 - (y % 2) * 20) % LANES
                    line = pltpu.roll(line, shift, 1) if shift else line
                    out = jnp.where(half == 2 * c + col, line, out)
            packed[m, k, 0:24, :] = out
            packed[m, k, 24:32, :] = jnp.ones((8, LANES), F32)
        return carry

    lax.fori_loop(0, 3, body, 0)


def face_arrays(level, packed, wt, ym, turned):
    nk, nx, nxr = level.nk, level.nx, level.nxr
    lane = lane_iota(nxr)
    chunk, seg, z = split_lane(level, lane)
    row = lax.broadcasted_iota(jnp.int32, (nxr, LANES), 0)
    ml, mz = level.margin, level.margin_depth
    inside_xz = (row > 0) & (row < nx - 1) & (z > 0) & (z < level.zw - 1) & (chunk < 3)
    el_x = (row >= ml) & (row < ml + level.edge)
    el_z = (z >= mz) & (z < mz + level.edge_depth) & (chunk < 3)
    el_xf = (row >= ml) & (row < ml + level.edge - 1)
    el_zf = (z >= mz) & (z < mz + level.edge_depth - 1) & (chunk < 3)
    first_edge = seg == 0
    if level.nseg == 4:
        first_edge = first_edge | (seg == 2)
    first_edge = first_edge & (z == 0)
    last_edge = jnp.logical_not((seg == 0) | (seg == 2)) & (z == level.zw - 2)

    el_zb = (z > mz) & (z < mz + level.edge_depth) & (chunk < 3)
    below_first = (z == 1) & ((seg == 0) | (seg == 2))
    below_last = (z == level.zw - 1) & jnp.logical_not((seg == 0) | (seg == 2))
    for k in range(nk):
        kz = packed[2, k, 0:nxr, :]
        turned[0, k] = pltpu.roll(kz, LANES - 1, 1)
        turned[1, k] = pltpu.roll(kz, 1, 1)

    def body(k, carry):
        y = chunk * nk + k
        inside = inside_xz & (y > 0) & (y < nx - 1)
        el_y = (y >= ml) & (y < ml + level.edge)
        el_yf = (y >= ml) & (y < ml + level.edge - 1)
        tx = harmonic(packed[0, k, 0:nxr, :], packed[0, k, 1:nxr + 1, :], level.spacing)
        ty = harmonic(packed[1, k, 0:nxr, :], packed[1, k + 1, 0:nxr, :], level.spacing)
        kz = packed[2, k, 0:nxr, :]
        kz_after, kz_before, kz_here = turned[0, k], turned[1, k], kz
        if level is FINE:
            kz_here = jnp.where(first_edge, kz_after, kz)
            kz_after = jnp.where(last_edge, kz, kz_after)
            kz_before = jnp.where(below_first, kz, kz_before)
            kz = jnp.where(below_last, kz_before, kz)
        tz = harmonic(kz_here, kz_after, level.spacing)
        tz_below = harmonic(kz_before, kz, level.spacing)
        wt[0, k] = tx
        wt[1, k] = ty
        wt[2, k] = tz
        wt[3, k] = tz_below
        wt[4, k] = jnp.where(inside, tx - pltpu.roll(tx, 1, 0), 0.0)
        wt[6, k] = jnp.where(inside, tz - tz_below, 0.0)
        wt[7, k] = jnp.where(el_xf & el_y & el_z, tx, 0.0)
        wt[8, k] = jnp.where(el_x & el_yf & el_z, ty, 0.0)
        wt[9, k] = jnp.where(el_x & el_y & el_zf, tz, 0.0)
        wt[10, k] = jnp.where(el_x & el_y & el_zb, tz_below, 0.0)
        return carry

    lax.fori_loop(0, nk, body, 0)
    ym[0] = pltpu.roll(wt[1, nk - 1], GROUP, 1)
    ym[1] = pltpu.roll(wt[8, nk - 1], GROUP, 1)

    def inside_at(k):
        y = chunk * nk + k
        return inside_xz & (y > 0) & (y < nx - 1)

    wt[5, 0] = jnp.where(inside_at(0), wt[1, 0] - ym[0], 0.0)

    def second(k, carry):
        wt[5, k] = jnp.where(inside_at(k), wt[1, k] - wt[1, k - 1], 0.0)
        return carry

    lax.fori_loop(1, nk, second, 0)


def basis_solve(level, wt, ym, cst, r0, r1, r2, w, w2, *rest):
    *rings, phi, planes = rest
    rings = rings[:4], rings[4:]
    nk, nx = level.nk, level.nx
    lane = lane_iota(8)
    chunk, seg, z = split_lane(level, lane)
    sub = lax.broadcasted_iota(jnp.int32, (8, LANES), 0)
    ax, ay, az = sub >= 4, ((sub >> 1) & 1) == 1, (sub & 1) == 1

    def ramp(flag, place, length):
        return jnp.where(flag, place / length, 1.0 - place / length)

    fz = ramp(az, z.astype(F32) - level.margin_depth + 0.5, level.edge_depth)
    sx = jnp.where(ax, 1.0 / level.edge, -1.0 / level.edge)
    sy = jnp.where(ay, 1.0 / level.edge, -1.0 / level.edge)
    sz = jnp.where(az, 1.0 / level.edge_depth, -1.0 / level.edge_depth)
    cst[4, 0] = sy * fz
    cst[4, 1] = sx
    for k in range(nk):
        fy = ramp(ay, (chunk * nk + k).astype(F32) - level.margin + 0.5, level.edge)
        cst[0, k] = sx * fy * fz
        cst[1, k] = sz * fy
        cst[2, k] = fy * fz

    cst[4, 2] = jnp.where(ax, (0.5 - level.margin) / level.edge, 1.0 - (0.5 - level.margin) / level.edge)

    def fx_at(x):
        return cst[4, 2] + cst[4, 1] * x.astype(F32)

    def mask_at(k):
        y = chunk * nk + k
        return (y > 0) & (y < nx - 1) & (z > 0) & (z < level.zw - 1) & (chunk < 3)

    cst[4, 3] = jnp.zeros((8, LANES), F32)
    zero = cst[4, 3]

    def row(n, k, x):
        return wt[n, k, pl.ds(x, 8, stride=0), :]

    def pipeline(base, low, high, depth, produce, keep, keep_w, consume, state):
        def apply(ring, x0, after, fx_prev, state):
            u_ring, above, below, beside = ring
            ahead = [u_ring[0, k] for k in range(nk)]
            for p in range(depth):
                x = x0 + p
                u = ahead
                ahead = after if p == depth - 1 else [u_ring[p + 1, k] for k in range(nk)]
                fy_prev = ym[base // 7, pl.ds(x, 8, stride=0), :] * (beside[p, 1] - u[0])
                image, fx_new = [], []
                for k in range(nk):
                    flux = row(base, k, x) * (u[k] - ahead[k])
                    fx_new.append(flux)
                    out = flux - fx_prev[k]
                    side = u[k + 1] if k < nk - 1 else beside[p, 0]
                    fy = row(base + 1, k, x) * (u[k] - side)
                    out = out + (fy - fy_prev)
                    fy_prev = fy
                    out = out + row(base + 2, k, x) * (u[k] - above[p, k])
                    image.append(out + row(base + 3, k, x) * (u[k] - below[p, k]))
                    if keep_w is not None:
                        keep_w[x, k] = image[k]
                    state = consume(state, u[k], image[k])
                fx_prev = fx_new
            return fx_prev, state

        def make(ring, x0):
            u_ring, above, below, beside = ring
            first = None
            for p in range(depth):
                u = produce(x0 + p)
                first = u if first is None else first
                for k in range(nk):
                    keep[x0 + p, k] = u[k]
                    u_ring[p, k] = u[k]
                    above[p, k] = pltpu.roll(u[k], LANES - 1, 1)
                    below[p, k] = pltpu.roll(u[k], 1, 1)
                beside[p, 0] = pltpu.roll(u[0], LANES - GROUP, 1)
                beside[p, 1] = pltpu.roll(u[nk - 1], GROUP, 1)
            return first

        even, odd = rings
        make(even, jnp.int32(low))

        def body(n, carry):
            fx_prev, state = carry
            x0 = low + n * (2 * depth)
            after = make(odd, x0 + depth)
            fx_prev, state = apply(even, x0, after, fx_prev, state)
            after = make(even, x0 + 2 * depth)
            return apply(odd, x0 + depth, after, fx_prev, state)

        count = (high - low) // (2 * depth)
        fx_prev, state = lax.fori_loop(0, count - 1, body, ([zero] * nk, state))
        x0 = jnp.int32(high - 2 * depth)
        after = make(odd, x0 + depth)
        fx_prev, state = apply(even, x0, after, fx_prev, state)
        _, state = apply(odd, x0 + depth, [zero] * nk, fx_prev, state)
        return state

    def norms(state, u, image):
        return state[0] + u * u, state[1] + u * image

    def sweep(produce, keep, keep_w):
        state = pipeline(0, 0, nx, planes[0], produce, keep, keep_w, norms, (zero, zero))
        if keep_w is not None:
            for k in range(nk):
                keep_w[0, k] = zero
                keep_w[nx - 1, k] = zero
        return by_segment(state[0]), by_segment(state[1])

    def by_segment(acc):
        out = jnp.sum(jnp.where(seg == 0, acc, 0.0), axis=1, keepdims=True)
        for s in range(1, level.nseg):
            total = jnp.sum(jnp.where(seg == s, acc, 0.0), axis=1, keepdims=True)
            out = jnp.where(seg == s, total, out)
        return out

    def first(x):
        fx = fx_at(x)
        return [
            row(4, k, x) * cst[0, k] + fx * (row(5, k, x) * cst[4, 0] + row(6, k, x) * cst[1, k])
            for k in range(nk)
        ]

    rr0, rw0 = sweep(first, r0, w)
    alpha0 = rr0 / rw0
    for k in range(nk):
        cst[3, k] = jnp.where(mask_at(k), alpha0, 0.0)
    rr1, rw1 = sweep(lambda x: [r0[x, k] - cst[3, k] * w[x, k] for k in range(nk)], r1, w2)
    beta0 = rr1 / rr0
    alpha1 = rr1 / (rw1 - beta0 / alpha0 * rr1)
    gamma = alpha1 * beta0 / alpha0
    for k in range(nk):
        cst[3, k] = jnp.where(mask_at(k), alpha1, 0.0)

    def third(x):
        return [
            r1[x, k] + gamma * (r1[x, k] - r0[x, k]) - cst[3, k] * w2[x, k] for k in range(nk)
        ]

    rr2, rw2 = sweep(third, r2, None)
    beta1 = rr2 / rr1
    alpha2 = rr2 / (rw2 - beta1 / alpha1 * rr2)
    c2 = alpha2
    c1 = alpha1 + alpha2 * beta1
    c0 = alpha0 + c1 * beta0
    low = level.margin

    def basis(x):
        fx = fx_at(x)
        return [
            fx * cst[2, k] + (c0 * r0[x, k] + (c1 * r1[x, k] + c2 * r2[x, k])) for k in range(nk)
        ]

    def diagonals(state, u, image):
        return tuple(
            state[s] + u * (pltpu.roll(image, 8 - s, 0) if s else image) for s in range(5)
        )

    acc = pipeline(7, low, low + level.edge, planes[1], basis, phi, None, diagonals, (zero,) * 5)
    return acc, seg


def stencil(level, acc, seg, masks, elements):
    out = jnp.zeros((8, LANES), F32)
    for e, s in enumerate(elements):
        for n in range(5):
            total = jnp.sum(jnp.where(seg == s, acc[n], 0.0), axis=1, keepdims=True)
            out = out + total * masks[e * 5 + n]
    return out


class Shifted:
    def __init__(self, ref, first, column=None):
        self.ref = ref
        self.first = first
        self.column = column

    def place(self, index):
        x, k = index
        return (x - self.first, k) if self.column is None else (self.column, x - self.first, k)

    def __getitem__(self, index):
        return self.ref[self.place(index)]

    def __setitem__(self, index, value):
        self.ref[self.place(index)] = value


def local_work(own, hx, hy, hc, matrix, masks, phi_f, phi_t, line, ext, pairs, small, merged, *scratch):
    pk_f, wt_f, ym_f, turned_f, cst_f, *fields_f = scratch[:18]
    pk_t, wt_t, ym_t, turned_t, cst_t, *fields_t = scratch[18:]
    assemble(own, hx, hy, hc, ext)
    pack_twin(ext, matrix, pairs, small, pk_t)
    face_arrays(TWIN, pk_t, wt_t, ym_t, turned_t)
    acc, seg = basis_solve(TWIN, wt_t, ym_t, cst_t, *fields_t, Shifted(phi_t, TWIN.margin), TWIN_PLANES)
    parts = [stencil(TWIN, acc, seg, masks, (2 * col, 2 * col + 1)) for col in range(2)]
    total = pltpu.roll(parts[0], 32, 1) + pltpu.roll(parts[1], 48, 1)

    def body(col, total):
        pack_fine(ext, pk_f, merged, col)
        face_arrays(FINE, pk_f, wt_f, ym_f, turned_f)
        phi = Shifted(phi_f, FINE.margin, col)
        acc, seg = basis_solve(FINE, wt_f, ym_f, cst_f, *fields_f, phi, FINE_PLANES)
        part = stencil(FINE, acc, seg, masks, (0, 1))
        here = jnp.full((8, LANES), col, jnp.int32) == 0
        return total + jnp.where(here, part, pltpu.roll(part, 16, 1))

    total = lax.fori_loop(0, 2, body, total)
    line[...] = jnp.sum(total, axis=0, keepdims=True)


def local_scratch():
    def scratch(level, depth):
        field = pltpu.VMEM((level.nx, level.nk, 8, LANES), F32)
        return [
            pltpu.VMEM((3, level.nk + 1, level.nxr + 8, LANES), F32),
            pltpu.VMEM((11, level.nk, level.nxr, LANES), F32),
            pltpu.VMEM((2, level.nxr, LANES), F32),
            pltpu.VMEM((2, level.nk, level.nxr, LANES), F32),
            pltpu.VMEM((5, level.nk, 8, LANES), F32),
        ] + [field] * 5 + (
            [pltpu.VMEM((depth, level.nk, 8, LANES), F32)] * 3 + [pltpu.VMEM((depth, 2, 8, LANES), F32)]
        ) * 2

    return [
        pltpu.VMEM((3, 18, 48, LANES), F32),
        pltpu.VMEM((18 * 24, LANES), F32),
        pltpu.VMEM((18 * 24, LANES), F32),
        pltpu.VMEM((3, FINE.nk + 1, GROUP, LANES), F32),
    ] + scratch(FINE, max(FINE_PLANES)) + scratch(TWIN, max(TWIN_PLANES))


def coarse_solve(quantity, lane):
    second = (lane & 63) >= 32
    place = lane & 31

    def next_q(x):
        same = pltpu.roll(x, LANES - 32, 1)
        inner = pltpu.roll(x, 31, 1)
        outer = pltpu.roll(x, 63, 1)
        return jnp.where(second, jnp.where(place < 31, inner, outer), same)

    def prev_q(x):
        same = pltpu.roll(x, 32, 1)
        inner = pltpu.roll(x, LANES - 31, 1)
        outer = pltpu.roll(x, LANES - 63, 1)
        return jnp.where(second, same, jnp.where(place > 0, inner, outer))

    def next_p(x):
        return pltpu.roll(x, 7, 0)

    def prev_p(x):
        return pltpu.roll(x, 1, 0)

    entry = {}
    n = 0
    for a in range(4):
        for b in range(a, 4):
            entry[a, b] = entry[b, a] = quantity(n)
            n += 1

    def corners(x):
        side = next_q(x)
        return [x, side, next_p(x), next_p(side)]

    def gather(parts):
        side = prev_q(parts[1] + prev_p(parts[3]))
        return parts[0] + side + prev_p(parts[2])

    def operate(x):
        values = corners(x)
        parts = []
        for a in range(4):
            terms = [entry[a, b] * values[b] for b in range(4)]
            parts.append((terms[0] + terms[1]) + (terms[2] + terms[3]))
        return gather(parts)

    upper = lane >= 64

    def total(x):
        column = jnp.sum(x, axis=0, keepdims=True)
        lo = jnp.sum(jnp.where(upper[:1], 0.0, column), axis=1, keepdims=True)
        hi = jnp.sum(jnp.where(upper[:1], column, 0.0), axis=1, keepdims=True)
        return jnp.where(upper, hi, lo)

    residual = -gather([quantity(10 + a) for a in range(4)])
    norm = total(residual * residual)
    image = operate(residual)
    alpha = norm / total(residual * image)
    update = alpha * residual
    after = residual - alpha * image
    norm_next = total(after * after)
    direction = after + norm_next / norm * residual
    image = operate(direction)
    alpha = norm_next / total(direction * image)
    update = update + alpha * direction
    return [value for value in corners(update)]


def greet(plans):
    i = lax.axis_index("gx")
    j = lax.axis_index("gy")
    ni = lax.axis_size("gx")
    nj = lax.axis_size("gy")
    barrier = pltpu.get_barrier_semaphore()
    for _, _, target in plans:
        pl.semaphore_signal(barrier, inc=1, device_id=target, device_id_type=MESH)

    def greet_y(d, carry):
        pl.semaphore_signal(barrier, inc=1, device_id=(i, lax.rem(j + d, nj)), device_id_type=MESH)
        return carry

    def greet_x(d, carry):
        pl.semaphore_signal(barrier, inc=1, device_id=(lax.rem(i + d, ni), j), device_id_type=MESH)
        return carry

    lax.fori_loop(1, nj, greet_y, 0)
    lax.fori_loop(1, ni, greet_x, 0)
    pl.semaphore_wait(barrier, ni + nj - 2 + len(plans))


def coarse_work(line, rows, block, grid, send1, recv1, send2, recv2):
    i = lax.axis_index("gx")
    j = lax.axis_index("gy")
    ni = lax.axis_size("gx")
    nj = lax.axis_size("gy")
    def copy_y(d):
        return pltpu.make_async_remote_copy(
            src_ref=line, dst_ref=rows.at[j], send_sem=send1.at[d], recv_sem=recv1.at[d],
            device_id=(i, lax.rem(j + d, nj)), device_id_type=MESH,
        )

    def copy_x(d):
        return pltpu.make_async_remote_copy(
            src_ref=block, dst_ref=grid.at[pl.ds(pl.multiple_of(i * 16, 16), 16)], send_sem=send2.at[d], recv_sem=recv2.at[d],
            device_id=(lax.rem(i + d, ni), j), device_id_type=MESH,
        )

    def start_y(d, carry):
        copy_y(d).start()
        return carry

    def wait_y(d, carry):
        copy_y(d).wait()
        return carry

    def start_x(d, carry):
        copy_x(d).start()
        return carry

    def wait_x(d, carry):
        copy_x(d).wait()
        return carry

    lax.fori_loop(1, nj, start_y, 0)
    rows[j] = line[...]
    lax.fori_loop(1, nj, wait_y, 0)
    quarter = rows[:, 0, :]
    turned = jnp.transpose(jnp.concatenate([quarter] * 4, axis=0))
    lane16 = lane_iota(16)
    out = turned[48:64]
    for b in range(3):
        out = jnp.where((lane16 >= 32 * b) & (lane16 < 32 * b + 32), turned[16 * b:16 * b + 16], out)
    block[...] = out
    lax.fori_loop(1, ni, start_x, 0)
    grid[pl.ds(pl.multiple_of(i * 16, 16), 16), :] = out
    lax.fori_loop(1, ni, wait_x, 0)
    return coarse_solve(lambda q: grid[pl.ds(q, 8, stride=16), :], lane_iota(8))


def fold_rows(values, sub):
    low = sub < 4
    step = [
        jnp.where(low, values[n], values[n + 4])
        + pltpu.roll(jnp.where(low, values[n + 4], values[n]), 4, 0)
        for n in range(4)
    ]
    for shift in (2, 1):
        keep = (sub & shift) == 0
        step = [
            jnp.where(
                keep,
                step[n] + pltpu.roll(step[n], 8 - shift, 0),
                step[n + shift] + pltpu.roll(step[n + shift], shift, 0),
            )
            for n in range(shift)
        ]
    return step[0]


def pressure_work(phi_f, phi_t, nodes, fine, twin, rows_f, rows_t):
    i = lax.axis_index("gx")
    j = lax.axis_index("gy")
    sub = lax.broadcasted_iota(jnp.int32, (8, LANES), 0)
    lane = lane_iota(8)
    corner, az = sub >> 1, (sub & 1) == 1

    def own_nodes(level, col):
        here = (sub == i) & (lane == level * 64 + col * 32 + j)
        out = jnp.zeros((8, LANES), F32)
        for a in range(4):
            value = jnp.where(here, nodes[a], 0.0)
            value = jnp.sum(jnp.sum(value, axis=0, keepdims=True), axis=1, keepdims=True)
            out = jnp.where(corner == a, value, out)
        return jnp.where(az, out, 1.0), jnp.where(az, 0.0, out)

    _, seg, _ = split_lane(FINE, lane)
    fine_weights = []
    for col in range(2):
        first, second = own_nodes(0, col)
        fine_weights.append(jnp.where(seg == 0, first, second))
    _, seg, _ = split_lane(TWIN, lane)
    twin_weights = jnp.zeros((8, LANES), F32)
    for col in range(2):
        first, second = own_nodes(1, col)
        twin_weights = jnp.where(seg == 2 * col, first, twin_weights)
        twin_weights = jnp.where(seg == 2 * col + 1, second, twin_weights)

    def fine_rows(k, carry):
        for col in range(2):
            for g in range(EL // 8):
                values = [phi_f[col, 8 * g + n, k] * fine_weights[col] for n in range(8)]
                rows_f[col, k, 8 * g:8 * g + 8, :] = fold_rows(values, sub)
        return carry

    lax.fori_loop(0, FINE.nk, fine_rows, 0)

    def twin_rows(k, carry):
        for g in range(EL // 16):
            values = [phi_t[8 * g + n, k] * twin_weights for n in range(8)]
            rows_t[k, 8 * g:8 * g + 8, :] = fold_rows(values, sub)
        return carry

    lax.fori_loop(0, TWIN.nk, twin_rows, 0)

    def turn(value, shift):
        return pltpu.roll(value, shift % LANES, 1) if shift % LANES else value

    wide = lane_iota(EL)
    for col in range(2):
        for t in range(8):
            out = None
            for h in range(4):
                y = 4 * t + h + MX
                c, k = y // FINE.nk, y % FINE.nk
                for e in range(2):
                    to = h * 32 + e * 16
                    piece = turn(rows_f[col, k], to - (c * GROUP + e * 20 + MZ))
                    out = piece if out is None else jnp.where(wide >= to, piece, out)
            fine[:, (col * 8 + t) * LANES:(col * 8 + t + 1) * LANES] = out
    wide = lane_iota(EL // 2)
    for t in range(4):
        out = None
        for h in range(8):
            col, y = (8 * t + h) // 16, (8 * t + h) % 16 + MX // 2
            c, k = y // TWIN.nk, y % TWIN.nk
            for e in range(2):
                to = h * 16 + e * 8
                piece = turn(rows_t[k], to - (c * GROUP + col * 20 + e * 10 + MZ // 2))
                out = piece if out is None else jnp.where(wide >= to, piece, out)
        twin[:, t * LANES:(t + 1) * LANES] = out


def solve_kernel(perm, matrix_in, masks_in, fine, twin, own, hx, hy, hc, matrix, masks, send, recv, fetch,
                 phi_f, phi_t, rows_f, rows_t, line, *scratch):
    exchange, local = scratch[:7], scratch[7:]
    plans = halo_plans(perm, hx, hy, hc)
    fetches = [
        pltpu.make_async_copy(src, dst, fetch.at[n])
        for n, (src, dst) in enumerate(((perm, own), (matrix_in, matrix), (masks_in, masks)))
    ]
    for copy in fetches:
        copy.start()
    greet(plans)
    copies = halo_copies(plans, send, recv)
    for copy in copies:
        copy.start()
    for copy in fetches:
        copy.wait()
    for copy in copies:
        copy.wait()
    local_work(own, hx, hy, hc, matrix, masks, phi_f, phi_t, line, *local)
    nodes = coarse_work(line, *exchange)
    pressure_work(phi_f, phi_t, nodes, fine, twin, rows_f, rows_t)


def solve(perm, ni, nj):
    vmem = pl.BlockSpec(memory_space=pltpu.VMEM)
    return pl.pallas_call(
        solve_kernel,
        out_shape=(
            jax.ShapeDtypeStruct((EL, 2048), F32),
            jax.ShapeDtypeStruct((EL // 2, 512), F32),
        ),
        in_specs=[pl.BlockSpec(memory_space=pl.ANY)] * 3,
        out_specs=(vmem, vmem),
        scratch_shapes=[
            pltpu.VMEM(perm.shape, F32),
            pltpu.VMEM((2, 3, MX, perm.shape[2]), F32),
            pltpu.VMEM((2, 3, perm.shape[1], LANES), F32),
            pltpu.VMEM((4, 3, MX, LANES), F32),
            pltpu.VMEM((LANES, LANES), jnp.bfloat16),
            pltpu.VMEM((10, 8, LANES), F32),
            pltpu.SemaphoreType.DMA((8,)),
            pltpu.SemaphoreType.DMA((8,)),
            pltpu.SemaphoreType.DMA((3,)),
            pltpu.VMEM((2, EL, FINE.nk, 8, LANES), F32),
            pltpu.VMEM((EL // 2, TWIN.nk, 8, LANES), F32),
            pltpu.VMEM((2, FINE.nk, EL, LANES), F32),
            pltpu.VMEM((TWIN.nk, EL // 2, LANES), F32),
            pltpu.VMEM((1, LANES), F32),
            pltpu.VMEM((nj, 1, LANES), F32),
            pltpu.VMEM((16, LANES), F32),
            pltpu.VMEM((ni * 16, LANES), F32),
            pltpu.SemaphoreType.DMA((nj,)),
            pltpu.SemaphoreType.DMA((nj,)),
            pltpu.SemaphoreType.DMA((ni,)),
            pltpu.SemaphoreType.DMA((ni,)),
        ] + local_scratch(),
        compiler_params=pltpu.CompilerParams(
            collective_id=1, has_side_effects=True, vmem_limit_bytes=VLIMIT
        ),
    )(
        perm,
        jnp.asarray(coarsen_matrix(), jnp.bfloat16), jnp.asarray(stencil_masks()),
    )


def solution(mesh):
    ni, nj = mesh.shape["gx"], mesh.shape["gy"]

    def shards(perm):
        return solve(perm, ni, nj)

    return jax.shard_map(
        shards,
        mesh=mesh,
        in_specs=(P(None, "gx", "gy"),),
        out_specs=(P("gx", "gy"), P("gx", "gy")),
        check_vma=False,
    )
```

```python
import functools

import jax
import jax.numpy as jnp
import numpy as np
from jax import lax
from jax.experimental import pallas as pl
from jax.experimental.pallas import tpu as pltpu
from jax.sharding import PartitionSpec as P

EL = 32
ELZ = 16
MX = 4
MZ = 2
LANES = 128
GROUP = 40
MESH = pl.DeviceIdType.MESH
F32 = jnp.float32
VLIMIT = 60 * 1024 * 1024
FINE_PLANES = (4, 4)
TWIN_PLANES = (5, 8)


class Level:
    def __init__(self, nk, nx, zw, edge, edge_depth, margin, margin_depth, spacing):
        self.nk = nk
        self.nx = nx
        self.nxr = -(-nx // 8) * 8
        self.zw = zw
        self.nseg = GROUP // zw
        self.edge = edge
        self.edge_depth = edge_depth
        self.margin = margin
        self.margin_depth = margin_depth
        self.spacing = spacing


FINE = Level(13, 40, 20, EL, ELZ, MX, MZ, 1.0)
TWIN = Level(7, 20, 10, EL // 2, ELZ // 2, MX // 2, MZ // 2, 2.0)


def stencil_masks():
    masks = np.zeros((10, 8, LANES), np.float32)

    def put(e, a, b, q):
        s = (b - a) % 8
        if s > 4:
            a, s = b, 8 - s
        masks[e * 5 + s, a, q] += 1.0

    q = 0
    for a in range(4):
        for b in range(a, 4):
            put(0, 2 * a + 1, 2 * b + 1, q)
            put(1, 2 * a, 2 * b, q)
            q += 1
    for a in range(4):
        for b in range(4):
            put(0, 2 * a + 1, 2 * b, q)
        q += 1
    return masks


def coarsen_matrix():
    matrix = np.zeros((LANES, LANES), np.float32)
    for h in range(4):
        for e in range(2):
            for zz in range(10):
                for part in range(2):
                    z = min(max(e * ELZ - MZ + 2 * zz + part, 0), 31)
                    matrix[h * 32 + z, (h // 2) * 20 + e * 10 + zz] += 0.125
    return matrix


def lane_iota(rows):
    return lax.broadcasted_iota(jnp.int32, (rows, LANES), 1)


def groups(lane):
    return (lane >= 40).astype(jnp.int32) + (lane >= 80).astype(jnp.int32) + (lane >= 120).astype(jnp.int32)


def split_lane(level, lane):
    chunk = groups(lane)
    inner = lane - GROUP * chunk
    seg = jnp.zeros_like(lane)
    for s in range(1, level.nseg):
        seg = seg + (inner >= s * level.zw).astype(jnp.int32)
    return chunk, seg, inner - level.zw * seg


def harmonic(first, second, spacing):
    return spacing * 2.0 * first * second / (first + second)


def halo_plans(perm, hx, hy, hc):
    i = lax.axis_index("gx")
    j = lax.axis_index("gy")
    ni = lax.axis_size("gx")
    nj = lax.axis_size("gy")
    up, down = lax.rem(i + 1, ni), lax.rem(i + ni - 1, ni)
    right, left = lax.rem(j + 1, nj), lax.rem(j + nj - 1, nj)
    rows, width = perm.shape[1], perm.shape[2]
    west, east = pl.ds(0, MX), pl.ds(rows - MX, MX)
    low, high = pl.ds(0, LANES), pl.ds(width - LANES, LANES)
    return [
        (perm.at[:, east], hx.at[0], (up, j)),
        (perm.at[:, west], hx.at[1], (down, j)),
        (perm.at[:, :, high], hy.at[0], (i, right)),
        (perm.at[:, :, low], hy.at[1], (i, left)),
        (perm.at[:, east, high], hc.at[0], (up, right)),
        (perm.at[:, east, low], hc.at[1], (up, left)),
        (perm.at[:, west, high], hc.at[2], (down, right)),
        (perm.at[:, west, low], hc.at[3], (down, left)),
    ]


def halo_copies(plans, send, recv):
    return [
        pltpu.make_async_remote_copy(
            src_ref=src, dst_ref=dst, send_sem=send.at[n], recv_sem=recv.at[n],
            device_id=target, device_id_type=MESH,
        )
        for n, (src, dst, target) in enumerate(plans)
    ]


def assemble(own, hx, hy, hc, ext):
    rows = own.shape[1]

    def body(m, carry):
        for t in range(18):
            if t == 0:
                top, mid, low = hc[0, m], hy[0, m], hc[2, m]
            elif t == 17:
                top, mid, low = hc[1, m], hy[1, m], hc[3, m]
            else:
                lanes = pl.ds((t - 1) * LANES, LANES)
                top, mid, low = hx[0, m, :, lanes], own[m, :, lanes], hx[1, m, :, lanes]
            ext[m, t, 0:MX, :] = top
            ext[m, t, MX:MX + rows, :] = mid
            ext[m, t, MX + rows:2 * MX + rows, :] = low
            ext[m, t, 2 * MX + rows:, :] = jnp.ones((8, LANES), F32)
        return carry

    lax.fori_loop(0, 3, body, 0)


def pack_fine(ext, packed, merged, column):
    lane = lane_iota(GROUP)
    chunk, _, _ = split_lane(FINE, lane)
    inner = lane - GROUP * chunk

    def body(m, carry):
        for k in range(FINE.nk + 1):
            lines = []
            for c in range(3):
                y = FINE.nk * c + k
                tile = ext[m, column * 8 + y // 4, 0:40, :]
                shift = (c * GROUP + MZ - (y % 4) * 32) % LANES
                lines.append(pltpu.roll(tile, shift, 1) if shift else tile)
            merged[m, k] = jnp.where(lane < GROUP, lines[0], jnp.where(lane < 2 * GROUP, lines[1], lines[2]))
        return carry

    lax.fori_loop(0, 3, body, 0)

    def widen(m, carry):
        for k in range(FINE.nk + 1):
            q = merged[m, k]
            out = jnp.where(inner < MZ, pltpu.roll(q, LANES - 1, 1), q)
            out = jnp.where(inner > 19, pltpu.roll(q, 4, 1), out)
            packed[m, k, 0:40, :] = jnp.where(inner > 37, pltpu.roll(q, 5, 1), out)
            packed[m, k, 40:48, :] = jnp.ones((8, LANES), F32)
        return carry

    lax.fori_loop(0, 3, widen, 0)


def pack_twin(ext, matrix, pairs, small, packed):
    lane = lane_iota(24)
    chunk = groups(lane)
    half = jnp.zeros_like(lane)
    for s in range(1, 7):
        half = half + (lane >= 20 * s).astype(jnp.int32)
    weights = matrix[...]

    def body(m, carry):
        for t in range(18):
            first = ext[m, t, pl.ds(0, 24, stride=2), :]
            second = ext[m, t, pl.ds(1, 24, stride=2), :]
            pairs[t * 24:(t + 1) * 24, :] = first + second
        value = pairs[...]
        high = value.astype(jnp.bfloat16)
        rest = value - high.astype(F32)
        mid = rest.astype(jnp.bfloat16)
        low = (rest - mid.astype(F32)).astype(jnp.bfloat16)
        small[...] = (
            jnp.dot(high, weights, preferred_element_type=F32)
            + jnp.dot(mid, weights, preferred_element_type=F32)
            + jnp.dot(low, weights, preferred_element_type=F32)
        )
        for k in range(TWIN.nk + 1):
            out = jnp.ones((24, LANES), F32)
            for c in range(3):
                y = min(TWIN.nk * c + k, TWIN.nx - 1)
                for col in range(2):
                    base = (col * 8 + y // 2) * 24
                    line = small[base:base + 24, :]
                    shift = (c * GROUP + col * 20 - (y % 2) * 20) % LANES
                    line = pltpu.roll(line, shift, 1) if shift else line
                    out = jnp.where(half == 2 * c + col, line, out)
            packed[m, k, 0:24, :] = out
            packed[m, k, 24:32, :] = jnp.ones((8, LANES), F32)
        return carry

    lax.fori_loop(0, 3, body, 0)


def face_arrays(level, packed, wt, ym, turned):
    nk, nx, nxr = level.nk, level.nx, level.nxr
    lane = lane_iota(nxr)
    chunk, seg, z = split_lane(level, lane)
    row = lax.broadcasted_iota(jnp.int32, (nxr, LANES), 0)
    ml, mz = level.margin, level.margin_depth
    inside_xz = (row > 0) & (row < nx - 1) & (z > 0) & (z < level.zw - 1) & (chunk < 3)
    el_x = (row >= ml) & (row < ml + level.edge)
    el_z = (z >= mz) & (z < mz + level.edge_depth) & (chunk < 3)
    el_xf = (row >= ml) & (row < ml + level.edge - 1)
    el_zf = (z >= mz) & (z < mz + level.edge_depth - 1) & (chunk < 3)
    first_edge = seg == 0
    if level.nseg == 4:
        first_edge = first_edge | (seg == 2)
    first_edge = first_edge & (z == 0)
    last_edge = jnp.logical_not((seg == 0) | (seg == 2)) & (z == level.zw - 2)

    el_zb = (z > mz) & (z < mz + level.edge_depth) & (chunk < 3)
    below_first = (z == 1) & ((seg == 0) | (seg == 2))
    below_last = (z == level.zw - 1) & jnp.logical_not((seg == 0) | (seg == 2))
    for k in range(nk):
        kz = packed[2, k, 0:nxr, :]
        turned[0, k] = pltpu.roll(kz, LANES - 1, 1)
        turned[1, k] = pltpu.roll(kz, 1, 1)

    def body(k, carry):
        y = chunk * nk + k
        inside = inside_xz & (y > 0) & (y < nx - 1)
        el_y = (y >= ml) & (y < ml + level.edge)
        el_yf = (y >= ml) & (y < ml + level.edge - 1)
        tx = harmonic(packed[0, k, 0:nxr, :], packed[0, k, 1:nxr + 1, :], level.spacing)
        ty = harmonic(packed[1, k, 0:nxr, :], packed[1, k + 1, 0:nxr, :], level.spacing)
        kz = packed[2, k, 0:nxr, :]
        kz_after, kz_before, kz_here = turned[0, k], turned[1, k], kz
        if level is FINE:
            kz_here = jnp.where(first_edge, kz_after, kz)
            kz_after = jnp.where(last_edge, kz, kz_after)
            kz_before = jnp.where(below_first, kz, kz_before)
            kz = jnp.where(below_last, kz_before, kz)
        tz = harmonic(kz_here, kz_after, level.spacing)
        tz_below = harmonic(kz_before, kz, level.spacing)
        wt[0, k] = tx
        wt[1, k] = ty
        wt[2, k] = tz
        wt[3, k] = tz_below
        wt[4, k] = jnp.where(inside, tx - pltpu.roll(tx, 1, 0), 0.0)
        wt[6, k] = jnp.where(inside, tz - tz_below, 0.0)
        wt[7, k] = jnp.where(el_xf & el_y & el_z, tx, 0.0)
        wt[8, k] = jnp.where(el_x & el_yf & el_z, ty, 0.0)
        wt[9, k] = jnp.where(el_x & el_y & el_zf, tz, 0.0)
        wt[10, k] = jnp.where(el_x & el_y & el_zb, tz_below, 0.0)
        return carry

    lax.fori_loop(0, nk, body, 0)
    ym[0] = pltpu.roll(wt[1, nk - 1], GROUP, 1)
    ym[1] = pltpu.roll(wt[8, nk - 1], GROUP, 1)

    def inside_at(k):
        y = chunk * nk + k
        return inside_xz & (y > 0) & (y < nx - 1)

    wt[5, 0] = jnp.where(inside_at(0), wt[1, 0] - ym[0], 0.0)

    def second(k, carry):
        wt[5, k] = jnp.where(inside_at(k), wt[1, k] - wt[1, k - 1], 0.0)
        return carry

    lax.fori_loop(1, nk, second, 0)


def basis_solve(level, wt, ym, cst, r0, r1, r2, w, w2, *rest):
    *rings, phi, planes = rest
    rings = rings[:4], rings[4:]
    nk, nx = level.nk, level.nx
    lane = lane_iota(8)
    chunk, seg, z = split_lane(level, lane)
    sub = lax.broadcasted_iota(jnp.int32, (8, LANES), 0)
    ax, ay, az = sub >= 4, ((sub >> 1) & 1) == 1, (sub & 1) == 1

    def ramp(flag, place, length):
        return jnp.where(flag, place / length, 1.0 - place / length)

    fz = ramp(az, z.astype(F32) - level.margin_depth + 0.5, level.edge_depth)
    sx = jnp.where(ax, 1.0 / level.edge, -1.0 / level.edge)
    sy = jnp.where(ay, 1.0 / level.edge, -1.0 / level.edge)
    sz = jnp.where(az, 1.0 / level.edge_depth, -1.0 / level.edge_depth)
    cst[4, 0] = sy * fz
    cst[4, 1] = sx
    for k in range(nk):
        fy = ramp(ay, (chunk * nk + k).astype(F32) - level.margin + 0.5, level.edge)
        cst[0, k] = sx * fy * fz
        cst[1, k] = sz * fy
        cst[2, k] = fy * fz

    cst[4, 2] = jnp.where(ax, (0.5 - level.margin) / level.edge, 1.0 - (0.5 - level.margin) / level.edge)

    def fx_at(x):
        return cst[4, 2] + cst[4, 1] * x.astype(F32)

    def mask_at(k):
        y = chunk * nk + k
        return (y > 0) & (y < nx - 1) & (z > 0) & (z < level.zw - 1) & (chunk < 3)

    cst[4, 3] = jnp.zeros((8, LANES), F32)
    zero = cst[4, 3]

    def row(n, k, x):
        return wt[n, k, pl.ds(x, 8, stride=0), :]

    def pipeline(base, low, high, depth, produce, keep, keep_w, consume, state):
        def apply(ring, x0, after, fx_prev, state):
            u_ring, above, below, beside = ring
            ahead = [u_ring[0, k] for k in range(nk)]
            for p in range(depth):
                x = x0 + p
                u = ahead
                ahead = after if p == depth - 1 else [u_ring[p + 1, k] for k in range(nk)]
                fy_prev = ym[base // 7, pl.ds(x, 8, stride=0), :] * (beside[p, 1] - u[0])
                image, fx_new = [], []
                for k in range(nk):
                    flux = row(base, k, x) * (u[k] - ahead[k])
                    fx_new.append(flux)
                    out = flux - fx_prev[k]
                    side = u[k + 1] if k < nk - 1 else beside[p, 0]
                    fy = row(base + 1, k, x) * (u[k] - side)
                    out = out + (fy - fy_prev)
                    fy_prev = fy
                    out = out + row(base + 2, k, x) * (u[k] - above[p, k])
                    image.append(out + row(base + 3, k, x) * (u[k] - below[p, k]))
                    if keep_w is not None:
                        keep_w[x, k] = image[k]
                    state = consume(state, u[k], image[k])
                fx_prev = fx_new
            return fx_prev, state

        def make(ring, x0):
            u_ring, above, below, beside = ring
            first = None
            for p in range(depth):
                u = produce(x0 + p)
                first = u if first is None else first
                for k in range(nk):
                    keep[x0 + p, k] = u[k]
                    u_ring[p, k] = u[k]
                    above[p, k] = pltpu.roll(u[k], LANES - 1, 1)
                    below[p, k] = pltpu.roll(u[k], 1, 1)
                beside[p, 0] = pltpu.roll(u[0], LANES - GROUP, 1)
                beside[p, 1] = pltpu.roll(u[nk - 1], GROUP, 1)
            return first

        even, odd = rings
        make(even, jnp.int32(low))

        def body(n, carry):
            fx_prev, state = carry
            x0 = low + n * (2 * depth)
            after = make(odd, x0 + depth)
            fx_prev, state = apply(even, x0, after, fx_prev, state)
            after = make(even, x0 + 2 * depth)
            return apply(odd, x0 + depth, after, fx_prev, state)

        count = (high - low) // (2 * depth)
        fx_prev, state = lax.fori_loop(0, count - 1, body, ([zero] * nk, state))
        x0 = jnp.int32(high - 2 * depth)
        after = make(odd, x0 + depth)
        fx_prev, state = apply(even, x0, after, fx_prev, state)
        _, state = apply(odd, x0 + depth, [zero] * nk, fx_prev, state)
        return state

    def norms(state, u, image):
        return state[0] + u * u, state[1] + u * image

    def sweep(produce, keep, keep_w):
        state = pipeline(0, 0, nx, planes[0], produce, keep, keep_w, norms, (zero, zero))
        if keep_w is not None:
            for k in range(nk):
                keep_w[0, k] = zero
                keep_w[nx - 1, k] = zero
        return by_segment(state[0]), by_segment(state[1])

    def by_segment(acc):
        out = jnp.sum(jnp.where(seg == 0, acc, 0.0), axis=1, keepdims=True)
        for s in range(1, level.nseg):
            total = jnp.sum(jnp.where(seg == s, acc, 0.0), axis=1, keepdims=True)
            out = jnp.where(seg == s, total, out)
        return out

    def first(x):
        fx = fx_at(x)
        return [
            row(4, k, x) * cst[0, k] + fx * (row(5, k, x) * cst[4, 0] + row(6, k, x) * cst[1, k])
            for k in range(nk)
        ]

    rr0, rw0 = sweep(first, r0, w)
    alpha0 = rr0 / rw0
    for k in range(nk):
        cst[3, k] = jnp.where(mask_at(k), alpha0, 0.0)
    rr1, rw1 = sweep(lambda x: [r0[x, k] - cst[3, k] * w[x, k] for k in range(nk)], r1, w2)
    beta0 = rr1 / rr0
    alpha1 = rr1 / (rw1 - beta0 / alpha0 * rr1)
    gamma = alpha1 * beta0 / alpha0
    for k in range(nk):
        cst[3, k] = jnp.where(mask_at(k), alpha1, 0.0)

    def third(x):
        return [
            r1[x, k] + gamma * (r1[x, k] - r0[x, k]) - cst[3, k] * w2[x, k] for k in range(nk)
        ]

    rr2, rw2 = sweep(third, r2, None)
    beta1 = rr2 / rr1
    alpha2 = rr2 / (rw2 - beta1 / alpha1 * rr2)
    c2 = alpha2
    c1 = alpha1 + alpha2 * beta1
    c0 = alpha0 + c1 * beta0
    low = level.margin

    def basis(x):
        fx = fx_at(x)
        return [
            fx * cst[2, k] + (c0 * r0[x, k] + (c1 * r1[x, k] + c2 * r2[x, k])) for k in range(nk)
        ]

    def diagonals(state, u, image):
        return tuple(
            state[s] + u * (pltpu.roll(image, 8 - s, 0) if s else image) for s in range(5)
        )

    acc = pipeline(7, low, low + level.edge, planes[1], basis, phi, None, diagonals, (zero,) * 5)
    return acc, seg


def stencil(level, acc, seg, masks, elements):
    out = jnp.zeros((8, LANES), F32)
    for e, s in enumerate(elements):
        for n in range(5):
            total = jnp.sum(jnp.where(seg == s, acc[n], 0.0), axis=1, keepdims=True)
            out = out + total * masks[e * 5 + n]
    return out


class Shifted:
    def __init__(self, ref, first, column=None):
        self.ref = ref
        self.first = first
        self.column = column

    def place(self, index):
        x, k = index
        return (x - self.first, k) if self.column is None else (self.column, x - self.first, k)

    def __getitem__(self, index):
        return self.ref[self.place(index)]

    def __setitem__(self, index, value):
        self.ref[self.place(index)] = value


def local_work(own, hx, hy, hc, matrix, masks, phi_f, phi_t, line, ext, pairs, small, merged, *scratch):
    pk_f, wt_f, ym_f, turned_f, cst_f, *fields_f = scratch[:18]
    pk_t, wt_t, ym_t, turned_t, cst_t, *fields_t = scratch[18:]
    assemble(own, hx, hy, hc, ext)
    pack_twin(ext, matrix, pairs, small, pk_t)
    face_arrays(TWIN, pk_t, wt_t, ym_t, turned_t)
    acc, seg = basis_solve(TWIN, wt_t, ym_t, cst_t, *fields_t, Shifted(phi_t, TWIN.margin), TWIN_PLANES)
    parts = [stencil(TWIN, acc, seg, masks, (2 * col, 2 * col + 1)) for col in range(2)]
    total = pltpu.roll(parts[0], 32, 1) + pltpu.roll(parts[1], 48, 1)

    def body(col, total):
        pack_fine(ext, pk_f, merged, col)
        face_arrays(FINE, pk_f, wt_f, ym_f, turned_f)
        phi = Shifted(phi_f, FINE.margin, col)
        acc, seg = basis_solve(FINE, wt_f, ym_f, cst_f, *fields_f, phi, FINE_PLANES)
        part = stencil(FINE, acc, seg, masks, (0, 1))
        here = jnp.full((8, LANES), col, jnp.int32) == 0
        return total + jnp.where(here, part, pltpu.roll(part, 16, 1))

    total = lax.fori_loop(0, 2, body, total)
    line[...] = jnp.sum(total, axis=0, keepdims=True)


def local_scratch():
    def scratch(level, depth):
        field = pltpu.VMEM((level.nx, level.nk, 8, LANES), F32)
        return [
            pltpu.VMEM((3, level.nk + 1, level.nxr + 8, LANES), F32),
            pltpu.VMEM((11, level.nk, level.nxr, LANES), F32),
            pltpu.VMEM((2, level.nxr, LANES), F32),
            pltpu.VMEM((2, level.nk, level.nxr, LANES), F32),
            pltpu.VMEM((5, level.nk, 8, LANES), F32),
        ] + [field] * 5 + (
            [pltpu.VMEM((depth, level.nk, 8, LANES), F32)] * 3 + [pltpu.VMEM((depth, 2, 8, LANES), F32)]
        ) * 2

    return [
        pltpu.VMEM((3, 18, 48, LANES), F32),
        pltpu.VMEM((18 * 24, LANES), F32),
        pltpu.VMEM((18 * 24, LANES), F32),
        pltpu.VMEM((3, FINE.nk + 1, GROUP, LANES), F32),
    ] + scratch(FINE, max(FINE_PLANES)) + scratch(TWIN, max(TWIN_PLANES))


def coarse_solve(quantity, lane):
    second = (lane & 63) >= 32
    place = lane & 31

    def next_q(x):
        same = pltpu.roll(x, LANES - 32, 1)
        inner = pltpu.roll(x, 31, 1)
        outer = pltpu.roll(x, 63, 1)
        return jnp.where(second, jnp.where(place < 31, inner, outer), same)

    def prev_q(x):
        same = pltpu.roll(x, 32, 1)
        inner = pltpu.roll(x, LANES - 31, 1)
        outer = pltpu.roll(x, LANES - 63, 1)
        return jnp.where(second, same, jnp.where(place > 0, inner, outer))

    def next_p(x):
        return pltpu.roll(x, 7, 0)

    def prev_p(x):
        return pltpu.roll(x, 1, 0)

    entry = {}
    n = 0
    for a in range(4):
        for b in range(a, 4):
            entry[a, b] = entry[b, a] = quantity(n)
            n += 1

    def corners(x):
        side = next_q(x)
        return [x, side, next_p(x), next_p(side)]

    def gather(parts):
        side = prev_q(parts[1] + prev_p(parts[3]))
        return parts[0] + side + prev_p(parts[2])

    def operate(x):
        values = corners(x)
        parts = []
        for a in range(4):
            terms = [entry[a, b] * values[b] for b in range(4)]
            parts.append((terms[0] + terms[1]) + (terms[2] + terms[3]))
        return gather(parts)

    upper = lane >= 64

    def total(x):
        column = jnp.sum(x, axis=0, keepdims=True)
        lo = jnp.sum(jnp.where(upper[:1], 0.0, column), axis=1, keepdims=True)
        hi = jnp.sum(jnp.where(upper[:1], column, 0.0), axis=1, keepdims=True)
        return jnp.where(upper, hi, lo)

    residual = -gather([quantity(10 + a) for a in range(4)])
    norm = total(residual * residual)
    image = operate(residual)
    alpha = norm / total(residual * image)
    update = alpha * residual
    after = residual - alpha * image
    norm_next = total(after * after)
    direction = after + norm_next / norm * residual
    image = operate(direction)
    alpha = norm_next / total(direction * image)
    update = update + alpha * direction
    return [value for value in corners(update)]


def greet(plans):
    i = lax.axis_index("gx")
    j = lax.axis_index("gy")
    ni = lax.axis_size("gx")
    nj = lax.axis_size("gy")
    barrier = pltpu.get_barrier_semaphore()
    for _, _, target in plans:
        pl.semaphore_signal(barrier, inc=1, device_id=target, device_id_type=MESH)

    def greet_y(d, carry):
        pl.semaphore_signal(barrier, inc=1, device_id=(i, lax.rem(j + d, nj)), device_id_type=MESH)
        return carry

    def greet_x(d, carry):
        pl.semaphore_signal(barrier, inc=1, device_id=(lax.rem(i + d, ni), j), device_id_type=MESH)
        return carry

    lax.fori_loop(1, nj, greet_y, 0)
    lax.fori_loop(1, ni, greet_x, 0)
    pl.semaphore_wait(barrier, ni + nj - 2 + len(plans))


def coarse_work(line, rows, block, grid, send1, recv1, send2, recv2, first_wait, second_wait):
    i = lax.axis_index("gx")
    j = lax.axis_index("gy")
    ni = lax.axis_size("gx")
    nj = lax.axis_size("gy")
    def copy_y(d):
        return pltpu.make_async_remote_copy(
            src_ref=line, dst_ref=rows.at[j], send_sem=send1.at[d], recv_sem=recv1.at[d],
            device_id=(i, lax.rem(j + d, nj)), device_id_type=MESH,
        )

    def copy_x(d):
        return pltpu.make_async_remote_copy(
            src_ref=block, dst_ref=grid.at[pl.ds(pl.multiple_of(i * 16, 16), 16)], send_sem=send2.at[d], recv_sem=recv2.at[d],
            device_id=(lax.rem(i + d, ni), j), device_id_type=MESH,
        )

    def start_y(d, carry):
        copy_y(d).start()
        return carry

    def wait_y(d, carry):
        copy_y(d).wait()
        return carry

    def start_x(d, carry):
        copy_x(d).start()
        return carry

    def wait_x(d, carry):
        copy_x(d).wait()
        return carry

    lax.fori_loop(1, nj, start_y, 0)
    rows[j] = line[...]
    first_wait()
    lax.fori_loop(1, nj, wait_y, 0)
    quarter = rows[:, 0, :]
    turned = jnp.transpose(jnp.concatenate([quarter] * 4, axis=0))
    lane16 = lane_iota(16)
    out = turned[48:64]
    for b in range(3):
        out = jnp.where((lane16 >= 32 * b) & (lane16 < 32 * b + 32), turned[16 * b:16 * b + 16], out)
    block[...] = out
    lax.fori_loop(1, ni, start_x, 0)
    grid[pl.ds(pl.multiple_of(i * 16, 16), 16), :] = out
    second_wait()
    lax.fori_loop(1, ni, wait_x, 0)
    return coarse_solve(lambda q: grid[pl.ds(q, 8, stride=16), :], lane_iota(8))


def turn_rows(values, sub):
    step = [values]
    for shift in (4, 2, 1):
        keep = (sub & shift) == 0
        after = []
        for part in step:
            low, high = [], []
            for n in range(shift):
                first, second = part[n], part[n + shift]
                low.append(jnp.where(keep, first, pltpu.roll(second, shift, 0)))
                high.append(jnp.where(keep, pltpu.roll(first, 8 - shift, 0), second))
            after += [low, high]
        step = after
    return [part[0] for part in step]


def row_sets(phi, sub, lower):
    rows = turn_rows(phi, sub)
    base = (rows[0] + rows[2]) + (rows[4] + rows[6])
    return [jnp.where(lower, base, 0.0)] + [
        jnp.where(lower, rows[2 * a + 1], rows[2 * a]) for a in range(4)
    ]


def prepare_rows(phi_f, phi_t, rows_f, rows_t):
    sub = lax.broadcasted_iota(jnp.int32, (8, LANES), 0)
    lane = lane_iota(8)
    _, seg, _ = split_lane(FINE, lane)
    lower_f = seg == 0
    _, seg, _ = split_lane(TWIN, lane)
    lower_t = (seg == 0) | (seg == 2)

    def fine_rows(k, carry):
        for col in range(2):
            for g in range(EL // 8):
                sets = row_sets([phi_f[col, 8 * g + n, k] for n in range(8)], sub, lower_f)
                for n in range(5):
                    rows_f[n, col, k, 8 * g:8 * g + 8, :] = sets[n]
        return carry

    lax.fori_loop(0, FINE.nk, fine_rows, 0)

    def twin_rows(k, carry):
        for g in range(EL // 16):
            sets = row_sets([phi_t[8 * g + n, k] for n in range(8)], sub, lower_t)
            for n in range(5):
                rows_t[n, k, 8 * g:8 * g + 8, :] = sets[n]
        return carry

    lax.fori_loop(0, TWIN.nk, twin_rows, 0)


def turn(value, shift):
    return pltpu.roll(value, shift % LANES, 1) if shift % LANES else value


def lay_out_fine(rows_f, sets_f, col):
    wide = lane_iota(EL)

    def body(n, carry):
        for t in range(8):
            out = None
            for h in range(4):
                y = 4 * t + h + MX
                c, k = y // FINE.nk, y % FINE.nk
                for e in range(2):
                    to = h * 32 + e * 16
                    piece = turn(rows_f[n, col, k], to - (c * GROUP + e * 20 + MZ))
                    out = piece if out is None else jnp.where(wide >= to, piece, out)
            sets_f[n, col * 8 + t] = out
        return carry

    lax.fori_loop(0, 5, body, 0)


def lay_out_twin(rows_t, sets_t):
    wide = lane_iota(EL // 2)

    def body(n, carry):
        for t in range(4):
            out = None
            for h in range(8):
                col, y = (8 * t + h) // 16, (8 * t + h) % 16 + MX // 2
                c, k = y // TWIN.nk, y % TWIN.nk
                for e in range(2):
                    to = h * 16 + e * 8
                    piece = turn(rows_t[n, k], to - (c * GROUP + col * 20 + e * 10 + MZ // 2))
                    out = piece if out is None else jnp.where(wide >= to, piece, out)
            sets_t[n, t] = out
        return carry

    lax.fori_loop(0, 5, body, 0)


def combine(nodes, sets_f, sets_t, fine, twin):
    i = lax.axis_index("gx")
    j = lax.axis_index("gy")
    sub = lax.broadcasted_iota(jnp.int32, (8, LANES), 0)
    lane = lane_iota(8)
    for level in range(2):
        for col in range(2):
            here = (sub == i) & (lane == level * 64 + col * 32 + j)
            weights = []
            for a in range(4):
                value = jnp.sum(jnp.where(here, nodes[a], 0.0), axis=0, keepdims=True)
                weights.append(jnp.sum(value, axis=1, keepdims=True))
            sets, out, count = (sets_t, twin, 2) if level else (sets_f, fine, 8)
            for t in range(col * count, (col + 1) * count):
                total = sets[0, t]
                for a in range(4):
                    total = total + weights[a] * sets[a + 1, t]
                out[:, t * LANES:(t + 1) * LANES] = total


def solve_kernel(perm, matrix_in, masks_in, fine, twin, own, hx, hy, hc, matrix, masks, send, recv, fetch,
                 phi_f, phi_t, rows_f, rows_t, sets_f, sets_t, line, *scratch):
    exchange, local = scratch[:7], scratch[7:]
    plans = halo_plans(perm, hx, hy, hc)
    fetches = [
        pltpu.make_async_copy(src, dst, fetch.at[n])
        for n, (src, dst) in enumerate(((perm, own), (matrix_in, matrix), (masks_in, masks)))
    ]
    for copy in fetches:
        copy.start()
    greet(plans)
    copies = halo_copies(plans, send, recv)
    for copy in copies:
        copy.start()
    for copy in fetches:
        copy.wait()
    for copy in copies:
        copy.wait()
    local_work(own, hx, hy, hc, matrix, masks, phi_f, phi_t, line, *local)

    def first_wait():
        prepare_rows(phi_f, phi_t, rows_f, rows_t)
        lay_out_fine(rows_f, sets_f, 0)

    def second_wait():
        lay_out_fine(rows_f, sets_f, 1)
        lay_out_twin(rows_t, sets_t)

    nodes = coarse_work(line, *exchange, first_wait, second_wait)
    combine(nodes, sets_f, sets_t, fine, twin)


def solve(perm, ni, nj):
    vmem = pl.BlockSpec(memory_space=pltpu.VMEM)
    return pl.pallas_call(
        solve_kernel,
        out_shape=(
            jax.ShapeDtypeStruct((EL, 2048), F32),
            jax.ShapeDtypeStruct((EL // 2, 512), F32),
        ),
        in_specs=[pl.BlockSpec(memory_space=pl.ANY)] * 3,
        out_specs=(vmem, vmem),
        scratch_shapes=[
            pltpu.VMEM(perm.shape, F32),
            pltpu.VMEM((2, 3, MX, perm.shape[2]), F32),
            pltpu.VMEM((2, 3, perm.shape[1], LANES), F32),
            pltpu.VMEM((4, 3, MX, LANES), F32),
            pltpu.VMEM((LANES, LANES), jnp.bfloat16),
            pltpu.VMEM((10, 8, LANES), F32),
            pltpu.SemaphoreType.DMA((8,)),
            pltpu.SemaphoreType.DMA((8,)),
            pltpu.SemaphoreType.DMA((3,)),
            pltpu.VMEM((2, EL, FINE.nk, 8, LANES), F32),
            pltpu.VMEM((EL // 2, TWIN.nk, 8, LANES), F32),
            pltpu.VMEM((5, 2, FINE.nk, EL, LANES), F32),
            pltpu.VMEM((5, TWIN.nk, EL // 2, LANES), F32),
            pltpu.VMEM((5, 16, EL, LANES), F32),
            pltpu.VMEM((5, 4, EL // 2, LANES), F32),
            pltpu.VMEM((1, LANES), F32),
            pltpu.VMEM((nj, 1, LANES), F32),
            pltpu.VMEM((16, LANES), F32),
            pltpu.VMEM((ni * 16, LANES), F32),
            pltpu.SemaphoreType.DMA((nj,)),
            pltpu.SemaphoreType.DMA((nj,)),
            pltpu.SemaphoreType.DMA((ni,)),
            pltpu.SemaphoreType.DMA((ni,)),
        ] + local_scratch(),
        compiler_params=pltpu.CompilerParams(
            collective_id=1, has_side_effects=True, vmem_limit_bytes=VLIMIT
        ),
    )(
        perm,
        jnp.asarray(coarsen_matrix(), jnp.bfloat16), jnp.asarray(stencil_masks()),
    )


def solution(mesh):
    ni, nj = mesh.shape["gx"], mesh.shape["gy"]

    def shards(perm):
        return solve(perm, ni, nj)

    return jax.shard_map(
        shards,
        mesh=mesh,
        in_specs=(P(None, "gx", "gy"),),
        out_specs=(P("gx", "gy"), P("gx", "gy")),
        check_vma=False,
    )
```
